32 devices in a mesh: rep: 8 (over z, y), ep: 4 (over x, core).
Axes of the slice: x: 2, y: 2, z: 4, core: 2. Of those that a mesh axis runs over, the one named last changes fastest.
Arguments:
- tokens: bfloat16 [16384, 1536], P(('rep', 'ep')), may hold values from -6 to 6
- norm_attn: bfloat16 [1536], replicated, may hold values from 0.099609375 to 1.8984375
- w_query: bfloat16 [1536, 1536], replicated, may hold values from -0.15625 to 0.15625
- key_projection: bfloat16 [1536, 512], replicated, may hold values from -0.15625 to 0.15625
- value_projection: bfloat16 [1536, 512], replicated, may hold values from -0.15625 to 0.15625
- w_out: bfloat16 [1536, 1536], replicated, may hold values from -2.5 to 2.5
- norm_ffn: bfloat16 [1536], replicated, may hold values from 0.099609375 to 1.8984375
- w_router: bfloat16 [1536, 20], replicated, may hold values from -0.078125 to 0.078125
- w_gate: bfloat16 [20, 1536, 512], P('ep'), may hold values from -0.15625 to 0.15625
- w_up: bfloat16 [20, 1536, 512], P('ep'), may hold values from -0.15625 to 0.15625
- w_down: bfloat16 [20, 512, 1536], P('ep'), may hold values from -3 to 3
- routes: int32 [16384, 8], P(('rep', 'ep')), may hold values from 0 to 19, as said below
- cotangent: bfloat16 [16384, 1536], P(('rep', 'ep')), may hold values from -6 to 6
Outputs:
- mixed: bfloat16 [16384, 1536], P(('rep', 'ep'))
- d_input: float32 [16384, 1536], P(('rep', 'ep'))
- grad_norm_attn: float32 [1536], P('ep')
- grad_query: float32 [1536, 1536], P('ep')
- grad_key: float32 [1536, 512], P('ep')
- grad_value: float32 [1536, 512], P('ep')
- grad_out: float32 [1536, 1536], P('ep')
- grad_norm_ffn: float32 [1536], P('ep')
- grad_router: float32 [1536, 20], P('ep')
- grad_gate: float32 [20, 1536, 512], P('ep')
- grad_up: float32 [20, 1536, 512], P('ep')
- grad_down: float32 [20, 512, 1536], P('ep')
The draws below stay inside these ranges and needn't reach their ends.
Inputs may be any that keep to these rules, and one draw needn't show every extreme that they name: `routes`: each row names 8 different experts. In each aligned block of 512 rows (the rows of one device) no expert is named by more than 384 rows, and in each group of 4 consecutive such blocks one expert is named by exactly 384 rows of every block of the group.
All inputs are finite; a program needn't handle non-finite values.
Results may differ from the reference program's by a relative error of at most 0.02.
Values may be sent and summed in bfloat16 or wider, within the bound.
A program may use at most 448 MiB of HBM per device.

```python
import math
import jax
import jax.numpy as jnp
from jax import lax

MODEL_WIDTH = 1536
QUERY_HEADS = 24
KEY_VALUE_HEADS = 8
HEAD_SIZE = 64
FF = 512
TOPK = 8
SEQUENCE_TOKENS = 512
BLOCK = 256
EXPERTS = 20
HOLDERS = 4
TOK_DEV = 512
CAP = 384
TOKENS = 16384


def route_block(block_key, group_key):
    expert_order = jax.random.permutation(jax.random.fold_in(group_key, 1), EXPERTS)
    star_run = jax.random.randint(jax.random.fold_in(group_key, 2), (), 0, EXPERTS)
    run_index = jnp.arange(EXPERTS)
    spread = jax.random.randint(jax.random.fold_in(block_key, 3), (EXPERTS,), 5, 9)
    others = run_index != star_run
    spread = jnp.where(others, spread, 0)
    remain = TOPK * TOK_DEV - CAP
    base_load = remain * spread // jnp.sum(spread)
    deficit = remain - jnp.sum(base_load)
    run_rank = jnp.cumsum(others.astype(jnp.int32)) - 1
    run_loads = base_load + jnp.where(others & (run_rank < deficit), 1, 0)
    run_loads = jnp.where(others, run_loads, CAP)
    run_ends = jnp.cumsum(run_loads)
    places = jnp.arange(TOPK * TOK_DEV)
    run_of = jnp.sum((places[:, None] >= run_ends[None, :]).astype(jnp.int32), 1)
    chosen = jnp.sum((run_of[:, None] == run_index[None, :]).astype(jnp.int32) * expert_order[None, :], 1)
    token_grid = chosen.reshape(TOPK, TOK_DEV).T
    shuffle = jax.random.permutation(jax.random.fold_in(block_key, 4), TOK_DEV)
    return token_grid[shuffle]


def draw_routes(key, part):
    blocks = TOKENS // TOK_DEV
    block_ids = jnp.arange(blocks)

    def one_block(block):
        group_key = jax.random.fold_in(jax.random.fold_in(key, 11), block // HOLDERS)
        block_key = jax.random.fold_in(jax.random.fold_in(key, 7), block)
        return route_block(block_key, group_key)
    return jax.vmap(one_block)(block_ids).reshape(TOKENS, TOPK).astype(jnp.int32)


def with_spikes(drawn, rng, source, target, blocks, factor):
    owner, partner = [(jnp.arange(drawn.shape[dim]) // (drawn.shape[dim] // blocks)).reshape([-1 if axis == dim else 1 for axis in range(drawn.ndim)]) for dim in (source, target)]
    chosen = jax.random.permutation(rng, blocks)[partner]
    strong = (owner == chosen) | (owner == (partner + blocks // 2) % blocks)
    return jnp.where(strong, factor * drawn, drawn)


def levels(rng, dims, pieces, smallest, largest):
    gain = 1.0
    for dim, parts in pieces:
        steps = jax.random.uniform(jax.random.fold_in(jax.random.fold_in(rng, 6), dim), (parts,), jnp.float32, smallest / len(pieces), largest / len(pieces))
        gain = gain * jnp.repeat(jnp.exp(steps), dims[dim] // parts).reshape((-1,) + (1,) * (len(dims) - 1 - dim))
    return gain


def gaussian(stream_key, dims, scale, most, shards=(), held_as=jnp.bfloat16):
    drawn = jax.random.normal(stream_key, dims, jnp.float32) * scale
    if len(shards) > 0:
        drawn = levels(stream_key, dims, shards, -0.22, 0.18) * drawn
    return jnp.clip(drawn, min=-most, max=most).astype(held_as)


def gaussian_with(key, extent, scale, most, split, heavy, held_as=jnp.bfloat16):
    array = scale * jax.random.normal(key, extent, jnp.float32)
    if split:
        array = array * levels(key, extent, split, -0.22, 0.18)
    return jnp.clip(with_spikes(array, jax.random.fold_in(key, 3), *heavy), -most, most).astype(held_as)


def setup_inputs(seed: int = 0) -> dict:
    arg_keys = jax.random.split(jax.random.key(seed), 14)
    tokens = gaussian(arg_keys[0], (TOKENS, MODEL_WIDTH), 1.0, 6.0, ((0, 32),))
    norm_attn = jnp.clip(1.0 + 0.18 * jax.random.normal(arg_keys[1], (MODEL_WIDTH,), jnp.float32), 0.099609375, 1.8984375).astype(jnp.bfloat16)
    w_query = gaussian(arg_keys[2], (MODEL_WIDTH, QUERY_HEADS * HEAD_SIZE), MODEL_WIDTH ** -0.5, 0.15625)
    key_projection = gaussian(arg_keys[3], (MODEL_WIDTH, KEY_VALUE_HEADS * HEAD_SIZE), MODEL_WIDTH ** -0.5, 0.15625)
    value_projection = gaussian(arg_keys[4], (MODEL_WIDTH, KEY_VALUE_HEADS * HEAD_SIZE), MODEL_WIDTH ** -0.5, 0.15625)
    w_out = gaussian(arg_keys[5], (QUERY_HEADS * HEAD_SIZE, MODEL_WIDTH), (max(QUERY_HEADS * HEAD_SIZE // 256, 1)) ** -0.5, 2.5)
    norm_ffn = jnp.clip(1.0 + 0.18 * jax.random.normal(arg_keys[6], (MODEL_WIDTH,), jnp.float32), 0.099609375, 1.8984375).astype(jnp.bfloat16)
    w_router = gaussian(arg_keys[7], (MODEL_WIDTH, EXPERTS), (4 * MODEL_WIDTH) ** -0.5, 0.078125)
    w_gate = gaussian(arg_keys[8], (EXPERTS, MODEL_WIDTH, FF), MODEL_WIDTH ** -0.5, 0.15625, ((0, 4),))
    w_up = gaussian(arg_keys[9], (EXPERTS, MODEL_WIDTH, FF), MODEL_WIDTH ** -0.5, 0.15625, ((0, 4),))
    w_down = gaussian(arg_keys[10], (EXPERTS, FF, MODEL_WIDTH), 4 ** -0.5, 3.0, ((0, 4),))
    routes = draw_routes(jax.random.fold_in(arg_keys[13], 71), 0)
    cotangent = gaussian_with(arg_keys[12], (TOKENS, MODEL_WIDTH), 1.0, 6.0, ((0, 32),), (0, 1, 32, 2.75))
    return {"tokens": tokens, "norm_attn": norm_attn, "w_query": w_query, "key_projection": key_projection, "value_projection": value_projection, "w_out": w_out, "norm_ffn": norm_ffn, "w_router": w_router, "w_gate": w_gate, "w_up": w_up, "w_down": w_down, "routes": routes, "cotangent": cotangent}


@jax.custom_vjp
def lower_precision(v):
    return lax.optimization_barrier(v.astype(jnp.bfloat16)).astype(jnp.float32)

@jax.custom_vjp
def lower_precision_backward(v):
    return v

def low_keep(v):
    return (lower_precision(v), None)

def low_pass(kept, grad):
    return (grad,)

def back_keep(v):
    return (v, None)

def back_low(kept, grad):
    return (lower_precision(grad),)
lower_precision.defvjp(low_keep, low_pass)
lower_precision_backward.defvjp(back_keep, back_low)
epsilon = 1e-06
masked_value = -1e+30

def product_highest_precision(left, right):
    return jnp.dot(left, right, precision=lax.Precision.HIGHEST)

def rope_tables(token_count, width):
    half_width = width // 2
    places = (jnp.arange(token_count) % SEQUENCE_TOKENS).astype(jnp.float32)
    rates = jnp.exp(jnp.arange(half_width, dtype=jnp.float32) * (-2.0 * math.log(10000.0) / width))
    angles = places[:, None] * rates[None, :]
    return (jnp.cos(angles)[:, None, :], jnp.sin(angles)[:, None, :])

def apply_rotary(field, cosine_table, sine_table):
    half_width = field.shape[-1] // 2
    first = field[..., :half_width]
    second = field[..., half_width:]
    return jnp.concatenate([first * cosine_table - second * sine_table, second * cosine_table + first * sine_table], -1)

def block_layer(x_in, weight_pack, route_seq):
    norm_a, w_q, key_weight_local, value_weight_local, w_o, norm_f, w_r, w_g, w_u, w_d = weight_pack
    token_count = x_in.shape[0]
    query_groups = QUERY_HEADS // KEY_VALUE_HEADS
    inv_one = lax.rsqrt(lax.optimization_barrier(jnp.mean(x_in * x_in, -1, keepdims=True)) + epsilon)
    hidden_first = lower_precision(x_in * inv_one * norm_a)
    query_unrotated = lower_precision_backward(product_highest_precision(hidden_first, w_q)).reshape(token_count, QUERY_HEADS, HEAD_SIZE)
    key_unrotated = lower_precision_backward(product_highest_precision(hidden_first, key_weight_local)).reshape(token_count, KEY_VALUE_HEADS, HEAD_SIZE)
    value_entries = lower_precision_backward(lower_precision(product_highest_precision(hidden_first, value_weight_local))).reshape(token_count, KEY_VALUE_HEADS, HEAD_SIZE)
    cosine_table, sine_table = rope_tables(token_count, HEAD_SIZE)
    query_rotated = lower_precision(apply_rotary(query_unrotated, cosine_table, sine_table)).reshape(token_count, KEY_VALUE_HEADS, query_groups, HEAD_SIZE)
    key_rotated = lower_precision(apply_rotary(key_unrotated, cosine_table, sine_table))
    scores = lower_precision_backward(jnp.einsum('qhgd,khd->hgqk', query_rotated, key_rotated, precision=lax.Precision.HIGHEST) * HEAD_SIZE ** (-0.5))
    places = jnp.arange(token_count) // BLOCK
    allowed = places[None, :] <= places[:, None]
    masked = jnp.where(allowed, scores, masked_value)
    probs_low = lower_precision(jax.nn.softmax(masked, -1))
    attn = jnp.einsum('hgqk,khd->qhgd', probs_low, value_entries, precision=lax.Precision.HIGHEST)
    attn = lower_precision_backward(lower_precision(attn)).reshape(token_count, QUERY_HEADS * HEAD_SIZE)
    branch = lower_precision_backward(product_highest_precision(attn, w_o))
    resid = x_in + branch
    inv_two = lax.rsqrt(lax.optimization_barrier(jnp.mean(resid * resid, -1, keepdims=True)) + epsilon)
    h_two = lower_precision(resid * inv_two * norm_f)
    logits = lower_precision_backward(product_highest_precision(h_two, w_r))
    router_probs = jax.nn.softmax(logits, -1)
    choose = (route_seq[:, :, None] == jnp.arange(EXPERTS)[None, None, :]).astype(jnp.float32)
    gates = lax.optimization_barrier(jnp.sum(choose * router_probs[:, None, :], -1))
    combine = lax.optimization_barrier(jnp.sum(choose * gates[:, :, None], 1))

    def expert_step(total, pack):
        gate_w, up_w, down_w, weight_col = pack
        rows = lower_precision_backward(h_two)
        gate_pre = lower_precision_backward(product_highest_precision(rows, gate_w))
        up_pre = lower_precision_backward(product_highest_precision(rows, up_w))
        hidden = lower_precision(jax.nn.silu(gate_pre) * up_pre)
        result = lower_precision_backward(lower_precision(product_highest_precision(hidden, down_w)))
        return (total + weight_col[:, None] * result, None)
    moe_sum, unused = lax.scan(expert_step, jnp.zeros_like(x_in), (w_g, w_u, w_d, combine.T))
    return resid + moe_sum

def reference(tokens, norm_attn, w_query, key_projection, value_projection, w_out, norm_ffn, w_router, w_gate, w_up, w_down, routes, cotangent):
    params = tuple((arr.astype(jnp.float32) for arr in (norm_attn, w_query, key_projection, value_projection, w_out, norm_ffn, w_router, w_gate, w_up, w_down)))
    sequence_total = tokens.shape[0] // SEQUENCE_TOKENS
    width = tokens.shape[1]
    x_all = tokens.astype(jnp.float32).reshape(sequence_total, SEQUENCE_TOKENS, width)
    cot_all = cotangent.astype(jnp.float32).reshape(sequence_total, SEQUENCE_TOKENS, width)
    route_all = routes.reshape(sequence_total, SEQUENCE_TOKENS, TOPK)

    def one_seq(grads, pack):
        x_seq, route_seq, cot_seq = pack

        def forward(x_in, weight_pack):
            return block_layer(x_in, weight_pack, route_seq)
        value, pull = jax.vjp(forward, x_seq, params)
        d_x, d_params = pull(cot_seq)
        summed = tuple((acc + part for acc, part in zip(grads, d_params)))
        return (summed, (value.astype(jnp.bfloat16), d_x))
    zeros = tuple((jnp.zeros_like(arr) for arr in params))
    grads, (outputs, d_all) = lax.scan(one_seq, zeros, (x_all, route_all, cot_all))
    return (outputs.reshape(tokens.shape), d_all.reshape(tokens.shape[0], width), grads[0], grads[1], grads[2], grads[3], grads[4], grads[5], grads[6], grads[7], grads[8], grads[9])
```

```python
import math

import jax
import jax.numpy as jnp
from jax import lax
from jax.sharding import PartitionSpec as P

QUERY_HEADS = 24
KEY_VALUE_HEADS = 8
HEAD_SIZE = 64
TOPK = 8
SEQUENCE_TOKENS = 512
BLOCK = 256


epsilon = 1e-06
masked_value = -1e30


def rope_tables(token_count, width):
    half_width = width // 2
    places = (jnp.arange(token_count) % SEQUENCE_TOKENS).astype(jnp.float32)
    rates = jnp.exp(jnp.arange(half_width, dtype=jnp.float32) * (-2.0 * math.log(10000.0) / width))
    angles = places[:, None] * rates[None, :]
    return (jnp.cos(angles)[:, None, :], jnp.sin(angles)[:, None, :])


def apply_rotary(field, cosine_table, sine_table):
    half_width = field.shape[-1] // 2
    first = field[..., :half_width]
    second = field[..., half_width:]
    return jnp.concatenate(
        [first * cosine_table - second * sine_table, second * cosine_table + first * sine_table], -1
    )


def invert_rotary(field, cosine_table, sine_table):
    half_width = field.shape[-1] // 2
    first = field[..., :half_width]
    second = field[..., half_width:]
    return jnp.concatenate(
        [first * cosine_table + second * sine_table, second * cosine_table - first * sine_table], -1
    )


def norm_forward(field, gain):
    inverse = lax.rsqrt(jnp.mean(field * field, -1, keepdims=True) + epsilon)
    normal = field * inverse
    return ((normal * gain.astype(jnp.float32)).astype(jnp.bfloat16), normal, inverse)


def norm_backward(d_normed, normal, inverse, gain):
    scaled = d_normed * gain.astype(jnp.float32)
    d_field = inverse * (scaled - normal * jnp.mean(scaled * normal, -1, keepdims=True))
    return (d_field, jnp.sum(d_normed * normal, 0))


def score_block(queries, key_rows):
    places = jnp.arange(SEQUENCE_TOKENS) // BLOCK
    allowed = places[None, :] <= places[:, None]
    scores = jnp.einsum(
        "qhgd,khd->hgqk", queries, key_rows, preferred_element_type=jnp.float32
    ) * HEAD_SIZE ** (-0.5)
    return jnp.where(allowed, scores, masked_value)


def attend(pack):
    queries, key_rows, value_rows = pack
    scores = score_block(queries, key_rows)
    highest = jnp.max(scores, -1, keepdims=True)
    shifted = jnp.exp(scores - highest)
    totals = jnp.sum(shifted, -1, keepdims=True)
    probs_bf = (shifted / totals).astype(jnp.bfloat16)
    head_mix = jnp.einsum(
        "hgqk,khd->qhgd", probs_bf, value_rows, preferred_element_type=jnp.float32
    )
    return (head_mix.astype(jnp.bfloat16), highest + jnp.log(totals))


def attend_back(pack):
    queries, key_rows, value_rows, d_mix, log_totals = pack
    factor = HEAD_SIZE ** (-0.5)
    scores = score_block(queries, key_rows)
    probs_f = jnp.exp(scores - log_totals)
    probs_bf = probs_f.astype(jnp.bfloat16)
    d_probs = jnp.einsum("qhgd,khd->hgqk", d_mix, value_rows, preferred_element_type=jnp.float32)
    centre = jnp.sum(probs_f * d_probs, -1, keepdims=True)
    d_scores = (probs_f * (d_probs - centre)).astype(jnp.bfloat16)
    d_queries = (
        jnp.einsum("hgqk,khd->qhgd", d_scores, key_rows, preferred_element_type=jnp.float32)
        * factor
    )
    d_keys = (
        jnp.einsum("hgqk,qhgd->khd", d_scores, queries, preferred_element_type=jnp.float32) * factor
    )
    d_values = jnp.einsum("hgqk,qhgd->khd", probs_bf, d_mix, preferred_element_type=jnp.float32)
    return (d_queries, d_keys, d_values)


def per_device(
    tokens,
    norm_attn,
    w_query,
    key_projection,
    value_projection,
    w_out,
    norm_ffn,
    w_router,
    w_gate,
    w_up,
    w_down,
    routes,
    cotangent,
):
    token_count = tokens.shape[0]
    width = tokens.shape[1]
    experts_all = w_router.shape[1]
    query_groups = QUERY_HEADS // KEY_VALUE_HEADS
    sequence_total = token_count // SEQUENCE_TOKENS
    x_float = tokens.astype(jnp.float32)
    cot_all = lax.all_gather(cotangent, "ep", axis=0, tiled=True)
    hidden_first, normal_one, inverse_one = norm_forward(x_float, norm_attn)
    query_unrotated = jnp.dot(hidden_first, w_query, preferred_element_type=jnp.float32)
    key_unrotated = jnp.dot(hidden_first, key_projection, preferred_element_type=jnp.float32)
    value_row_block = jnp.dot(
        hidden_first, value_projection, preferred_element_type=jnp.float32
    ).astype(jnp.bfloat16)
    cosine_table, sine_table = rope_tables(token_count, HEAD_SIZE)
    query_rotated = apply_rotary(
        query_unrotated.reshape(token_count, QUERY_HEADS, HEAD_SIZE), cosine_table, sine_table
    ).astype(jnp.bfloat16)
    key_rotated = apply_rotary(
        key_unrotated.reshape(token_count, KEY_VALUE_HEADS, HEAD_SIZE), cosine_table, sine_table
    ).astype(jnp.bfloat16)
    query_sequence = query_rotated.reshape(
        sequence_total, SEQUENCE_TOKENS, KEY_VALUE_HEADS, query_groups, HEAD_SIZE
    )
    key_sequence = key_rotated.reshape(sequence_total, SEQUENCE_TOKENS, KEY_VALUE_HEADS, HEAD_SIZE)
    value_sequence = value_row_block.reshape(
        sequence_total, SEQUENCE_TOKENS, KEY_VALUE_HEADS, HEAD_SIZE
    )
    attn_seq, log_totals = lax.map(attend, (query_sequence, key_sequence, value_sequence))
    attn_flat = attn_seq.reshape(token_count, QUERY_HEADS * HEAD_SIZE)
    branch = jnp.dot(attn_flat, w_out, preferred_element_type=jnp.float32)
    resid = x_float + branch
    h_two, normal_two, inverse_two = norm_forward(resid, norm_ffn)
    logits = jnp.dot(h_two, w_router, preferred_element_type=jnp.float32)
    router_probs = jax.nn.softmax(logits, -1)
    expert_ids = jnp.arange(experts_all)
    chosen = jnp.max((routes[:, :, None] == jnp.arange(experts_all)[None, None, :]).astype(jnp.float32), 1)
    combine = chosen * router_probs
    h_all = lax.all_gather(h_two, "ep", axis=0, tiled=True)
    combine_all = lax.all_gather(combine, "ep", axis=0, tiled=True)
    holder = lax.axis_index("ep")
    held = w_gate.shape[0]
    weight = lax.dynamic_slice_in_dim(combine_all, holder * held, held, 1)
    y_part = jnp.zeros((h_all.shape[0], width), jnp.float32)
    dh_part = jnp.zeros((h_all.shape[0], width), jnp.float32)
    d_router_cols, grads = [], []
    gh_list, dg_list, du_list = [], [], []
    for e in range(held):
        gate_pre = jnp.dot(h_all, w_gate[e], preferred_element_type=jnp.float32)
        up_pre = jnp.dot(h_all, w_up[e], preferred_element_type=jnp.float32)
        back = jnp.einsum("td,fd->tf", cot_all, w_down[e], preferred_element_type=jnp.float32)
        column = weight[:, e : e + 1]
        sigma = jax.nn.sigmoid(gate_pre)
        swish = gate_pre * sigma
        hidden = (swish * up_pre).astype(jnp.bfloat16).astype(jnp.float32)
        d_router_cols.append(jnp.sum(hidden * back, -1))
        d_hidden = column * back
        dg = (d_hidden * up_pre * sigma * (1.0 + gate_pre * (1.0 - sigma))).astype(jnp.bfloat16)
        du = (d_hidden * swish).astype(jnp.bfloat16)
        gh = (column * hidden).astype(jnp.bfloat16)
        gh_list.append(gh)
        dg_list.append(dg)
        du_list.append(du)
        grads.append(
            (
                jnp.einsum("td,tf->df", h_all, dg, preferred_element_type=jnp.float32).astype(jnp.bfloat16),
                jnp.einsum("td,tf->df", h_all, du, preferred_element_type=jnp.float32).astype(jnp.bfloat16),
                jnp.einsum("tf,td->fd", gh, cot_all, preferred_element_type=jnp.float32).astype(jnp.bfloat16),
            )
        )
    gh_all, dg_all, du_all = (jnp.concatenate(v, 1) for v in (gh_list, dg_list, du_list))
    y_part = jnp.dot(gh_all, w_down.reshape(-1, width), preferred_element_type=jnp.float32).astype(jnp.bfloat16)
    wg_t = jnp.transpose(w_gate, (1, 0, 2)).reshape(width, -1)
    wu_t = jnp.transpose(w_up, (1, 0, 2)).reshape(width, -1)
    dh_part = (
        jnp.einsum("tf,df->td", dg_all, wg_t, preferred_element_type=jnp.float32)
        + jnp.einsum("tf,df->td", du_all, wu_t, preferred_element_type=jnp.float32)
    ).astype(jnp.bfloat16)
    d_router_held = jnp.stack(d_router_cols, 1)
    d_router_wide = lax.dynamic_update_slice_in_dim(
        jnp.zeros((h_all.shape[0], experts_all), jnp.float32), d_router_held, holder * held, 1
    )
    d_router = chosen * lax.psum_scatter(d_router_wide, "ep", scatter_dimension=0, tiled=True)
    dh_sum = lax.psum_scatter(dh_part, "ep", scatter_dimension=0, tiled=True)
    moe_sum = lax.psum_scatter(y_part, "ep", scatter_dimension=0, tiled=True)
    mixed = (resid + moe_sum.astype(jnp.float32)).astype(jnp.bfloat16)
    d_out = cotangent.astype(jnp.float32)
    d_logits = (
        router_probs * (d_router - jnp.sum(router_probs * d_router, -1, keepdims=True))
    ).astype(jnp.bfloat16)
    grad_router = jnp.einsum("td,te->de", h_two, d_logits, preferred_element_type=jnp.float32)
    d_htwo = jnp.einsum("te,de->td", d_logits, w_router, preferred_element_type=jnp.float32)
    d_htwo = d_htwo + dh_sum.astype(jnp.float32)
    grad_gate, grad_up, grad_down = (jnp.stack([g[i] for g in grads]) for i in range(3))
    d_resid_norm, grad_norm_ffn = norm_backward(d_htwo, normal_two, inverse_two, norm_ffn)
    d_resid = d_out + d_resid_norm
    d_branch = d_resid.astype(jnp.bfloat16)
    grad_out = jnp.einsum("ta,td->ad", attn_flat, d_branch, preferred_element_type=jnp.float32)
    attention_gradient = jnp.einsum(
        "td,ad->ta", d_branch, w_out, preferred_element_type=jnp.float32
    ).astype(jnp.bfloat16)
    attention_gradient = attention_gradient.reshape(
        sequence_total, SEQUENCE_TOKENS, KEY_VALUE_HEADS, query_groups, HEAD_SIZE
    )
    d_q_rot, rotated_key_gradient, value_sequence_gradient = lax.map(
        attend_back, (query_sequence, key_sequence, value_sequence, attention_gradient, log_totals)
    )
    d_q_pre = (
        invert_rotary(
            d_q_rot.reshape(token_count, QUERY_HEADS, HEAD_SIZE), cosine_table, sine_table
        )
        .reshape(token_count, QUERY_HEADS * HEAD_SIZE)
        .astype(jnp.bfloat16)
    )
    d_k_pre = (
        invert_rotary(
            rotated_key_gradient.reshape(token_count, KEY_VALUE_HEADS, HEAD_SIZE),
            cosine_table,
            sine_table,
        )
        .reshape(token_count, KEY_VALUE_HEADS * HEAD_SIZE)
        .astype(jnp.bfloat16)
    )
    value_rows_gradient = value_sequence_gradient.reshape(
        token_count, KEY_VALUE_HEADS * HEAD_SIZE
    ).astype(jnp.bfloat16)
    grad_query = jnp.einsum("td,tq->dq", hidden_first, d_q_pre, preferred_element_type=jnp.float32)
    grad_key = jnp.einsum("td,tq->dq", hidden_first, d_k_pre, preferred_element_type=jnp.float32)
    grad_value = jnp.einsum(
        "td,tq->dq", hidden_first, value_rows_gradient, preferred_element_type=jnp.float32
    )
    d_hone = jnp.einsum("tq,dq->td", d_q_pre, w_query, preferred_element_type=jnp.float32)
    d_hone = d_hone + jnp.einsum(
        "tq,dq->td", d_k_pre, key_projection, preferred_element_type=jnp.float32
    )
    d_hone = d_hone + jnp.einsum(
        "tq,dq->td", value_rows_gradient, value_projection, preferred_element_type=jnp.float32
    )
    d_x_norm, grad_norm_attn = norm_backward(d_hone, normal_one, inverse_one, norm_attn)
    d_input = d_resid + d_x_norm
    part_na, part_q, part_k, part_v, part_o, part_nf, part_r = (
        lax.psum_scatter(
            grad_norm_attn.astype(jnp.bfloat16), "ep", scatter_dimension=0, tiled=True
        ).astype(jnp.float32),
        lax.psum_scatter(
            grad_query.astype(jnp.bfloat16), "ep", scatter_dimension=0, tiled=True
        ).astype(jnp.float32),
        lax.psum_scatter(
            grad_key.astype(jnp.bfloat16), "ep", scatter_dimension=0, tiled=True
        ).astype(jnp.float32),
        lax.psum_scatter(
            grad_value.astype(jnp.bfloat16), "ep", scatter_dimension=0, tiled=True
        ).astype(jnp.float32),
        lax.psum_scatter(
            grad_out.astype(jnp.bfloat16), "ep", scatter_dimension=0, tiled=True
        ).astype(jnp.float32),
        lax.psum_scatter(
            grad_norm_ffn.astype(jnp.bfloat16), "ep", scatter_dimension=0, tiled=True
        ).astype(jnp.float32),
        lax.psum_scatter(
            grad_router.astype(jnp.bfloat16), "ep", scatter_dimension=0, tiled=True
        ).astype(jnp.float32),
    )
    part_gate, part_up, part_down = (grad_gate, grad_up, grad_down)
    sum_na, sum_q, sum_k, sum_v, sum_o, sum_nf, sum_r = lax.psum(
        (part_na, part_q, part_k, part_v, part_o, part_nf, part_r), "rep"
    )
    share_gate, share_up, share_down = (
        lax.psum_scatter(part_gate, "rep", scatter_dimension=1, tiled=True),
        lax.psum_scatter(part_up, "rep", scatter_dimension=1, tiled=True),
        lax.psum_scatter(part_down, "rep", scatter_dimension=2, tiled=True),
    )
    full_gate, full_up, full_down = (
        lax.all_gather(share_gate.astype(jnp.bfloat16), "rep", axis=1, tiled=True).astype(
            jnp.float32
        ),
        lax.all_gather(share_up.astype(jnp.bfloat16), "rep", axis=1, tiled=True).astype(
            jnp.float32
        ),
        lax.all_gather(share_down.astype(jnp.bfloat16), "rep", axis=2, tiled=True).astype(
            jnp.float32
        ),
    )
    return (
        mixed,
        d_input,
        sum_na,
        sum_q,
        sum_k,
        sum_v,
        sum_o,
        sum_nf,
        sum_r,
        full_gate,
        full_up,
        full_down,
    )


def solution(mesh):
    placed = (
        P(("rep", "ep"), None),
        P(),
        P(),
        P(),
        P(),
        P(),
        P(),
        P(),
        P("ep", None, None),
        P("ep", None, None),
        P("ep", None, None),
        P(("rep", "ep"), None),
        P(("rep", "ep"), None),
    )
    return jax.shard_map(
        per_device,
        mesh=mesh,
        in_specs=placed,
        out_specs=(
            P(("rep", "ep"), None),
            P(("rep", "ep"), None),
            P("ep"),
            P("ep", None),
            P("ep", None),
            P("ep", None),
            P("ep", None),
            P("ep"),
            P("ep", None),
            P("ep", None, None),
            P("ep", None, None),
            P("ep", None, None),
        ),
        check_vma=False,
    )
```

```python
import functools
import math

import jax
import jax.numpy as jnp
from jax import lax
from jax.experimental import pallas as pl
from jax.experimental.pallas import tpu as pltpu
from jax.sharding import PartitionSpec as P

QUERY_HEADS = 24
KEY_VALUE_HEADS = 8
HEAD_SIZE = 64
TOPK = 8
SEQUENCE_TOKENS = 512
BLOCK = 256
EARLY = 2


epsilon = 1e-06
masked_value = -1e30


def rope_tables(token_count, width):
    half_width = width // 2
    places = (jnp.arange(token_count) % SEQUENCE_TOKENS).astype(jnp.float32)
    rates = jnp.exp(jnp.arange(half_width, dtype=jnp.float32) * (-2.0 * math.log(10000.0) / width))
    angles = places[:, None] * rates[None, :]
    return (jnp.cos(angles)[:, None, :], jnp.sin(angles)[:, None, :])


def apply_rotary(field, cosine_table, sine_table):
    half_width = field.shape[-1] // 2
    first = field[..., :half_width]
    second = field[..., half_width:]
    return jnp.concatenate(
        [first * cosine_table - second * sine_table, second * cosine_table + first * sine_table], -1
    )


def invert_rotary(field, cosine_table, sine_table):
    half_width = field.shape[-1] // 2
    first = field[..., :half_width]
    second = field[..., half_width:]
    return jnp.concatenate(
        [first * cosine_table + second * sine_table, second * cosine_table - first * sine_table], -1
    )


def norm_forward(field, gain):
    inverse = lax.rsqrt(jnp.mean(field * field, -1, keepdims=True) + epsilon)
    normal = field * inverse
    return ((normal * gain.astype(jnp.float32)).astype(jnp.bfloat16), normal, inverse)


def norm_backward(d_normed, normal, inverse, gain):
    scaled = d_normed * gain.astype(jnp.float32)
    d_field = inverse * (scaled - normal * jnp.mean(scaled * normal, -1, keepdims=True))
    return (d_field, jnp.sum(d_normed * normal, 0))


def score_block(queries, key_rows):
    places = jnp.arange(SEQUENCE_TOKENS) // BLOCK
    allowed = places[None, :] <= places[:, None]
    scores = jnp.einsum(
        "qhgd,khd->hgqk", queries, key_rows, preferred_element_type=jnp.float32
    ) * HEAD_SIZE ** (-0.5)
    return jnp.where(allowed, scores, masked_value)


def attend(pack):
    queries, key_rows, value_rows = pack
    scores = score_block(queries, key_rows)
    highest = jnp.max(scores, -1, keepdims=True)
    shifted = jnp.exp(scores - highest)
    totals = jnp.sum(shifted, -1, keepdims=True)
    probs_bf = (shifted / totals).astype(jnp.bfloat16)
    head_mix = jnp.einsum(
        "hgqk,khd->qhgd", probs_bf, value_rows, preferred_element_type=jnp.float32
    )
    return (head_mix.astype(jnp.bfloat16), highest + jnp.log(totals))


def attend_back(pack):
    queries, key_rows, value_rows, d_mix, log_totals = pack
    factor = HEAD_SIZE ** (-0.5)
    scores = score_block(queries, key_rows)
    probs_f = jnp.exp(scores - log_totals)
    probs_bf = probs_f.astype(jnp.bfloat16)
    d_probs = jnp.einsum("qhgd,khd->hgqk", d_mix, value_rows, preferred_element_type=jnp.float32)
    centre = jnp.sum(probs_f * d_probs, -1, keepdims=True)
    d_scores = (probs_f * (d_probs - centre)).astype(jnp.bfloat16)
    d_queries = (
        jnp.einsum("hgqk,khd->qhgd", d_scores, key_rows, preferred_element_type=jnp.float32)
        * factor
    )
    d_keys = (
        jnp.einsum("hgqk,qhgd->khd", d_scores, queries, preferred_element_type=jnp.float32) * factor
    )
    d_values = jnp.einsum("hgqk,qhgd->khd", probs_bf, d_mix, preferred_element_type=jnp.float32)
    return (d_queries, d_keys, d_values)


SLOTS = 3


def ring_device(place, count):
    back = place // (count // 2)
    return (1 - back) * 2 * place + back * (2 * (count - 1 - place) + 1)


def ring_kernel(count, shapes, *refs):
    total = len(shapes)
    sources, sums = refs[:total], refs[total : 2 * total]
    held, terms = refs[2 * total : 3 * total], refs[3 * total : 4 * total]
    arrived, sent, loaded, stored, credit = refs[4 * total :]
    here = lax.axis_index("rep")
    odd = here % 2
    rank = here // 2 + odd * (count - 1 - 2 * (here // 2))
    after = ring_device((rank + 1) % count, count)
    before = ring_device((rank + count - 1) % count, count)
    hops = 2 * (count - 1)

    barrier = pltpu.get_barrier_semaphore()
    for neighbour in (before, after):
        pl.semaphore_signal(barrier, inc=1, device_id={"rep": neighbour})
    pl.semaphore_wait(barrier, 2)

    streams = [(index, way) for index in range(total) for way in (0, 1)]

    def columns(index, way):
        half = shapes[index][1] // 2
        return pl.ds(way * half, half)

    def send(index, way, hop):
        stream = 2 * index + way
        source = (hop + SLOTS - 1) % SLOTS
        slot = hop % SLOTS
        return pltpu.make_async_remote_copy(
            src_ref=held[index].at[way, source],
            dst_ref=held[index].at[way, slot],
            send_sem=sent.at[stream, slot],
            recv_sem=arrived.at[stream, slot],
            device_id={"rep": before if way else after},
        )

    def load(index, way, hop):
        step = hop + 2
        chunk = (rank + step) % count if way else (rank + 2 * count - step) % count
        return pltpu.make_async_copy(
            sources[index].at[chunk, :, columns(index, way)],
            terms[index].at[way, hop % 2],
            loaded.at[2 * index + way, hop % 2],
        )

    def first(index, way):
        chunk = (rank + 1) % count if way else (rank + count - 1) % count
        return pltpu.make_async_copy(
            sources[index].at[chunk, :, columns(index, way)],
            held[index].at[way, SLOTS - 1],
            stored.at[2 * index + way, SLOTS - 1],
        )

    def store(index, way, hop):
        step = hop - (count - 2)
        chunk = (rank + step) % count if way else (rank + count - step) % count
        return pltpu.make_async_copy(
            held[index].at[way, hop % SLOTS],
            sums[index].at[chunk, :, columns(index, way)],
            stored.at[2 * index + way, hop % SLOTS],
        )

    def release(index, way):
        pl.semaphore_signal(
            credit.at[2 * index + way], inc=1, device_id={"rep": after if way else before}
        )

    for index, way in streams:
        first(index, way).start()
    for index, way in streams:
        load(index, way, 0).start()
        load(index, way, 1).start()
    for index, way in streams:
        first(index, way).wait()
        send(index, way, 0).start()

    def take(index, way, hop):
        send(index, way, hop).wait_recv()
        send(index, way, hop).wait_send()

    def pass_on(index, way, hop):
        @pl.when(hop + 1 >= 2)
        def _():
            pl.semaphore_wait(credit.at[2 * index + way], 1)

        send(index, way, hop + 1).start()

    def add_step(hop, carry):
        for index, way in streams:
            take(index, way, hop)

            @pl.when(hop <= hops - 3)
            def _():
                release(index, way)

            load(index, way, hop).wait()
            slot = hop % SLOTS
            held[index][way, slot] = (
                held[index][way, slot].astype(jnp.float32)
                + terms[index][way, hop % 2].astype(jnp.float32)
            ).astype(jnp.bfloat16)
            pass_on(index, way, hop)

            @pl.when(hop + 2 <= count - 2)
            def _():
                load(index, way, hop + 2).start()

            @pl.when(hop == count - 2)
            def _():
                store(index, way, hop).start()

        return carry

    def hand_step(hop, carry):
        for index, way in streams:
            take(index, way, hop)
            store(index, way, hop - 1).wait()

            @pl.when(hop <= hops - 3)
            def _():
                release(index, way)

            @pl.when(hop + 1 < hops)
            def _():
                pass_on(index, way, hop)

            store(index, way, hop).start()

        return carry

    lax.fori_loop(0, count - 1, add_step, 0)
    lax.fori_loop(count - 1, hops, hand_step, 0)
    for index, way in streams:
        store(index, way, hops - 1).wait()


def ring_sum(sources):
    count = sources[0].shape[0]
    shapes = [source.shape[1:] for source in sources]
    total = len(shapes)
    size = sum(source.size for source in sources)
    halves = [(rows, columns // 2) for rows, columns in shapes]
    return pl.pallas_call(
        functools.partial(ring_kernel, count, shapes),
        out_shape=[jax.ShapeDtypeStruct(source.shape, source.dtype) for source in sources],
        in_specs=[pl.BlockSpec(memory_space=pl.ANY)] * total,
        out_specs=[pl.BlockSpec(memory_space=pl.ANY)] * total,
        scratch_shapes=[pltpu.VMEM((2, SLOTS) + half, jnp.bfloat16) for half in halves]
        + [pltpu.VMEM((2, 2) + half, jnp.bfloat16) for half in halves]
        + [
            pltpu.SemaphoreType.DMA((2 * total, SLOTS)),
            pltpu.SemaphoreType.DMA((2 * total, SLOTS)),
            pltpu.SemaphoreType.DMA((2 * total, 2)),
            pltpu.SemaphoreType.DMA((2 * total, SLOTS)),
            pltpu.SemaphoreType.REGULAR((2 * total,)),
        ],
        compiler_params=pltpu.CompilerParams(
            collective_id=0, has_side_effects=True, vmem_limit_bytes=48 * 2**20
        ),
        cost_estimate=pl.CostEstimate(flops=2 * size, bytes_accessed=8 * size, transcendentals=0),
        name="ring_sum",
    )(*sources)


def finish_kernel(*refs):
    units, (gate, up, down) = refs[:-3], refs[-3:]
    for index, unit in enumerate(units):

        @pl.when(pl.program_id(0) == index)
        def _():
            rows = unit.shape[1] // 3
            cut = rows * unit.shape[2] // down.shape[2]
            columns = unit.shape[2]
            for k in range(unit.shape[0]):
                gate[0, k * rows : (k + 1) * rows] = unit[k, :rows].astype(jnp.float32)
                up[0, k * rows : (k + 1) * rows] = unit[k, rows : 2 * rows].astype(jnp.float32)
                for j in range(down.shape[2] // columns):
                    start = 2 * rows + j * cut
                    down[0, k * cut : (k + 1) * cut, j * columns : (j + 1) * columns] = unit[
                        k, start : start + cut
                    ].astype(jnp.float32)


def finish(units, width):
    experts = len(units)
    count, rows3, columns = units[0].shape
    rows = rows3 // 3
    pair = 2
    last = count // pair - 1

    def place(index):
        def chunk(e, c):
            return (jnp.where(e == index, c, jnp.where(e < index, 0, last)), 0, 0)

        return chunk

    return pl.pallas_call(
        finish_kernel,
        grid=(experts, count // pair),
        in_specs=[pl.BlockSpec((pair, rows3, columns), place(index)) for index in range(experts)],
        out_specs=[
            pl.BlockSpec((1, pair * rows, columns), lambda e, c: (e, c, 0)),
            pl.BlockSpec((1, pair * rows, columns), lambda e, c: (e, c, 0)),
            pl.BlockSpec((1, pair * rows * columns // width, width), lambda e, c: (e, c, 0)),
        ],
        out_shape=[
            jax.ShapeDtypeStruct((experts, width, columns), jnp.float32),
            jax.ShapeDtypeStruct((experts, width, columns), jnp.float32),
            jax.ShapeDtypeStruct((experts, columns, width), jnp.float32),
        ],
        name="finish",
        compiler_params=pltpu.CompilerParams(vmem_limit_bytes=48 * 2**20),
    )(*units)


def swap_core(value):
    return lax.ppermute(value, "ep", [(0, 1), (1, 0), (2, 3), (3, 2)])


def swap_chip(value):
    return lax.ppermute(value, "ep", [(0, 2), (2, 0), (1, 3), (3, 1)])


def gather_group(block):
    far = swap_chip(block)
    return (block, swap_core(block), far, swap_core(far))


def in_order(blocks, place):
    stacked = jnp.stack(blocks)
    return jnp.concatenate(
        [lax.dynamic_index_in_dim(stacked, place ^ k, 0, keepdims=False) for k in range(len(blocks))], 0
    )


def add_bf(a, b):
    return (a.astype(jnp.float32) + b.astype(jnp.float32)).astype(jnp.bfloat16)


def scatter_group(blocks):
    near = add_bf(blocks[0], swap_core(blocks[1]))
    far = add_bf(blocks[2], swap_core(blocks[3]))
    return near.astype(jnp.float32) + swap_chip(far).astype(jnp.float32)


def per_device(
    tokens,
    norm_attn,
    w_query,
    key_projection,
    value_projection,
    w_out,
    norm_ffn,
    w_router,
    w_gate,
    w_up,
    w_down,
    routes,
    cotangent,
):
    token_count = tokens.shape[0]
    width = tokens.shape[1]
    experts_all = w_router.shape[1]
    query_groups = QUERY_HEADS // KEY_VALUE_HEADS
    sequence_total = token_count // SEQUENCE_TOKENS
    x_float = tokens.astype(jnp.float32)
    cot_blocks = gather_group(cotangent)
    cot_all = jnp.concatenate(cot_blocks, 0)
    hidden_first, normal_one, inverse_one = norm_forward(x_float, norm_attn)
    query_unrotated = jnp.dot(hidden_first, w_query, preferred_element_type=jnp.float32)
    key_unrotated = jnp.dot(hidden_first, key_projection, preferred_element_type=jnp.float32)
    value_row_block = jnp.dot(
        hidden_first, value_projection, preferred_element_type=jnp.float32
    ).astype(jnp.bfloat16)
    cosine_table, sine_table = rope_tables(token_count, HEAD_SIZE)
    query_rotated = apply_rotary(
        query_unrotated.reshape(token_count, QUERY_HEADS, HEAD_SIZE), cosine_table, sine_table
    ).astype(jnp.bfloat16)
    key_rotated = apply_rotary(
        key_unrotated.reshape(token_count, KEY_VALUE_HEADS, HEAD_SIZE), cosine_table, sine_table
    ).astype(jnp.bfloat16)
    query_sequence = query_rotated.reshape(
        sequence_total, SEQUENCE_TOKENS, KEY_VALUE_HEADS, query_groups, HEAD_SIZE
    )
    key_sequence = key_rotated.reshape(sequence_total, SEQUENCE_TOKENS, KEY_VALUE_HEADS, HEAD_SIZE)
    value_sequence = value_row_block.reshape(
        sequence_total, SEQUENCE_TOKENS, KEY_VALUE_HEADS, HEAD_SIZE
    )
    attn_seq, log_totals = lax.map(attend, (query_sequence, key_sequence, value_sequence))
    attn_flat = attn_seq.reshape(token_count, QUERY_HEADS * HEAD_SIZE)
    branch = jnp.dot(attn_flat, w_out, preferred_element_type=jnp.float32)
    resid = x_float + branch
    h_two, normal_two, inverse_two = norm_forward(resid, norm_ffn)
    logits = jnp.dot(h_two, w_router, preferred_element_type=jnp.float32)
    router_probs = jax.nn.softmax(logits, -1)
    expert_ids = jnp.arange(experts_all)
    chosen = jnp.max((routes[:, :, None] == jnp.arange(experts_all)[None, None, :]).astype(jnp.float32), 1)
    combine = chosen * router_probs
    h_all = jnp.concatenate(gather_group(h_two), 0)
    combine_all = jnp.concatenate(gather_group(combine), 0)
    holder = lax.axis_index("ep")
    held = w_gate.shape[0]
    replicas = lax.axis_size("rep")
    weight = lax.dynamic_slice_in_dim(combine_all, holder * held, held, 1)
    d_router_cols, units = [], []
    gh_list, dg_list, du_list = [], [], []
    for e in range(held):
        gate_pre = jnp.dot(h_all, w_gate[e], preferred_element_type=jnp.float32)
        up_pre = jnp.dot(h_all, w_up[e], preferred_element_type=jnp.float32)
        back = jnp.einsum("td,fd->tf", cot_all, w_down[e], preferred_element_type=jnp.float32)
        column = weight[:, e : e + 1]
        sigma = jax.nn.sigmoid(gate_pre)
        swish = gate_pre * sigma
        hidden = (swish * up_pre).astype(jnp.bfloat16).astype(jnp.float32)
        d_router_cols.append(jnp.sum(hidden * back, -1))
        d_hidden = column * back
        dg = (d_hidden * up_pre * sigma * (1.0 + gate_pre * (1.0 - sigma))).astype(jnp.bfloat16)
        du = (d_hidden * swish).astype(jnp.bfloat16)
        gh = (column * hidden).astype(jnp.bfloat16)
        gh_list.append(gh)
        dg_list.append(dg)
        du_list.append(du)
        gate_grad = jnp.einsum("td,tf->df", h_all, dg, preferred_element_type=jnp.float32)
        up_grad = jnp.einsum("td,tf->df", h_all, du, preferred_element_type=jnp.float32)
        down_grad = jnp.einsum("tf,td->fd", gh, cot_all, preferred_element_type=jnp.float32)
        hidden_units = down_grad.shape[0]
        rows = width // replicas
        down_cut = down_grad.astype(jnp.bfloat16).reshape(replicas, hidden_units // replicas, width // hidden_units, hidden_units)
        down_cut = jnp.transpose(down_cut, (0, 2, 1, 3)).reshape(replicas, rows, hidden_units)
        unit = jnp.concatenate(
            [
                gate_grad.astype(jnp.bfloat16).reshape(replicas, rows, hidden_units),
                up_grad.astype(jnp.bfloat16).reshape(replicas, rows, hidden_units),
                down_cut,
            ],
            1,
        )
        h_all, cot_all, unit = lax.optimization_barrier((h_all, cot_all, unit))
        units.append(unit)
    totals = [
        lax.all_gather(
            lax.psum_scatter(unit, "rep", scatter_dimension=0, tiled=True), "rep", axis=0, tiled=True
        )
        for unit in units[:EARLY]
    ]

    def blocks_of(value):
        return [value[k * token_count : (k + 1) * token_count] for k in range(4)]

    dh_part = sum(
        jnp.einsum("tf,df->td", dg_list[e], w_gate[e], preferred_element_type=jnp.float32)
        + jnp.einsum("tf,df->td", du_list[e], w_up[e], preferred_element_type=jnp.float32)
        for e in range(held)
    ).astype(jnp.bfloat16)
    y_part = sum(
        jnp.dot(gh_list[e], w_down[e], preferred_element_type=jnp.float32) for e in range(held)
    ).astype(jnp.bfloat16)
    d_router_held = jnp.stack(d_router_cols, 1)
    d_router_wide = lax.dynamic_update_slice_in_dim(
        jnp.zeros((h_all.shape[0], experts_all), jnp.float32), d_router_held, holder * held, 1
    )
    router_blocks = blocks_of(d_router_wide)
    d_router = router_blocks[0] + swap_core(router_blocks[1])
    d_router = chosen * (d_router + swap_chip(router_blocks[2] + swap_core(router_blocks[3])))
    dh_sum = scatter_group(blocks_of(dh_part))
    mixed = (resid + scatter_group(blocks_of(y_part))).astype(jnp.bfloat16)
    d_out = cotangent.astype(jnp.float32)
    d_logits = (
        router_probs * (d_router - jnp.sum(router_probs * d_router, -1, keepdims=True))
    ).astype(jnp.bfloat16)
    grad_router = jnp.einsum("td,te->de", h_two, d_logits, preferred_element_type=jnp.float32)
    d_htwo = jnp.einsum("te,de->td", d_logits, w_router, preferred_element_type=jnp.float32)
    d_htwo = d_htwo + dh_sum
    d_resid_norm, grad_norm_ffn = norm_backward(d_htwo, normal_two, inverse_two, norm_ffn)
    d_resid = d_out + d_resid_norm
    d_branch = d_resid.astype(jnp.bfloat16)
    grad_out = jnp.einsum("ta,td->ad", attn_flat, d_branch, preferred_element_type=jnp.float32)
    attention_gradient = jnp.einsum(
        "td,ad->ta", d_branch, w_out, preferred_element_type=jnp.float32
    ).astype(jnp.bfloat16)
    attention_gradient = attention_gradient.reshape(
        sequence_total, SEQUENCE_TOKENS, KEY_VALUE_HEADS, query_groups, HEAD_SIZE
    )
    d_q_rot, rotated_key_gradient, value_sequence_gradient = lax.map(
        attend_back, (query_sequence, key_sequence, value_sequence, attention_gradient, log_totals)
    )
    d_q_pre = (
        invert_rotary(
            d_q_rot.reshape(token_count, QUERY_HEADS, HEAD_SIZE), cosine_table, sine_table
        )
        .reshape(token_count, QUERY_HEADS * HEAD_SIZE)
        .astype(jnp.bfloat16)
    )
    d_k_pre = (
        invert_rotary(
            rotated_key_gradient.reshape(token_count, KEY_VALUE_HEADS, HEAD_SIZE),
            cosine_table,
            sine_table,
        )
        .reshape(token_count, KEY_VALUE_HEADS * HEAD_SIZE)
        .astype(jnp.bfloat16)
    )
    value_rows_gradient = value_sequence_gradient.reshape(
        token_count, KEY_VALUE_HEADS * HEAD_SIZE
    ).astype(jnp.bfloat16)
    grad_query = jnp.einsum("td,tq->dq", hidden_first, d_q_pre, preferred_element_type=jnp.float32)
    grad_key = jnp.einsum("td,tq->dq", hidden_first, d_k_pre, preferred_element_type=jnp.float32)
    grad_value = jnp.einsum(
        "td,tq->dq", hidden_first, value_rows_gradient, preferred_element_type=jnp.float32
    )
    d_hone = jnp.einsum("tq,dq->td", d_q_pre, w_query, preferred_element_type=jnp.float32)
    d_hone = d_hone + jnp.einsum(
        "tq,dq->td", d_k_pre, key_projection, preferred_element_type=jnp.float32
    )
    d_hone = d_hone + jnp.einsum(
        "tq,dq->td", value_rows_gradient, value_projection, preferred_element_type=jnp.float32
    )
    d_x_norm, grad_norm_attn = norm_backward(d_hone, normal_one, inverse_one, norm_attn)
    d_input = d_resid + d_x_norm
    def group_part(value):
        quarter = value.shape[0] // 4
        cut = value.reshape(4, quarter, value.shape[1])
        blocks = [lax.dynamic_index_in_dim(cut, holder ^ k, 0, keepdims=False) for k in range(4)]
        return scatter_group(blocks).astype(jnp.bfloat16)

    def in_chunks(parts):
        wide = jnp.concatenate(parts, 1)
        chunk_rows = -(-wide.shape[0] // (8 * replicas)) * 8
        wide = jnp.pad(wide, ((0, chunk_rows * replicas - wide.shape[0]), (0, 0)))
        return wide.reshape(replicas, chunk_rows, wide.shape[1])

    def out_of_chunks(total):
        return total.reshape(-1, total.shape[2])[: width // 4].astype(jnp.float32)

    lanes = 128
    filler = jnp.zeros((width, lanes - experts_all - 1), jnp.float32)
    part_o = group_part(
        jnp.concatenate([grad_out, grad_router, grad_norm_ffn[:, None], filler], 1).astype(jnp.bfloat16)
    )
    part_qkv = group_part(
        jnp.concatenate(
            [grad_query, grad_key, grad_value, grad_norm_attn[:, None], jnp.zeros((width, lanes - 1))], 1
        ).astype(jnp.bfloat16)
    )
    dense = in_chunks([part_o, part_qkv])
    *late, dense = ring_sum([*units[EARLY:], dense])
    dense = out_of_chunks(dense)
    key_width = grad_key.shape[1]
    edges = []
    for part in (width, experts_all, 1, lanes - experts_all - 1, width, key_width, key_width, 1):
        edges.append(part + (edges[-1] if edges else 0))
    sum_o, sum_r, sum_nf, _, sum_q, sum_k, sum_v, sum_na, _ = jnp.split(dense, edges, 1)
    sum_nf, sum_na = (sum_nf[:, 0], sum_na[:, 0])
    full_gate, full_up, full_down = finish(totals + late, width)
    return (
        mixed,
        d_input,
        sum_na,
        sum_q,
        sum_k,
        sum_v,
        sum_o,
        sum_nf,
        sum_r,
        full_gate,
        full_up,
        full_down,
    )


def solution(mesh):
    placed = (
        P(("rep", "ep"), None),
        P(),
        P(),
        P(),
        P(),
        P(),
        P(),
        P(),
        P("ep", None, None),
        P("ep", None, None),
        P("ep", None, None),
        P(("rep", "ep"), None),
        P(("rep", "ep"), None),
    )
    return jax.shard_map(
        per_device,
        mesh=mesh,
        in_specs=placed,
        out_specs=(
            P(("rep", "ep"), None),
            P(("rep", "ep"), None),
            P("ep"),
            P("ep", None),
            P("ep", None),
            P("ep", None),
            P("ep", None),
            P("ep"),
            P("ep", None),
            P("ep", None, None),
            P("ep", None, None),
            P("ep", None, None),
        ),
        check_vma=False,
    )
```

```python
import functools
import math

import jax
import jax.numpy as jnp
from jax import lax
from jax.experimental import pallas as pl
from jax.experimental.pallas import tpu as pltpu
from jax.sharding import PartitionSpec as P

QUERY_HEADS = 24
KEY_VALUE_HEADS = 8
HEAD_SIZE = 64
TOPK = 8
SEQUENCE_TOKENS = 512
BLOCK = 256
EARLY = 1


epsilon = 1e-06
masked_value = -1e30


def rope_tables(token_count):
    half = HEAD_SIZE // 2
    places = (jnp.arange(token_count) % SEQUENCE_TOKENS).astype(jnp.float32)
    rates = jnp.exp(jnp.arange(half, dtype=jnp.float32) * (-2.0 * math.log(10000.0) / HEAD_SIZE))
    angles = places[:, None] * rates[None, :]
    cosine, sine = jnp.cos(angles), jnp.sin(angles)
    return (
        jnp.concatenate([cosine] * 4, 1),
        jnp.concatenate([-sine, sine] * 2, 1),
    )


def contract(left, right, left_dim, right_dim):
    return lax.dot_general(
        left, right, (((left_dim,), (right_dim,)), ((), ())), preferred_element_type=jnp.float32
    )


def whole(array):
    return pl.BlockSpec(
        array.shape, lambda *_: (0,) * array.ndim, pipeline_mode=pl.Buffered(1)
    )


def each(array):
    return pl.BlockSpec((1,) + array.shape[1:], lambda e, *_: (e,) + (0,) * (array.ndim - 1))


VMEM_BYTES = 56 * 2**20


def expert_kernel(tile, h0, h1, c0, c1, gates0, gates1, w_gate, w_up, w_down, gh, dg, du, d_router0, d_router1):
    e = pl.program_id(0)
    tokens, lanes = gates0.shape
    lane = lax.broadcasted_iota(jnp.int32, (tile, lanes), 1)

    @pl.when(e == 0)
    def _():
        d_router0[...] = jnp.zeros_like(d_router0)
        d_router1[...] = jnp.zeros_like(d_router1)

    for base, rows_h, rows_c, gates, d_router in (
        (0, h0, c0, gates0, d_router0),
        (tokens, h1, c1, gates1, d_router1),
    ):
        for start in range(0, tokens, tile):
            rows = slice(start, start + tile)
            out = slice(base + start, base + start + tile)
            entries = rows_h[rows, :]
            gate_pre = contract(entries, w_gate[0], 1, 0)
            up_pre = contract(entries, w_up[0], 1, 0)
            back = contract(rows_c[rows, :], w_down[0], 1, 1)
            column = jnp.sum(jnp.where(lane == e, gates[rows, :], 0.0), 1, keepdims=True)
            sigma = jax.nn.sigmoid(gate_pre)
            swish = gate_pre * sigma
            hidden = (swish * up_pre).astype(jnp.bfloat16).astype(jnp.float32)
            d_router[rows, :] = jnp.where(
                lane == e, jnp.sum(hidden * back, 1, keepdims=True), d_router[rows, :]
            )
            d_hidden = column * back
            dg[0, out, :] = (
                d_hidden * up_pre * (sigma * (1.0 + gate_pre * (1.0 - sigma)))
            ).astype(jnp.bfloat16)
            du[0, out, :] = (d_hidden * swish).astype(jnp.bfloat16)
            gh[0, out, :] = (column * hidden).astype(jnp.bfloat16)


def expert_pass(hs, cots, gates, w_gate, w_up, w_down):
    count, width = hs[0].shape
    tokens = 2 * count
    held, _, hidden_units = w_gate.shape
    part = jax.ShapeDtypeStruct((held, tokens, hidden_units), jnp.bfloat16)
    gate_shape = gates[0].shape
    return pl.pallas_call(
        functools.partial(expert_kernel, 256),
        grid=(held,),
        in_specs=[whole(a) for a in (*hs, *cots, *gates)] + [each(a) for a in (w_gate, w_up, w_down)],
        out_specs=[each(part)] * 3 + [pl.BlockSpec(gate_shape, lambda e: (0, 0))] * 2,
        out_shape=[part] * 3 + [jax.ShapeDtypeStruct(gate_shape, jnp.float32)] * 2,
        compiler_params=pltpu.CompilerParams(vmem_limit_bytes=VMEM_BYTES),
        cost_estimate=pl.CostEstimate(
            flops=6 * held * tokens * width * hidden_units,
            bytes_accessed=6 * held * width * hidden_units,
            transcendentals=held * tokens * hidden_units,
        ),
        name="expert_pass",
    )(*hs, *cots, *gates, w_gate, w_up, w_down)


def weight_kernel(*refs):
    hs, cots, passes, unit = refs[:4], refs[4:8], refs[8:14], refs[14]
    kind = pl.program_id(1)

    def put(lefts, rights):
        count = lefts[0].shape[0]
        result = sum(
            contract(lefts[k][...], rights[k // 2][0, (k % 2) * count : (k % 2 + 1) * count], 0, 0)
            for k in range(4)
        ).astype(jnp.bfloat16)
        rows = unit.shape[3]
        for j in range(unit.shape[1]):
            unit[0, j, 0] = result[j * rows : (j + 1) * rows]

    pl.when(kind == 0)(lambda: put(hs, passes[2:4]))
    pl.when(kind == 1)(lambda: put(hs, passes[4:6]))
    pl.when(kind == 2)(lambda: put(cots, passes[:2]))


def weight_grads(count, first, many, hs, cots, ghs, dgs, dus):
    width = hs[0].shape[1]
    _, tokens, hidden_units = dgs[0].shape
    entry = pl.BlockSpec((1, tokens, hidden_units), lambda e, k: (e + first, 0, 0))
    unit = pl.pallas_call(
        weight_kernel,
        grid=(many, 3),
        in_specs=[whole(hs[0])] * 8 + [entry] * 6,
        out_specs=pl.BlockSpec((1, count, 1, width // count, hidden_units), lambda e, k: (e, 0, k, 0, 0)),
        out_shape=jax.ShapeDtypeStruct((many, count, 3, width // count, hidden_units), jnp.bfloat16),
        compiler_params=pltpu.CompilerParams(vmem_limit_bytes=VMEM_BYTES),
        cost_estimate=pl.CostEstimate(
            flops=12 * many * tokens * width * hidden_units,
            bytes_accessed=6 * many * (width + 2 * tokens) * hidden_units,
            transcendentals=0,
        ),
        name="weight_grads",
    )(*hs, *cots, *ghs, *dgs, *dus)
    return unit.reshape(many, count, 3 * (width // count), hidden_units)


def sum_kernel(right_dim, pairs, *refs):
    lefts, rights, outs, total = refs[:pairs], refs[pairs : 2 * pairs], refs[-3:-1], refs[-1]
    e = pl.program_id(0)
    term = sum(contract(left[0], right[0], 1, right_dim) for left, right in zip(lefts, rights))

    @pl.when(e == 0)
    def _():
        total[...] = term

    @pl.when(e > 0)
    def _():
        total[...] += term

    @pl.when(e == pl.num_programs(0) - 1)
    def _():
        for k, out in enumerate(outs):
            count = out.shape[0]
            out[...] = total[k * count : (k + 1) * count].astype(out.dtype)


def sum_over_experts(lefts, rights, right_dim):
    held, tokens, inner = lefts[0].shape
    width = rights[0].shape[2 - right_dim]
    return pl.pallas_call(
        functools.partial(sum_kernel, right_dim, len(lefts)),
        grid=(held,),
        in_specs=[each(a) for a in lefts] + [each(a) for a in rights],
        out_specs=[pl.BlockSpec((tokens // 2, width), lambda e: (0, 0))] * 2,
        out_shape=[jax.ShapeDtypeStruct((tokens // 2, width), jnp.bfloat16)] * 2,
        scratch_shapes=[pltpu.VMEM((tokens, width), jnp.float32)],
        compiler_params=pltpu.CompilerParams(vmem_limit_bytes=VMEM_BYTES),
        cost_estimate=pl.CostEstimate(
            flops=2 * len(lefts) * held * tokens * width * inner,
            bytes_accessed=2 * len(lefts) * held * (tokens + width) * inner,
            transcendentals=0,
        ),
        name="sum_over_experts",
    )(*lefts, *rights)


def rotate(values, cosine, sine, way):
    lane = lax.broadcasted_iota(jnp.int32, cosine.shape, 1)
    first = lane % HEAD_SIZE < HEAD_SIZE // 2
    lanes = cosine.shape[1]
    half = HEAD_SIZE // 2
    pieces = []
    for start in range(0, values.shape[1], lanes):
        piece = values[:, start : start + lanes]
        other = jnp.where(first, pltpu.roll(piece, lanes - half, 1), pltpu.roll(piece, half, 1))
        pieces.append(piece * cosine + way * (other * sine))
    return jnp.concatenate(pieces, 1)


def heads_of(array, group, rows, queries):
    return jnp.concatenate(
        [
            array[rows, (group * queries + j) * HEAD_SIZE : (group * queries + j + 1) * HEAD_SIZE]
            for j in range(queries)
        ],
        0,
    )


def attention_kernel(
    tokens, norm_attn, w_query, w_key, w_value, cosine, sine, w_out, norm_ffn, w_router, routes,
    normed, queries, keys, values, log_totals, attn, resid, h_two, probs, combine,
):
    count, width = tokens.shape
    field = tokens[...].astype(jnp.float32)
    inverse = lax.rsqrt(jnp.mean(field * field, -1, keepdims=True) + epsilon)
    first = (field * inverse * norm_attn[...].astype(jnp.float32)).astype(jnp.bfloat16)
    normed[...] = first
    queries[...] = rotate(contract(first, w_query[...], 1, 0), cosine[...], sine[...], 1).astype(jnp.bfloat16)
    keys[...] = rotate(contract(first, w_key[...], 1, 0), cosine[...], sine[...], 1).astype(jnp.bfloat16)
    values[...] = contract(first, w_value[...], 1, 0).astype(jnp.bfloat16)
    groups = keys.shape[1] // HEAD_SIZE
    per_group = queries.shape[1] // keys.shape[1]
    lane = lax.broadcasted_iota(jnp.int32, (BLOCK, log_totals.shape[1]), 1)
    for block in range(count // BLOCK):
        rows = slice(block * BLOCK, (block + 1) * BLOCK)
        seen = slice(0, (block + 1) * BLOCK)
        logs = jnp.zeros((BLOCK, log_totals.shape[1]), jnp.float32)
        for group in range(groups):
            cut = slice(group * HEAD_SIZE, (group + 1) * HEAD_SIZE)
            scores = contract(heads_of(queries, group, rows, per_group), keys[seen, cut], 1, 1)
            scores = scores * HEAD_SIZE ** (-0.5)
            highest = jnp.max(scores, -1, keepdims=True)
            shifted = jnp.exp(scores - highest)
            sums = jnp.sum(shifted, -1, keepdims=True)
            probs_bf = (shifted * (1.0 / sums)).astype(jnp.bfloat16)
            mix = contract(probs_bf, values[seen, cut], 1, 0).astype(jnp.bfloat16)
            log_sum = highest + jnp.log(sums)
            for j in range(per_group):
                head = group * per_group + j
                part = slice(j * BLOCK, (j + 1) * BLOCK)
                attn[rows, head * HEAD_SIZE : (head + 1) * HEAD_SIZE] = mix[part]
                logs = jnp.where(lane == head, log_sum[part], logs)
        log_totals[rows, :] = logs
    total = field + contract(attn[...], w_out[...], 1, 0)
    resid[...] = total
    inverse = lax.rsqrt(jnp.mean(total * total, -1, keepdims=True) + epsilon)
    second = (total * inverse * norm_ffn[...].astype(jnp.float32)).astype(jnp.bfloat16)
    h_two[...] = second
    logits = contract(second, w_router[...], 1, 0)
    lane = lax.broadcasted_iota(jnp.int32, logits.shape, 1)
    experts = probs.shape[1]
    logits = jnp.where(lane < experts, logits, masked_value)
    shifted = jnp.exp(logits - jnp.max(logits, -1, keepdims=True))
    soft = shifted / jnp.sum(shifted, -1, keepdims=True)
    chosen = jnp.zeros(logits.shape, jnp.bool_)
    for k in range(routes.shape[1]):
        chosen = chosen | (routes[:, k : k + 1] == lane)
    probs[...] = soft[:, :experts]
    combine[...] = jnp.where(chosen, soft, 0.0)[:, :experts]


LANES = 128


def attention_forward(tokens, norm_attn, w_query, w_key, w_value, cosine, sine, w_out, norm_ffn, w_router, routes):
    count, width = tokens.shape
    experts = w_router.shape[1]
    wide_router = jnp.pad(w_router, ((0, 0), (0, LANES - experts)))
    key_width = w_key.shape[1]
    shape = jax.ShapeDtypeStruct
    return pl.pallas_call(
        attention_kernel,
        out_shape=[
            shape((count, width), jnp.bfloat16),
            shape((count, width), jnp.bfloat16),
            shape((count, key_width), jnp.bfloat16),
            shape((count, key_width), jnp.bfloat16),
            shape((count, LANES), jnp.float32),
            shape((count, width), jnp.bfloat16),
            shape((count, width), jnp.float32),
            shape((count, width), jnp.bfloat16),
            shape((count, experts), jnp.float32),
            shape((count, experts), jnp.float32),
        ],
        compiler_params=pltpu.CompilerParams(vmem_limit_bytes=VMEM_BYTES),
        cost_estimate=pl.CostEstimate(
            flops=6 * count * width * width, bytes_accessed=8 * width * width, transcendentals=24 * count * count
        ),
        name="attention_forward",
    )(
        tokens, norm_attn[None], w_query, w_key, w_value, cosine, sine, w_out, norm_ffn[None], wide_router, routes
    )


def as_lane(row):
    first = lax.broadcasted_iota(jnp.int32, (LANES, row.shape[1]), 0) == 0
    return jnp.where(first, row, 0.0).T.astype(jnp.bfloat16)


def attention_back_kernel(
    dh_own, dh_near, dh_far, d_router, probs, resid, norm_ffn, cotangent, w_router, w_out, h_two, attn,
    queries, keys, values, log_totals, cosine, sine,
    d_resid, d_pre, grad_out, d_branch, d_attn, d_queries, d_keys, d_values,
):
    count, width = resid.shape
    experts = probs.shape[1]
    soft = probs[...]
    to_router = d_router[...]
    d_logits = (soft * (to_router - jnp.sum(soft * to_router, -1, keepdims=True))).astype(jnp.bfloat16)
    d_logits = jnp.concatenate([d_logits, jnp.zeros((count, LANES - experts), jnp.bfloat16)], 1)
    d_normed = (
        dh_own[...].astype(jnp.float32)
        + dh_near[...].astype(jnp.float32)
        + dh_far[...].astype(jnp.float32)
        + contract(d_logits, w_router[...], 1, 1)
    )
    total = resid[...]
    inverse = lax.rsqrt(jnp.mean(total * total, -1, keepdims=True) + epsilon)
    normal = total * inverse
    scaled = d_normed * norm_ffn[...].astype(jnp.float32)
    back = cotangent[...].astype(jnp.float32) + inverse * (
        scaled - normal * jnp.mean(scaled * normal, -1, keepdims=True)
    )
    d_resid[...] = back
    d_branch[...] = back.astype(jnp.bfloat16)
    grad_out[:, :width] = contract(attn[...], d_branch[...], 0, 0).astype(jnp.bfloat16)
    grad_out[:, width : width + LANES] = contract(h_two[...], d_logits, 0, 0).astype(jnp.bfloat16)
    grad_out[:, width + LANES :] = as_lane(jnp.sum(d_normed * normal, 0, keepdims=True))
    d_attn[...] = contract(d_branch[...], w_out[...], 1, 1).astype(jnp.bfloat16)
    groups = keys.shape[1] // HEAD_SIZE
    per_group = queries.shape[1] // keys.shape[1]
    factor = HEAD_SIZE ** (-0.5)
    lane = lax.broadcasted_iota(jnp.int32, (BLOCK, log_totals.shape[1]), 1)
    for block in reversed(range(count // BLOCK)):
        rows = slice(block * BLOCK, (block + 1) * BLOCK)
        seen = slice(0, (block + 1) * BLOCK)
        logs = log_totals[rows, :]
        for group in range(groups):
            cut = slice(group * HEAD_SIZE, (group + 1) * HEAD_SIZE)
            part_q = heads_of(queries, group, rows, per_group)
            part_d = heads_of(d_attn, group, rows, per_group)
            log_sum = jnp.concatenate(
                [
                    jnp.sum(jnp.where(lane == group * per_group + j, logs, 0.0), 1, keepdims=True)
                    for j in range(per_group)
                ],
                0,
            )
            part_k, part_v = keys[seen, cut], values[seen, cut]
            probs_f = jnp.exp(contract(part_q, part_k, 1, 1) * factor - log_sum)
            d_probs = contract(part_d, part_v, 1, 1)
            centre = jnp.sum(probs_f * d_probs, -1, keepdims=True)
            d_scores = (probs_f * (d_probs - centre)).astype(jnp.bfloat16)
            turned = contract(d_scores, part_k, 1, 0) * factor
            for j in range(per_group):
                head = group * per_group + j
                d_queries[rows, head * HEAD_SIZE : (head + 1) * HEAD_SIZE] = turned[j * BLOCK : (j + 1) * BLOCK]
            new_k = contract(d_scores, part_q, 0, 0) * factor
            new_v = contract(probs_f.astype(jnp.bfloat16), part_d, 0, 0)
            if block == count // BLOCK - 1:
                d_keys[seen, cut] = new_k
                d_values[seen, cut] = new_v
            else:
                d_keys[seen, cut] += new_k
                d_values[seen, cut] += new_v
    key_width = keys.shape[1]
    d_pre[:, :width] = rotate(d_queries[...], cosine[...], sine[...], -1).astype(jnp.bfloat16)
    d_pre[:, width : width + key_width] = rotate(d_keys[...], cosine[...], sine[...], -1).astype(jnp.bfloat16)
    d_pre[:, width + key_width :] = d_values[...].astype(jnp.bfloat16)


def attention_back(dh_own, dh_near, dh_far, d_router, probs, resid, norm_ffn, cotangent, w_router, w_out, h_two, attn,
                   queries, keys, values, log_totals, cosine, sine):
    count, width = resid.shape
    key_width = keys.shape[1]
    wide_router = jnp.pad(w_router, ((0, 0), (0, LANES - w_router.shape[1])))
    shape = jax.ShapeDtypeStruct
    return pl.pallas_call(
        attention_back_kernel,
        out_shape=[
            shape((count, width), jnp.float32),
            shape((count, width + 2 * key_width), jnp.bfloat16),
            shape((width, width + 2 * LANES), jnp.bfloat16),
        ],
        scratch_shapes=[
            pltpu.VMEM((count, width), jnp.bfloat16),
            pltpu.VMEM((count, width), jnp.bfloat16),
            pltpu.VMEM((count, width), jnp.float32),
            pltpu.VMEM((count, key_width), jnp.float32),
            pltpu.VMEM((count, key_width), jnp.float32),
        ],
        compiler_params=pltpu.CompilerParams(vmem_limit_bytes=VMEM_BYTES),
        cost_estimate=pl.CostEstimate(
            flops=10 * count * width * width, bytes_accessed=8 * width * width, transcendentals=24 * count * count
        ),
        name="attention_back",
    )(
        dh_own, dh_near, dh_far, d_router, probs, resid, norm_ffn[None], cotangent, wide_router, w_out, h_two, attn,
        queries, keys, values, log_totals, cosine, sine,
    )


def input_kernel(d_pre, normed, tokens, norm_attn, d_resid, w_query, w_key, w_value, d_input, grads):
    width, key_width = w_query.shape[1], w_key.shape[1]
    entries = d_pre[...]
    d_normed = (
        contract(entries[:, :width], w_query[...], 1, 1)
        + contract(entries[:, width : width + key_width], w_key[...], 1, 1)
        + contract(entries[:, width + key_width :], w_value[...], 1, 1)
    )
    field = tokens[...].astype(jnp.float32)
    inverse = lax.rsqrt(jnp.mean(field * field, -1, keepdims=True) + epsilon)
    normal = field * inverse
    scaled = d_normed * norm_attn[...].astype(jnp.float32)
    d_input[...] = d_resid[...] + inverse * (scaled - normal * jnp.mean(scaled * normal, -1, keepdims=True))
    wide = entries.shape[1]
    grads[:, :wide] = contract(normed[...], entries, 0, 0).astype(jnp.bfloat16)
    grads[:, wide : wide + LANES] = as_lane(jnp.sum(d_normed * normal, 0, keepdims=True))
    grads[:, wide + LANES :] = jnp.zeros((width, LANES), jnp.bfloat16)


def input_back(d_pre, normed, tokens, norm_attn, d_resid, w_query, w_key, w_value):
    count, width = tokens.shape
    shape = jax.ShapeDtypeStruct
    return pl.pallas_call(
        input_kernel,
        out_shape=[
            shape((count, width), jnp.float32),
            shape((width, d_pre.shape[1] + 2 * LANES), jnp.bfloat16),
        ],
        compiler_params=pltpu.CompilerParams(vmem_limit_bytes=VMEM_BYTES),
        cost_estimate=pl.CostEstimate(
            flops=8 * count * width * width, bytes_accessed=12 * width * width, transcendentals=0
        ),
        name="input_back",
    )(d_pre, normed, tokens, norm_attn[None], d_resid, w_query, w_key, w_value)


SLOTS = 3


def ring_device(place, count):
    back = place // (count // 2)
    return (1 - back) * 2 * place + back * (2 * (count - 1 - place) + 1)


def ring_kernel(count, many, lag, shapes, *refs):
    dense = len(shapes) - many
    inputs, outputs, rest = refs[: 1 + dense], refs[1 + dense : 2 + 2 * dense], refs[2 + 2 * dense :]
    total = len(shapes)
    held, terms, rest = rest[:total], rest[total : 2 * total], rest[2 * total :]
    own, near, far, joined, rest = (
        rest[:dense], rest[dense : 2 * dense], rest[2 * dense : 3 * dense], rest[3 * dense : 4 * dense], rest[4 * dense :]
    )
    arrived, sent, loaded, stored, near_sent, near_arrived, own_loaded, far_sent, far_arrived, credit = rest
    sources = [inputs[0].at[k] for k in range(many)] + list(joined)
    sums = [outputs[0].at[k] for k in range(many)] + list(outputs[1:])
    here = lax.axis_index("rep")
    odd = here % 2
    rank = here // 2 + odd * (count - 1 - 2 * (here // 2))
    after = ring_device((rank + 1) % count, count)
    before = ring_device((rank + count - 1) % count, count)
    hops = 2 * (count - 1)
    holder = lax.axis_index("ep")
    core = holder + 1 - 2 * (holder % 2)
    chip = (holder + 2) % 4
    far_core = (core + 2) % 4

    barrier = pltpu.get_barrier_semaphore()
    for neighbour in (before, after):
        pl.semaphore_signal(barrier, inc=1, device_id={"rep": neighbour})
    for neighbour in (core, chip):
        pl.semaphore_signal(barrier, inc=1, device_id={"ep": neighbour})
    pl.semaphore_wait(barrier, 4)

    def columns(index, way):
        half = shapes[index][1] // 2
        return pl.ds(way * half, half)

    def send(index, way, hop):
        stream = 2 * index + way
        source = (hop + SLOTS - 1) % SLOTS
        slot = hop % SLOTS
        return pltpu.make_async_remote_copy(
            src_ref=held[index].at[way, source],
            dst_ref=held[index].at[way, slot],
            send_sem=sent.at[stream, slot],
            recv_sem=arrived.at[stream, slot],
            device_id={"rep": before if way else after},
        )

    def load(index, way, hop):
        step = hop + 2
        chunk = (rank + step) % count if way else (rank + 2 * count - step) % count
        return pltpu.make_async_copy(
            sources[index].at[chunk, :, columns(index, way)],
            terms[index].at[way, hop % 2],
            loaded.at[2 * index + way, hop % 2],
        )

    def first(index, way):
        chunk = (rank + 1) % count if way else (rank + count - 1) % count
        return pltpu.make_async_copy(
            sources[index].at[chunk, :, columns(index, way)],
            held[index].at[way, SLOTS - 1],
            stored.at[2 * index + way, SLOTS - 1],
        )

    def store(index, way, hop):
        step = hop - (count - 2)
        chunk = (rank + step) % count if way else (rank + count - step) % count
        return pltpu.make_async_copy(
            held[index].at[way, hop % SLOTS],
            sums[index].at[chunk, :, columns(index, way)],
            stored.at[2 * index + way, hop % SLOTS],
        )

    def release(index, way):
        pl.semaphore_signal(
            credit.at[2 * index + way], inc=1, device_id={"rep": after if way else before}
        )

    def begin(streams):
        for index, way in streams:
            first(index, way).start()
        for index, way in streams:
            load(index, way, 0).start()
            load(index, way, 1).start()
        for index, way in streams:
            first(index, way).wait()
            send(index, way, 0).start()

    def take(index, way, hop):
        send(index, way, hop).wait_recv()
        send(index, way, hop).wait_send()

    def pass_on(index, way, hop):
        @pl.when(hop + 1 >= 2)
        def _():
            pl.semaphore_wait(credit.at[2 * index + way], 1)

        send(index, way, hop + 1).start()

    def add_step(streams, hop):
        for index, way in streams:
            take(index, way, hop)

            @pl.when(hop <= hops - 3)
            def _():
                release(index, way)

            load(index, way, hop).wait()
            slot = hop % SLOTS
            held[index][way, slot] = (
                held[index][way, slot].astype(jnp.float32)
                + terms[index][way, hop % 2].astype(jnp.float32)
            ).astype(jnp.bfloat16)
            pass_on(index, way, hop)

            @pl.when(hop + 2 <= count - 2)
            def _():
                load(index, way, hop + 2).start()

            @pl.when(hop == count - 2)
            def _():
                store(index, way, hop).start()

    def hand_step(streams, hop):
        for index, way in streams:
            take(index, way, hop)
            store(index, way, hop - 1).wait()

            @pl.when(hop <= hops - 3)
            def _():
                release(index, way)

            @pl.when(hop + 1 < hops)
            def _():
                pass_on(index, way, hop)

            store(index, way, hop).start()

    def block(k, index):
        rows = own[k].shape[1]
        return inputs[1 + k].at[pl.ds(pl.multiple_of(index * rows, 8), rows), :]

    def to_core(k, part):
        return pltpu.make_async_remote_copy(
            src_ref=block(k, far_core if part else core),
            dst_ref=near[k].at[part],
            send_sem=near_sent.at[k, part],
            recv_sem=near_arrived.at[k, part],
            device_id={"ep": core},
        )

    def own_block(k, part):
        return pltpu.make_async_copy(
            block(k, chip if part else holder), own[k].at[part], own_loaded.at[k, part]
        )

    def to_chip(k):
        return pltpu.make_async_remote_copy(
            src_ref=own[k].at[1],
            dst_ref=far[k],
            send_sem=far_sent.at[k],
            recv_sem=far_arrived.at[k],
            device_id={"ep": chip},
        )

    pieces = 8

    def send_far():
        for k in range(dense):
            to_core(k, 1).wait_recv()
            own_block(k, 1).wait()
            rows = own[k].shape[1] // pieces
            for j in range(pieces):
                cut = slice(j * rows, (j + 1) * rows)
                own[k][1, cut] = (
                    own[k][1, cut].astype(jnp.float32) + near[k][1, cut].astype(jnp.float32)
                ).astype(jnp.bfloat16)
            to_chip(k).start()

    def join():
        for k in range(dense):
            to_core(k, 0).wait_recv()
            own_block(k, 0).wait()
            to_chip(k).wait_recv()
            to_chip(k).wait_send()
            for part in (0, 1):
                to_core(k, part).wait_send()
            rows = joined[k].shape[1]
            for j in range(count):
                if j * rows < own[k].shape[1]:
                    cut = slice(j * rows, (j + 1) * rows)
                    joined[k][j] = (
                        own[k][0, cut].astype(jnp.float32)
                        + near[k][0, cut].astype(jnp.float32)
                        + far[k][cut].astype(jnp.float32)
                    ).astype(jnp.bfloat16)
                else:
                    joined[k][j] = jnp.zeros(joined[k].shape[1:], jnp.bfloat16)

    early_streams = [(index, way) for index in range(many) for way in (0, 1)]
    late_streams = [(index, way) for index in range(many, total) for way in (0, 1)]
    for k in range(dense):
        for part in (1, 0):
            to_core(k, part).start()
            own_block(k, part).start()
    begin(early_streams)
    ends = sorted({0, 1, lag, count - 1, hops, lag + count - 1, lag + hops})
    for low, high in zip(ends[:-1], ends[1:]):
        if low == 1:
            send_far()
        if low == lag:
            join()
            begin(late_streams)

        def ticks(tick, carry, low=low):
            for streams, start in ((early_streams, 0), (late_streams, lag)):
                if start <= low < start + count - 1:
                    add_step(streams, tick - start)
                elif start + count - 1 <= low < start + hops:
                    hand_step(streams, tick - start)
            return carry

        lax.fori_loop(low, high, ticks, 0)
    for index, way in early_streams + late_streams:
        store(index, way, hops - 1).wait()


def ring_sum(late, partials):
    many, count = late.shape[:2]
    quarters = [(partial.shape[0] // 4, partial.shape[1]) for partial in partials]
    cuts = [(-(-rows // (8 * count)) * 8, columns) for rows, columns in quarters]
    shapes = [late.shape[2:]] * many + cuts
    total, dense = len(shapes), len(partials)
    halves = [(rows, columns // 2) for rows, columns in shapes]
    size = late.size + sum(partial.size for partial in partials)
    dma = pltpu.SemaphoreType.DMA
    return pl.pallas_call(
        functools.partial(ring_kernel, count, many, 5, shapes),
        out_shape=[jax.ShapeDtypeStruct(late.shape, late.dtype)]
        + [jax.ShapeDtypeStruct((count,) + cut, late.dtype) for cut in cuts],
        in_specs=[pl.BlockSpec(memory_space=pl.ANY)] * (1 + dense),
        out_specs=[pl.BlockSpec(memory_space=pl.ANY)] * (1 + dense),
        scratch_shapes=[pltpu.VMEM((2, SLOTS) + half, jnp.bfloat16) for half in halves]
        + [pltpu.VMEM((2, 2) + half, jnp.bfloat16) for half in halves]
        + [pltpu.VMEM((2,) + quarter, jnp.bfloat16) for quarter in quarters]
        + [pltpu.VMEM((2,) + quarter, jnp.bfloat16) for quarter in quarters]
        + [pltpu.VMEM(quarter, jnp.bfloat16) for quarter in quarters]
        + [pltpu.VMEM((count,) + cut, jnp.bfloat16) for cut in cuts]
        + [
            dma((2 * total, SLOTS)),
            dma((2 * total, SLOTS)),
            dma((2 * total, 2)),
            dma((2 * total, SLOTS)),
            dma((dense, 2)),
            dma((dense, 2)),
            dma((dense, 2)),
            dma((dense,)),
            dma((dense,)),
            pltpu.SemaphoreType.REGULAR((2 * total,)),
        ],
        compiler_params=pltpu.CompilerParams(
            collective_id=0, has_side_effects=True, vmem_limit_bytes=VMEM_BYTES
        ),
        cost_estimate=pl.CostEstimate(flops=2 * size, bytes_accessed=8 * size, transcendentals=0),
        name="ring_sum",
    )(late, *partials)


def finish_kernel(firsts, *refs):
    units, (gate, up, down) = refs[:-3], refs[-3:]
    for index, unit in enumerate(units):
        e = pl.program_id(0)

        @pl.when((e >= firsts[index]) & (e < firsts[index + 1]))
        def _():
            rows = unit.shape[2] // 3
            for k in range(unit.shape[1]):
                gate[0, k * rows : (k + 1) * rows] = unit[0, k, :rows].astype(jnp.float32)
                up[0, k * rows : (k + 1) * rows] = unit[0, k, rows : 2 * rows].astype(jnp.float32)
            turned = jnp.concatenate([unit[0, k, 2 * rows :] for k in range(unit.shape[1])], 0)
            down[0] = turned.astype(jnp.float32).T


def finish(units, width):
    count, rows3, columns = units[0].shape[1:]
    rows = rows3 // 3
    pair = count // 4
    firsts = [0]
    for unit in units:
        firsts.append(firsts[-1] + unit.shape[0])
    experts = firsts[-1]

    def place(index):
        first, end = firsts[index], firsts[index + 1]

        def chunk(e, c):
            inside = jnp.clip(e, first, end - 1)
            return (inside - first, jnp.where(e < first, 0, jnp.where(e >= end, 3, c)), 0, 0)

        return chunk

    return pl.pallas_call(
        functools.partial(finish_kernel, firsts),
        grid=(experts, 4),
        in_specs=[pl.BlockSpec((1, pair, rows3, columns), place(index)) for index in range(len(units))],
        out_specs=[
            pl.BlockSpec((1, pair * rows, columns), lambda e, c: (e, c, 0)),
            pl.BlockSpec((1, pair * rows, columns), lambda e, c: (e, c, 0)),
            pl.BlockSpec((1, columns, pair * rows), lambda e, c: (e, 0, c)),
        ],
        out_shape=[
            jax.ShapeDtypeStruct((experts, width, columns), jnp.float32),
            jax.ShapeDtypeStruct((experts, width, columns), jnp.float32),
            jax.ShapeDtypeStruct((experts, columns, width), jnp.float32),
        ],
        name="finish",
        compiler_params=pltpu.CompilerParams(vmem_limit_bytes=48 * 2**20),
    )(*units)


def swap_core(value):
    return lax.ppermute(value, "ep", [(0, 1), (1, 0), (2, 3), (3, 2)])


def swap_chip(value):
    return lax.ppermute(value, "ep", [(0, 2), (2, 0), (1, 3), (3, 1)])


def add_bf(a, b):
    return (a.astype(jnp.float32) + b.astype(jnp.float32)).astype(jnp.bfloat16)


def per_device(
    tokens,
    norm_attn,
    w_query,
    key_projection,
    value_projection,
    w_out,
    norm_ffn,
    w_router,
    w_gate,
    w_up,
    w_down,
    routes,
    cotangent,
):
    token_count, width = tokens.shape
    experts_all = w_router.shape[1]
    holder = lax.axis_index("ep")
    held = w_gate.shape[0]
    replicas = lax.axis_size("rep")
    cot_near = (cotangent, swap_core(cotangent))
    cot_far = swap_chip(cotangent)
    cosine, sine = rope_tables(token_count)
    normed, queries, keys, values, log_totals, attn, resid, h_two, probs, combine = attention_forward(
        tokens, norm_attn, w_query, key_projection, value_projection, cosine, sine, w_out, norm_ffn, w_router, routes
    )
    h_two, combine, cot_far = lax.optimization_barrier((h_two, combine, cot_far))
    chosen = jnp.max((routes[:, :, None] == jnp.arange(experts_all)[None, None, :]).astype(jnp.float32), 1)

    def own_columns(block):
        return lax.dynamic_slice_in_dim(block, holder * held, held, 1)

    h_near = (h_two, swap_core(h_two))
    gates_near = (own_columns(combine), own_columns(swap_core(combine)))
    h_far, gates_far = swap_chip(h_two), swap_chip(combine)
    near = expert_pass(h_near, cot_near, gates_near, w_gate, w_up, w_down)
    near, h_far, gates_far = lax.optimization_barrier((near, h_far, gates_far))
    h_far = (h_far, swap_core(h_far))
    cot_far = (cot_far, swap_core(cot_far))
    gates_far = (own_columns(gates_far), own_columns(swap_core(gates_far)))
    far = expert_pass(h_far, cot_far, gates_far, w_gate, w_up, w_down)
    ghs, dgs, dus = zip(near[:3], far[:3])
    hs, cots = h_near + h_far, cot_near + cot_far

    def widen(block):
        return lax.dynamic_update_slice_in_dim(
            jnp.zeros((block.shape[0], experts_all), jnp.float32), block, holder * held, 1
        )

    router_near = widen(near[3]) + swap_core(widen(near[4]))
    d_router = chosen * (router_near + swap_chip(widen(far[3]) + swap_core(widen(far[4]))))
    dh_far, other = sum_over_experts([dgs[1], dus[1]], [w_gate, w_up], 1)
    dh_far = swap_chip(add_bf(dh_far, swap_core(other)))
    dh_own, other = sum_over_experts([dgs[0], dus[0]], [w_gate, w_up], 1)
    dh_near = swap_core(other)
    ghs, dh_own = lax.optimization_barrier((ghs, dh_own))
    early = weight_grads(replicas, 0, EARLY, hs, cots, ghs, dgs, dus)
    y_far, other = sum_over_experts([ghs[1]], [w_down], 0)
    y_far = swap_chip(add_bf(y_far, swap_core(other)))
    early, y_far_started, dh_far = lax.optimization_barrier((early, other, dh_far))
    early = [lax.psum_scatter(early[e], "rep", scatter_dimension=0, tiled=True) for e in range(EARLY)]
    d_resid, d_pre, grad_out = attention_back(
        dh_own, dh_near, dh_far, d_router, probs, resid, norm_ffn, cotangent, w_router, w_out, h_two, attn,
        queries, keys, values, log_totals, cosine, sine,
    )
    d_input, grad_qkv = input_back(
        d_pre, normed, tokens, norm_attn, d_resid, w_query, key_projection, value_projection
    )
    ghs, grad_qkv = lax.optimization_barrier((ghs, grad_qkv))
    late = weight_grads(replicas, EARLY, held - EARLY, hs, cots, ghs, dgs, dus)
    y_own, other = sum_over_experts([ghs[0]], [w_down], 0)
    mixed = (
        resid
        + y_own.astype(jnp.float32)
        + swap_core(other).astype(jnp.float32)
        + y_far.astype(jnp.float32)
    ).astype(jnp.bfloat16)
    early, late, mixed = lax.optimization_barrier((early, late, mixed))
    early = jnp.stack([lax.all_gather(part, "rep", axis=0, tiled=True) for part in early])
    late, sum_o, sum_qkv = ring_sum(late, [grad_out, grad_qkv])
    key_width = key_projection.shape[1]
    sum_o, sum_qkv = (
        total.reshape(-1, total.shape[2])[: width // 4].astype(jnp.float32) for total in (sum_o, sum_qkv)
    )
    sum_o, sum_r, sum_nf = (
        sum_o[:, :width], sum_o[:, width : width + experts_all], sum_o[:, width + LANES]
    )
    sum_q, sum_k, sum_v, sum_na = jnp.split(
        sum_qkv[:, : width + 2 * key_width + 1], [width, width + key_width, width + 2 * key_width], 1
    )
    sum_na = sum_na[:, 0]
    full_gate, full_up, full_down = finish([early, late], width)
    return (
        mixed,
        d_input,
        sum_na,
        sum_q,
        sum_k,
        sum_v,
        sum_o,
        sum_nf,
        sum_r,
        full_gate,
        full_up,
        full_down,
    )


def solution(mesh):
    placed = (
        P(("rep", "ep"), None),
        P(),
        P(),
        P(),
        P(),
        P(),
        P(),
        P(),
        P("ep", None, None),
        P("ep", None, None),
        P("ep", None, None),
        P(("rep", "ep"), None),
        P(("rep", "ep"), None),
    )
    return jax.shard_map(
        per_device,
        mesh=mesh,
        in_specs=placed,
        out_specs=(
            P(("rep", "ep"), None),
            P(("rep", "ep"), None),
            P("ep"),
            P("ep", None),
            P("ep", None),
            P("ep", None),
            P("ep", None),
            P("ep"),
            P("ep", None),
            P("ep", None, None),
            P("ep", None, None),
            P("ep", None, None),
        ),
        check_vma=False,
    )
```

```python
import functools
import math

import jax
import jax.numpy as jnp
from jax import lax
from jax.experimental import pallas as pl
from jax.experimental.pallas import tpu as pltpu
from jax.sharding import PartitionSpec as P

QUERY_HEADS = 24
KEY_VALUE_HEADS = 8
HEAD_SIZE = 64
TOPK = 8
SEQUENCE_TOKENS = 512
BLOCK = 256
EARLY = 1


epsilon = 1e-06
masked_value = -1e30


def rope_tables(token_count):
    half = HEAD_SIZE // 2
    places = (jnp.arange(token_count) % SEQUENCE_TOKENS).astype(jnp.float32)
    rates = jnp.exp(jnp.arange(half, dtype=jnp.float32) * (-2.0 * math.log(10000.0) / HEAD_SIZE))
    angles = places[:, None] * rates[None, :]
    cosine, sine = jnp.cos(angles), jnp.sin(angles)
    return (
        jnp.concatenate([cosine] * 4, 1),
        jnp.concatenate([-sine, sine] * 2, 1),
    )


def contract(left, right, left_dim, right_dim):
    return lax.dot_general(
        left, right, (((left_dim,), (right_dim,)), ((), ())), preferred_element_type=jnp.float32
    )


def whole(array):
    return pl.BlockSpec(
        array.shape, lambda *_: (0,) * array.ndim, pipeline_mode=pl.Buffered(1)
    )


def each(array):
    return pl.BlockSpec((1,) + array.shape[1:], lambda e, *_: (e,) + (0,) * (array.ndim - 1))


VMEM_BYTES = 56 * 2**20


def expert_kernel(tile, h0, h1, c0, c1, gates0, gates1, w_gate, w_up, w_down, gh, dg, du, d_router0, d_router1):
    e = pl.program_id(0)
    tokens, lanes = gates0.shape
    expert = lax.axis_index("ep") * pl.num_programs(0) + e
    lane = lax.broadcasted_iota(jnp.int32, (tile, lanes), 1)

    @pl.when(e == 0)
    def _():
        d_router0[...] = jnp.zeros_like(d_router0)
        d_router1[...] = jnp.zeros_like(d_router1)

    for base, rows_h, rows_c, gates, d_router in (
        (0, h0, c0, gates0, d_router0),
        (tokens, h1, c1, gates1, d_router1),
    ):
        for start in range(0, tokens, tile):
            rows = slice(start, start + tile)
            out = slice(base + start, base + start + tile)
            entries = rows_h[rows, :]
            gate_pre = contract(entries, w_gate[0], 1, 0)
            up_pre = contract(entries, w_up[0], 1, 0)
            back = contract(rows_c[rows, :], w_down[0], 1, 1)
            column = jnp.sum(jnp.where(lane == expert, gates[rows, :], 0.0), 1, keepdims=True)
            sigma = jax.nn.sigmoid(gate_pre)
            swish = gate_pre * sigma
            hidden = (swish * up_pre).astype(jnp.bfloat16).astype(jnp.float32)
            d_router[rows, :] = jnp.where(
                lane == expert, jnp.sum(hidden * back, 1, keepdims=True), d_router[rows, :]
            )
            d_hidden = column * back
            dg[0, out, :] = (
                d_hidden * up_pre * (sigma * (1.0 + gate_pre * (1.0 - sigma)))
            ).astype(jnp.bfloat16)
            du[0, out, :] = (d_hidden * swish).astype(jnp.bfloat16)
            gh[0, out, :] = (column * hidden).astype(jnp.bfloat16)


def expert_pass(hs, cots, gates, w_gate, w_up, w_down):
    count, width = hs[0].shape
    tokens = 2 * count
    held, _, hidden_units = w_gate.shape
    part = jax.ShapeDtypeStruct((held, tokens, hidden_units), jnp.bfloat16)
    gate_shape = gates[0].shape
    return pl.pallas_call(
        functools.partial(expert_kernel, 256),
        grid=(held,),
        in_specs=[whole(a) for a in (*hs, *cots, *gates)] + [each(a) for a in (w_gate, w_up, w_down)],
        out_specs=[each(part)] * 3 + [pl.BlockSpec(gate_shape, lambda e: (0, 0))] * 2,
        out_shape=[part] * 3 + [jax.ShapeDtypeStruct(gate_shape, jnp.float32)] * 2,
        compiler_params=pltpu.CompilerParams(vmem_limit_bytes=VMEM_BYTES),
        cost_estimate=pl.CostEstimate(
            flops=6 * held * tokens * width * hidden_units,
            bytes_accessed=6 * held * width * hidden_units,
            transcendentals=held * tokens * hidden_units,
        ),
        name="expert_pass",
    )(*hs, *cots, *gates, w_gate, w_up, w_down)


def weight_kernel(*refs):
    hs, cots, passes, unit = refs[:4], refs[4:8], refs[8:14], refs[14]
    kind = pl.program_id(1)

    def put(lefts, rights):
        count = lefts[0].shape[0]
        result = sum(
            contract(lefts[k][...], rights[k // 2][0, (k % 2) * count : (k % 2 + 1) * count], 0, 0)
            for k in range(4)
        ).astype(jnp.bfloat16)
        rows = unit.shape[3]
        for j in range(unit.shape[1]):
            unit[0, j, 0] = result[j * rows : (j + 1) * rows]

    pl.when(kind == 0)(lambda: put(hs, passes[2:4]))
    pl.when(kind == 1)(lambda: put(hs, passes[4:6]))
    pl.when(kind == 2)(lambda: put(cots, passes[:2]))


def weight_grads(count, first, many, hs, cots, ghs, dgs, dus):
    width = hs[0].shape[1]
    _, tokens, hidden_units = dgs[0].shape
    entry = pl.BlockSpec((1, tokens, hidden_units), lambda e, k: (e + first, 0, 0))
    unit = pl.pallas_call(
        weight_kernel,
        grid=(many, 3),
        in_specs=[whole(hs[0])] * 8 + [entry] * 6,
        out_specs=pl.BlockSpec((1, count, 1, width // count, hidden_units), lambda e, k: (e, 0, k, 0, 0)),
        out_shape=jax.ShapeDtypeStruct((many, count, 3, width // count, hidden_units), jnp.bfloat16),
        compiler_params=pltpu.CompilerParams(vmem_limit_bytes=VMEM_BYTES),
        cost_estimate=pl.CostEstimate(
            flops=12 * many * tokens * width * hidden_units,
            bytes_accessed=6 * many * (width + 2 * tokens) * hidden_units,
            transcendentals=0,
        ),
        name="weight_grads",
    )(*hs, *cots, *ghs, *dgs, *dus)
    return unit.reshape(many, count, 3 * (width // count), hidden_units)


def sum_kernel(right_dim, pairs, *refs):
    lefts, rights, outs, total = refs[:pairs], refs[pairs : 2 * pairs], refs[-3:-1], refs[-1]
    e = pl.program_id(0)
    term = sum(contract(left[0], right[0], 1, right_dim) for left, right in zip(lefts, rights))

    @pl.when(e == 0)
    def _():
        total[...] = term

    @pl.when(e > 0)
    def _():
        total[...] += term

    @pl.when(e == pl.num_programs(0) - 1)
    def _():
        for k, out in enumerate(outs):
            count = out.shape[0]
            out[...] = total[k * count : (k + 1) * count].astype(out.dtype)


def sum_over_experts(lefts, rights, right_dim):
    held, tokens, inner = lefts[0].shape
    width = rights[0].shape[2 - right_dim]
    return pl.pallas_call(
        functools.partial(sum_kernel, right_dim, len(lefts)),
        grid=(held,),
        in_specs=[each(a) for a in lefts] + [each(a) for a in rights],
        out_specs=[pl.BlockSpec((tokens // 2, width), lambda e: (0, 0))] * 2,
        out_shape=[jax.ShapeDtypeStruct((tokens // 2, width), jnp.bfloat16)] * 2,
        scratch_shapes=[pltpu.VMEM((tokens, width), jnp.float32)],
        compiler_params=pltpu.CompilerParams(vmem_limit_bytes=VMEM_BYTES),
        cost_estimate=pl.CostEstimate(
            flops=2 * len(lefts) * held * tokens * width * inner,
            bytes_accessed=2 * len(lefts) * held * (tokens + width) * inner,
            transcendentals=0,
        ),
        name="sum_over_experts",
    )(*lefts, *rights)


def rotate(values, cosine, sine, way):
    lane = lax.broadcasted_iota(jnp.int32, cosine.shape, 1)
    first = lane % HEAD_SIZE < HEAD_SIZE // 2
    lanes = cosine.shape[1]
    half = HEAD_SIZE // 2
    pieces = []
    for start in range(0, values.shape[1], lanes):
        piece = values[:, start : start + lanes]
        other = jnp.where(first, pltpu.roll(piece, lanes - half, 1), pltpu.roll(piece, half, 1))
        pieces.append(piece * cosine + way * (other * sine))
    return jnp.concatenate(pieces, 1)


def heads_of(array, group, rows, queries):
    return jnp.concatenate(
        [
            array[rows, (group * queries + j) * HEAD_SIZE : (group * queries + j + 1) * HEAD_SIZE]
            for j in range(queries)
        ],
        0,
    )


def chosen_of(routes, shape):
    expert = lax.broadcasted_iota(jnp.int32, shape, 1)
    picks = routes[...].T
    chosen = picks[:, :1] == expert
    for k in range(1, picks.shape[1]):
        chosen = chosen | (picks[:, k : k + 1] == expert)
    return chosen


def attention_kernel(
    tokens, norm_attn, w_query, w_key, w_value, cosine, sine, w_out, norm_ffn, w_router, routes,
    normed, queries, keys, values, log_totals, attn, resid, h_two, probs, combine,
):
    count, width = tokens.shape
    field = tokens[...].astype(jnp.float32)
    inverse = lax.rsqrt(jnp.mean(field * field, -1, keepdims=True) + epsilon)
    first = (field * inverse * norm_attn[...].astype(jnp.float32)).astype(jnp.bfloat16)
    normed[...] = first
    queries[...] = rotate(contract(first, w_query[...], 1, 0), cosine[...], sine[...], 1).astype(jnp.bfloat16)
    keys[...] = rotate(contract(first, w_key[...], 1, 0), cosine[...], sine[...], 1).astype(jnp.bfloat16)
    values[...] = contract(first, w_value[...], 1, 0).astype(jnp.bfloat16)
    groups = keys.shape[1] // HEAD_SIZE
    per_group = queries.shape[1] // keys.shape[1]
    lane = lax.broadcasted_iota(jnp.int32, (BLOCK, log_totals.shape[1]), 1)
    for block in range(count // BLOCK):
        rows = slice(block * BLOCK, (block + 1) * BLOCK)
        seen = slice(0, (block + 1) * BLOCK)
        logs = jnp.zeros((BLOCK, log_totals.shape[1]), jnp.float32)
        for group in range(groups):
            cut = slice(group * HEAD_SIZE, (group + 1) * HEAD_SIZE)
            scores = contract(heads_of(queries, group, rows, per_group), keys[seen, cut], 1, 1)
            scores = scores * HEAD_SIZE ** (-0.5)
            highest = jnp.max(scores, -1, keepdims=True)
            shifted = jnp.exp(scores - highest)
            sums = jnp.sum(shifted, -1, keepdims=True)
            probs_bf = (shifted * (1.0 / sums)).astype(jnp.bfloat16)
            mix = contract(probs_bf, values[seen, cut], 1, 0).astype(jnp.bfloat16)
            log_sum = highest + jnp.log(sums)
            for j in range(per_group):
                head = group * per_group + j
                part = slice(j * BLOCK, (j + 1) * BLOCK)
                attn[rows, head * HEAD_SIZE : (head + 1) * HEAD_SIZE] = mix[part]
                logs = jnp.where(lane == head, log_sum[part], logs)
        log_totals[rows, :] = logs
    total = field + contract(attn[...], w_out[...], 1, 0)
    resid[...] = total
    inverse = lax.rsqrt(jnp.mean(total * total, -1, keepdims=True) + epsilon)
    second = (total * inverse * norm_ffn[...].astype(jnp.float32)).astype(jnp.bfloat16)
    h_two[...] = second
    logits = contract(second, w_router[...], 1, 1)
    shifted = jnp.exp(logits - jnp.max(logits, -1, keepdims=True))
    soft = shifted / jnp.sum(shifted, -1, keepdims=True)
    probs[...] = soft
    combine[...] = jnp.where(chosen_of(routes, logits.shape), soft, 0.0)


LANES = 128


def attention_forward(tokens, norm_attn, w_query, w_key, w_value, cosine, sine, w_out, norm_ffn, w_router, routes):
    count, width = tokens.shape
    experts = w_router.shape[1]
    key_width = w_key.shape[1]
    shape = jax.ShapeDtypeStruct
    return pl.pallas_call(
        attention_kernel,
        out_shape=[
            shape((count, width), jnp.bfloat16),
            shape((count, width), jnp.bfloat16),
            shape((count, key_width), jnp.bfloat16),
            shape((count, key_width), jnp.bfloat16),
            shape((count, LANES), jnp.float32),
            shape((count, width), jnp.bfloat16),
            shape((count, width), jnp.float32),
            shape((count, width), jnp.bfloat16),
            shape((count, experts), jnp.float32),
            shape((count, experts), jnp.float32),
        ],
        compiler_params=pltpu.CompilerParams(vmem_limit_bytes=VMEM_BYTES),
        cost_estimate=pl.CostEstimate(
            flops=6 * count * width * width, bytes_accessed=8 * width * width, transcendentals=24 * count * count
        ),
        name="attention_forward",
    )(
        tokens, norm_attn[None], w_query, w_key, w_value, cosine, sine, w_out, norm_ffn[None], w_router.T, routes.T
    )


def as_lane(row):
    first = lax.broadcasted_iota(jnp.int32, (LANES, row.shape[1]), 0) == 0
    return jnp.where(first, row, 0.0).T.astype(jnp.bfloat16)


def attention_back_kernel(
    dh_own, dh_near, dh_far, router_own, router_near, router_far, routes, probs, resid, norm_ffn, cotangent, w_router, w_out, h_two, attn,
    queries, keys, values, log_totals, cosine, sine,
    d_resid, d_pre, grad_out, d_branch, d_attn, d_queries, d_keys, d_values,
):
    count, width = resid.shape
    experts = probs.shape[1]
    soft = probs[...]
    to_router = jnp.where(
        chosen_of(routes, soft.shape), router_own[...] + router_near[...] + router_far[...], 0.0
    )
    d_logits = (soft * (to_router - jnp.sum(soft * to_router, -1, keepdims=True))).astype(jnp.bfloat16)
    d_normed = (
        dh_own[...].astype(jnp.float32)
        + dh_near[...].astype(jnp.float32)
        + dh_far[...].astype(jnp.float32)
        + contract(d_logits, w_router[...], 1, 0)
    )
    total = resid[...]
    inverse = lax.rsqrt(jnp.mean(total * total, -1, keepdims=True) + epsilon)
    normal = total * inverse
    scaled = d_normed * norm_ffn[...].astype(jnp.float32)
    back = cotangent[...].astype(jnp.float32) + inverse * (
        scaled - normal * jnp.mean(scaled * normal, -1, keepdims=True)
    )
    d_resid[...] = back
    d_branch[...] = back.astype(jnp.bfloat16)
    grad_out[:, :width] = contract(attn[...], d_branch[...], 0, 0).astype(jnp.bfloat16)
    d_logits = jnp.concatenate([d_logits, jnp.zeros((count, LANES - experts), jnp.bfloat16)], 1)
    grad_out[:, width : width + LANES] = contract(h_two[...], d_logits, 0, 0).astype(jnp.bfloat16)
    grad_out[:, width + LANES :] = as_lane(jnp.sum(d_normed * normal, 0, keepdims=True))
    d_attn[...] = contract(d_branch[...], w_out[...], 1, 1).astype(jnp.bfloat16)
    groups = keys.shape[1] // HEAD_SIZE
    per_group = queries.shape[1] // keys.shape[1]
    factor = HEAD_SIZE ** (-0.5)
    lane = lax.broadcasted_iota(jnp.int32, (BLOCK, log_totals.shape[1]), 1)
    for block in reversed(range(count // BLOCK)):
        rows = slice(block * BLOCK, (block + 1) * BLOCK)
        seen = slice(0, (block + 1) * BLOCK)
        logs = log_totals[rows, :]
        for group in range(groups):
            cut = slice(group * HEAD_SIZE, (group + 1) * HEAD_SIZE)
            part_q = heads_of(queries, group, rows, per_group)
            part_d = heads_of(d_attn, group, rows, per_group)
            log_sum = jnp.concatenate(
                [
                    jnp.sum(jnp.where(lane == group * per_group + j, logs, 0.0), 1, keepdims=True)
                    for j in range(per_group)
                ],
                0,
            )
            part_k, part_v = keys[seen, cut], values[seen, cut]
            probs_f = jnp.exp(contract(part_q, part_k, 1, 1) * factor - log_sum)
            d_probs = contract(part_d, part_v, 1, 1)
            centre = jnp.sum(probs_f * d_probs, -1, keepdims=True)
            d_scores = (probs_f * (d_probs - centre)).astype(jnp.bfloat16)
            turned = contract(d_scores, part_k, 1, 0) * factor
            for j in range(per_group):
                head = group * per_group + j
                d_queries[rows, head * HEAD_SIZE : (head + 1) * HEAD_SIZE] = turned[j * BLOCK : (j + 1) * BLOCK]
            new_k = contract(d_scores, part_q, 0, 0) * factor
            new_v = contract(probs_f.astype(jnp.bfloat16), part_d, 0, 0)
            if block == count // BLOCK - 1:
                d_keys[seen, cut] = new_k
                d_values[seen, cut] = new_v
            else:
                d_keys[seen, cut] += new_k
                d_values[seen, cut] += new_v
    key_width = keys.shape[1]
    d_pre[:, :width] = rotate(d_queries[...], cosine[...], sine[...], -1).astype(jnp.bfloat16)
    d_pre[:, width : width + key_width] = rotate(d_keys[...], cosine[...], sine[...], -1).astype(jnp.bfloat16)
    d_pre[:, width + key_width :] = d_values[...].astype(jnp.bfloat16)


def attention_back(dh_own, dh_near, dh_far, router_own, router_near, router_far, routes, probs, resid, norm_ffn, cotangent, w_router, w_out, h_two, attn,
                   queries, keys, values, log_totals, cosine, sine):
    count, width = resid.shape
    key_width = keys.shape[1]
    shape = jax.ShapeDtypeStruct
    return pl.pallas_call(
        attention_back_kernel,
        out_shape=[
            shape((count, width), jnp.float32),
            shape((count, width + 2 * key_width), jnp.bfloat16),
            shape((width, width + 2 * LANES), jnp.bfloat16),
        ],
        scratch_shapes=[
            pltpu.VMEM((count, width), jnp.bfloat16),
            pltpu.VMEM((count, width), jnp.bfloat16),
            pltpu.VMEM((count, width), jnp.float32),
            pltpu.VMEM((count, key_width), jnp.float32),
            pltpu.VMEM((count, key_width), jnp.float32),
        ],
        compiler_params=pltpu.CompilerParams(vmem_limit_bytes=VMEM_BYTES),
        cost_estimate=pl.CostEstimate(
            flops=10 * count * width * width, bytes_accessed=8 * width * width, transcendentals=24 * count * count
        ),
        name="attention_back",
    )(
        dh_own, dh_near, dh_far, router_own, router_near, router_far, routes.T, probs, resid, norm_ffn[None], cotangent,
        w_router.T, w_out, h_two, attn, queries, keys, values, log_totals, cosine, sine,
    )


def input_kernel(d_pre, normed, tokens, norm_attn, d_resid, w_query, w_key, w_value, d_input, grads):
    width, key_width = w_query.shape[1], w_key.shape[1]
    entries = d_pre[...]
    d_normed = (
        contract(entries[:, :width], w_query[...], 1, 1)
        + contract(entries[:, width : width + key_width], w_key[...], 1, 1)
        + contract(entries[:, width + key_width :], w_value[...], 1, 1)
    )
    field = tokens[...].astype(jnp.float32)
    inverse = lax.rsqrt(jnp.mean(field * field, -1, keepdims=True) + epsilon)
    normal = field * inverse
    scaled = d_normed * norm_attn[...].astype(jnp.float32)
    d_input[...] = d_resid[...] + inverse * (scaled - normal * jnp.mean(scaled * normal, -1, keepdims=True))
    wide = entries.shape[1]
    grads[:, :wide] = contract(normed[...], entries, 0, 0).astype(jnp.bfloat16)
    grads[:, wide : wide + LANES] = as_lane(jnp.sum(d_normed * normal, 0, keepdims=True))
    grads[:, wide + LANES :] = jnp.zeros((width, LANES), jnp.bfloat16)


def input_back(d_pre, normed, tokens, norm_attn, d_resid, w_query, w_key, w_value):
    count, width = tokens.shape
    shape = jax.ShapeDtypeStruct
    return pl.pallas_call(
        input_kernel,
        out_shape=[
            shape((count, width), jnp.float32),
            shape((width, d_pre.shape[1] + 2 * LANES), jnp.bfloat16),
        ],
        compiler_params=pltpu.CompilerParams(vmem_limit_bytes=VMEM_BYTES),
        cost_estimate=pl.CostEstimate(
            flops=8 * count * width * width, bytes_accessed=12 * width * width, transcendentals=0
        ),
        name="input_back",
    )(d_pre, normed, tokens, norm_attn[None], d_resid, w_query, w_key, w_value)


SLOTS = 3


def ring_device(place, count):
    back = place // (count // 2)
    return (1 - back) * 2 * place + back * (2 * (count - 1 - place) + 1)


def ring_kernel(count, many, lag, shapes, *refs):
    dense = len(shapes) - many
    inputs, outputs, rest = refs[: 1 + dense], refs[1 + dense : 2 + 2 * dense], refs[2 + 2 * dense :]
    total = len(shapes)
    held, terms, rest = rest[:total], rest[total : 2 * total], rest[2 * total :]
    own, near, far, joined, rest = (
        rest[:dense], rest[dense : 2 * dense], rest[2 * dense : 3 * dense], rest[3 * dense : 4 * dense], rest[4 * dense :]
    )
    arrived, sent, loaded, stored, near_sent, near_arrived, own_loaded, far_sent, far_arrived, credit = rest
    sources = [inputs[0].at[k] for k in range(many)] + list(joined)
    sums = [outputs[0].at[k] for k in range(many)] + list(outputs[1:])
    here = lax.axis_index("rep")
    odd = here % 2
    rank = here // 2 + odd * (count - 1 - 2 * (here // 2))
    after = ring_device((rank + 1) % count, count)
    before = ring_device((rank + count - 1) % count, count)
    hops = 2 * (count - 1)
    holder = lax.axis_index("ep")
    core = holder + 1 - 2 * (holder % 2)
    chip = (holder + 2) % 4
    far_core = (core + 2) % 4

    barrier = pltpu.get_barrier_semaphore()
    for neighbour in (before, after):
        pl.semaphore_signal(barrier, inc=1, device_id={"rep": neighbour})
    for neighbour in (core, chip):
        pl.semaphore_signal(barrier, inc=1, device_id={"ep": neighbour})
    pl.semaphore_wait(barrier, 4)

    def columns(index, way):
        half = shapes[index][1] // 2
        return pl.ds(way * half, half)

    def send(index, way, hop):
        stream = 2 * index + way
        source = (hop + SLOTS - 1) % SLOTS
        slot = hop % SLOTS
        return pltpu.make_async_remote_copy(
            src_ref=held[index].at[way, source],
            dst_ref=held[index].at[way, slot],
            send_sem=sent.at[stream, slot],
            recv_sem=arrived.at[stream, slot],
            device_id={"rep": before if way else after},
        )

    def load(index, way, hop):
        step = hop + 2
        chunk = (rank + step) % count if way else (rank + 2 * count - step) % count
        return pltpu.make_async_copy(
            sources[index].at[chunk, :, columns(index, way)],
            terms[index].at[way, hop % 2],
            loaded.at[2 * index + way, hop % 2],
        )

    def first(index, way):
        chunk = (rank + 1) % count if way else (rank + count - 1) % count
        return pltpu.make_async_copy(
            sources[index].at[chunk, :, columns(index, way)],
            held[index].at[way, SLOTS - 1],
            stored.at[2 * index + way, SLOTS - 1],
        )

    def store(index, way, hop):
        step = hop - (count - 2)
        chunk = (rank + step) % count if way else (rank + count - step) % count
        return pltpu.make_async_copy(
            held[index].at[way, hop % SLOTS],
            sums[index].at[chunk, :, columns(index, way)],
            stored.at[2 * index + way, hop % SLOTS],
        )

    def release(index, way):
        pl.semaphore_signal(
            credit.at[2 * index + way], inc=1, device_id={"rep": after if way else before}
        )

    def begin(streams):
        for index, way in streams:
            first(index, way).start()
        for index, way in streams:
            load(index, way, 0).start()
            load(index, way, 1).start()
        for index, way in streams:
            first(index, way).wait()
            send(index, way, 0).start()

    def take(index, way, hop):
        send(index, way, hop).wait_recv()
        send(index, way, hop).wait_send()

    def pass_on(index, way, hop):
        @pl.when(hop + 1 >= 2)
        def _():
            pl.semaphore_wait(credit.at[2 * index + way], 1)

        send(index, way, hop + 1).start()

    def add_step(streams, hop):
        for index, way in streams:
            take(index, way, hop)

            @pl.when(hop <= hops - 3)
            def _():
                release(index, way)

            load(index, way, hop).wait()
            slot = hop % SLOTS
            held[index][way, slot] = (
                held[index][way, slot].astype(jnp.float32)
                + terms[index][way, hop % 2].astype(jnp.float32)
            ).astype(jnp.bfloat16)
            pass_on(index, way, hop)

            @pl.when(hop + 2 <= count - 2)
            def _():
                load(index, way, hop + 2).start()

            @pl.when(hop == count - 2)
            def _():
                store(index, way, hop).start()

    def hand_step(streams, hop):
        for index, way in streams:
            take(index, way, hop)
            store(index, way, hop - 1).wait()

            @pl.when(hop <= hops - 3)
            def _():
                release(index, way)

            @pl.when(hop + 1 < hops)
            def _():
                pass_on(index, way, hop)

            store(index, way, hop).start()

    def block(k, index):
        rows = own[k].shape[1]
        return inputs[1 + k].at[pl.ds(pl.multiple_of(index * rows, 8), rows), :]

    def to_core(k, part):
        return pltpu.make_async_remote_copy(
            src_ref=block(k, far_core if part else core),
            dst_ref=near[k].at[part],
            send_sem=near_sent.at[k, part],
            recv_sem=near_arrived.at[k, part],
            device_id={"ep": core},
        )

    def own_block(k, part):
        return pltpu.make_async_copy(
            block(k, chip if part else holder), own[k].at[part], own_loaded.at[k, part]
        )

    def to_chip(k):
        return pltpu.make_async_remote_copy(
            src_ref=own[k].at[1],
            dst_ref=far[k],
            send_sem=far_sent.at[k],
            recv_sem=far_arrived.at[k],
            device_id={"ep": chip},
        )

    pieces = 8

    def send_far():
        for k in range(dense):
            to_core(k, 1).wait_recv()
            own_block(k, 1).wait()
            rows = own[k].shape[1] // pieces
            for j in range(pieces):
                cut = slice(j * rows, (j + 1) * rows)
                own[k][1, cut] = (
                    own[k][1, cut].astype(jnp.float32) + near[k][1, cut].astype(jnp.float32)
                ).astype(jnp.bfloat16)
            to_chip(k).start()

    def join():
        for k in range(dense):
            to_core(k, 0).wait_recv()
            own_block(k, 0).wait()
            to_chip(k).wait_recv()
            to_chip(k).wait_send()
            for part in (0, 1):
                to_core(k, part).wait_send()
            rows = joined[k].shape[1]
            for j in range(count):
                if j * rows < own[k].shape[1]:
                    cut = slice(j * rows, (j + 1) * rows)
                    joined[k][j] = (
                        own[k][0, cut].astype(jnp.float32)
                        + near[k][0, cut].astype(jnp.float32)
                        + far[k][cut].astype(jnp.float32)
                    ).astype(jnp.bfloat16)
                else:
                    joined[k][j] = jnp.zeros(joined[k].shape[1:], jnp.bfloat16)

    early_streams = [(index, way) for index in range(many) for way in (0, 1)]
    late_streams = [(index, way) for index in range(many, total) for way in (0, 1)]
    for k in range(dense):
        for part in (1, 0):
            to_core(k, part).start()
            own_block(k, part).start()
    begin(early_streams)
    ends = sorted({0, 1, lag, count - 1, hops, lag + count - 1, lag + hops})
    for low, high in zip(ends[:-1], ends[1:]):
        if low == 1:
            send_far()
        if low == lag:
            join()
            begin(late_streams)

        def ticks(tick, carry, low=low):
            for streams, start in ((early_streams, 0), (late_streams, lag)):
                if start <= low < start + count - 1:
                    add_step(streams, tick - start)
                elif start + count - 1 <= low < start + hops:
                    hand_step(streams, tick - start)
            return carry

        lax.fori_loop(low, high, ticks, 0)
    for index, way in early_streams + late_streams:
        store(index, way, hops - 1).wait()


def ring_sum(late, partials):
    many, count = late.shape[:2]
    quarters = [(partial.shape[0] // 4, partial.shape[1]) for partial in partials]
    cuts = [(-(-rows // (8 * count)) * 8, columns) for rows, columns in quarters]
    shapes = [late.shape[2:]] * many + cuts
    total, dense = len(shapes), len(partials)
    halves = [(rows, columns // 2) for rows, columns in shapes]
    size = late.size + sum(partial.size for partial in partials)
    dma = pltpu.SemaphoreType.DMA
    return pl.pallas_call(
        functools.partial(ring_kernel, count, many, 5, shapes),
        out_shape=[jax.ShapeDtypeStruct(late.shape, late.dtype)]
        + [jax.ShapeDtypeStruct((count,) + cut, late.dtype) for cut in cuts],
        in_specs=[pl.BlockSpec(memory_space=pl.ANY)] * (1 + dense),
        out_specs=[pl.BlockSpec(memory_space=pl.ANY)] * (1 + dense),
        scratch_shapes=[pltpu.VMEM((2, SLOTS) + half, jnp.bfloat16) for half in halves]
        + [pltpu.VMEM((2, 2) + half, jnp.bfloat16) for half in halves]
        + [pltpu.VMEM((2,) + quarter, jnp.bfloat16) for quarter in quarters]
        + [pltpu.VMEM((2,) + quarter, jnp.bfloat16) for quarter in quarters]
        + [pltpu.VMEM(quarter, jnp.bfloat16) for quarter in quarters]
        + [pltpu.VMEM((count,) + cut, jnp.bfloat16) for cut in cuts]
        + [
            dma((2 * total, SLOTS)),
            dma((2 * total, SLOTS)),
            dma((2 * total, 2)),
            dma((2 * total, SLOTS)),
            dma((dense, 2)),
            dma((dense, 2)),
            dma((dense, 2)),
            dma((dense,)),
            dma((dense,)),
            pltpu.SemaphoreType.REGULAR((2 * total,)),
        ],
        compiler_params=pltpu.CompilerParams(
            collective_id=0, has_side_effects=True, vmem_limit_bytes=VMEM_BYTES
        ),
        cost_estimate=pl.CostEstimate(flops=2 * size, bytes_accessed=8 * size, transcendentals=0),
        name="ring_sum",
    )(late, *partials)


def finish_kernel(firsts, *refs):
    units, (dense_o, dense_qkv) = refs[: len(firsts) - 1], refs[len(firsts) - 1 : len(firsts) + 1]
    gate, up, down, out, query, key, value, extra_o, extra_qkv = refs[len(firsts) + 1 :]

    @pl.when((pl.program_id(0) == 0) & (pl.program_id(1) == 0))
    def _():
        for dense, parts in ((dense_o, (out, extra_o)), (dense_qkv, (query, key, value, extra_qkv))):
            start = 0
            for part in parts:
                columns = part.shape[1]
                rows = dense.shape[1]
                for j in range(part.shape[0] // rows):
                    part[j * rows : (j + 1) * rows] = dense[j, :, start : start + columns].astype(jnp.float32)
                start += columns

    for index, unit in enumerate(units):
        e = pl.program_id(0)

        @pl.when((e >= firsts[index]) & (e < firsts[index + 1]))
        def _():
            rows = unit.shape[2] // 3
            for k in range(unit.shape[1]):
                gate[0, k * rows : (k + 1) * rows] = unit[0, k, :rows].astype(jnp.float32)
                up[0, k * rows : (k + 1) * rows] = unit[0, k, rows : 2 * rows].astype(jnp.float32)
            turned = jnp.concatenate([unit[0, k, 2 * rows :] for k in range(unit.shape[1])], 0)
            down[0] = turned.astype(jnp.float32).T


def finish(units, dense, width, key_width):
    count, rows3, columns = units[0].shape[1:]
    rows = rows3 // 3
    pair = count // 4
    small = [
        jax.ShapeDtypeStruct((width // 4, part), jnp.float32)
        for part in (width, width, key_width, key_width, 2 * LANES, 2 * LANES)
    ]
    firsts = [0]
    for unit in units:
        firsts.append(firsts[-1] + unit.shape[0])
    experts = firsts[-1]

    def place(index):
        first, end = firsts[index], firsts[index + 1]

        def chunk(e, c):
            inside = jnp.clip(e, first, end - 1)
            return (inside - first, jnp.where(e < first, 0, jnp.where(e >= end, 3, c)), 0, 0)

        return chunk

    return pl.pallas_call(
        functools.partial(finish_kernel, firsts),
        grid=(experts, 4),
        in_specs=[pl.BlockSpec((1, pair, rows3, columns), place(index)) for index in range(len(units))]
        + [whole(part) for part in dense],
        out_specs=[
            pl.BlockSpec((1, pair * rows, columns), lambda e, c: (e, c, 0)),
            pl.BlockSpec((1, pair * rows, columns), lambda e, c: (e, c, 0)),
            pl.BlockSpec((1, columns, pair * rows), lambda e, c: (e, 0, c)),
        ]
        + [whole(part) for part in small],
        out_shape=[
            jax.ShapeDtypeStruct((experts, width, columns), jnp.float32),
            jax.ShapeDtypeStruct((experts, width, columns), jnp.float32),
            jax.ShapeDtypeStruct((experts, columns, width), jnp.float32),
        ]
        + small,
        name="finish",
        compiler_params=pltpu.CompilerParams(vmem_limit_bytes=VMEM_BYTES),
    )(*units, *dense)


def swap_core(value):
    return lax.ppermute(value, "ep", [(0, 1), (1, 0), (2, 3), (3, 2)])


def swap_chip(value):
    return lax.ppermute(value, "ep", [(0, 2), (2, 0), (1, 3), (3, 1)])


def add_bf(a, b):
    return (a.astype(jnp.float32) + b.astype(jnp.float32)).astype(jnp.bfloat16)


def per_device(
    tokens,
    norm_attn,
    w_query,
    key_projection,
    value_projection,
    w_out,
    norm_ffn,
    w_router,
    w_gate,
    w_up,
    w_down,
    routes,
    cotangent,
):
    token_count, width = tokens.shape
    experts_all = w_router.shape[1]
    held = w_gate.shape[0]
    replicas = lax.axis_size("rep")
    cot_near = (cotangent, swap_core(cotangent))
    cot_far = swap_chip(cotangent)
    cosine, sine = rope_tables(token_count)
    normed, queries, keys, values, log_totals, attn, resid, h_two, probs, combine = attention_forward(
        tokens, norm_attn, w_query, key_projection, value_projection, cosine, sine, w_out, norm_ffn, w_router, routes
    )
    h_two, combine, cot_far = lax.optimization_barrier((h_two, combine, cot_far))
    h_near = (h_two, swap_core(h_two))
    gates_near = (combine, swap_core(combine))
    h_far, gates_far = swap_chip(h_two), swap_chip(combine)
    near = expert_pass(h_near, cot_near, gates_near, w_gate, w_up, w_down)
    near, h_far, gates_far = lax.optimization_barrier((near, h_far, gates_far))
    h_far = (h_far, swap_core(h_far))
    cot_far = (cot_far, swap_core(cot_far))
    gates_far = (gates_far, swap_core(gates_far))
    far = expert_pass(h_far, cot_far, gates_far, w_gate, w_up, w_down)
    ghs, dgs, dus = zip(near[:3], far[:3])
    hs, cots = h_near + h_far, cot_near + cot_far

    router_own, router_near = near[3], swap_core(near[4])
    router_far = swap_chip(far[3] + swap_core(far[4]))
    early = weight_grads(replicas, 0, EARLY, hs, cots, ghs, dgs, dus)
    dgs, early = lax.optimization_barrier((dgs, early))
    early = [lax.psum_scatter(early[e], "rep", scatter_dimension=0, tiled=True) for e in range(EARLY)]
    dh_far, other = sum_over_experts([dgs[1], dus[1]], [w_gate, w_up], 1)
    dh_far = swap_chip(add_bf(dh_far, swap_core(other)))
    dh_own, other = sum_over_experts([dgs[0], dus[0]], [w_gate, w_up], 1)
    dh_near = swap_core(other)
    ghs, dh_own = lax.optimization_barrier((ghs, dh_own))
    y_far, other = sum_over_experts([ghs[1]], [w_down], 0)
    dh_far, other = lax.optimization_barrier((dh_far, other))
    y_far = swap_chip(add_bf(y_far, swap_core(other)))
    d_resid, d_pre, grad_out = attention_back(
        dh_own, dh_near, dh_far, router_own, router_near, router_far, routes, probs, resid, norm_ffn, cotangent, w_router, w_out, h_two, attn,
        queries, keys, values, log_totals, cosine, sine,
    )
    early, d_pre = lax.optimization_barrier((early, d_pre))
    early = jnp.stack([lax.all_gather(part, "rep", axis=0, tiled=True) for part in early])
    d_input, grad_qkv = input_back(
        d_pre, normed, tokens, norm_attn, d_resid, w_query, key_projection, value_projection
    )
    ghs, grad_qkv = lax.optimization_barrier((ghs, grad_qkv))
    late = weight_grads(replicas, EARLY, held - EARLY, hs, cots, ghs, dgs, dus)
    y_own, other = sum_over_experts([ghs[0]], [w_down], 0)
    mixed = (
        resid
        + y_own.astype(jnp.float32)
        + swap_core(other).astype(jnp.float32)
        + y_far.astype(jnp.float32)
    ).astype(jnp.bfloat16)
    late, mixed = lax.optimization_barrier((late, mixed))
    late, sum_o, sum_qkv = ring_sum(late, [grad_out, grad_qkv])
    full_gate, full_up, full_down, sum_o, sum_q, sum_k, sum_v, extra_o, extra_qkv = finish(
        [early, late], [sum_o, sum_qkv], width, key_projection.shape[1]
    )
    sum_r, sum_nf, sum_na = extra_o[:, :experts_all], extra_o[:, LANES], extra_qkv[:, 0]
    return (
        mixed,
        d_input,
        sum_na,
        sum_q,
        sum_k,
        sum_v,
        sum_o,
        sum_nf,
        sum_r,
        full_gate,
        full_up,
        full_down,
    )


def solution(mesh):
    placed = (
        P(("rep", "ep"), None),
        P(),
        P(),
        P(),
        P(),
        P(),
        P(),
        P(),
        P("ep", None, None),
        P("ep", None, None),
        P("ep", None, None),
        P(("rep", "ep"), None),
        P(("rep", "ep"), None),
    )
    return jax.shard_map(
        per_device,
        mesh=mesh,
        in_specs=placed,
        out_specs=(
            P(("rep", "ep"), None),
            P(("rep", "ep"), None),
            P("ep"),
            P("ep", None),
            P("ep", None),
            P("ep", None),
            P("ep", None),
            P("ep"),
            P("ep", None),
            P("ep", None, None),
            P("ep", None, None),
            P("ep", None, None),
        ),
        check_vma=False,
    )
```

```python
import functools
import math

import jax
import jax.numpy as jnp
from jax import lax
from jax.experimental import pallas as pl
from jax.experimental.pallas import tpu as pltpu
from jax.sharding import PartitionSpec as P

QUERY_HEADS = 24
KEY_VALUE_HEADS = 8
HEAD_SIZE = 64
TOPK = 8
SEQUENCE_TOKENS = 512
BLOCK = 256
EARLY = 2


epsilon = 1e-06
masked_value = -1e30


def rope_tables(token_count):
    half = HEAD_SIZE // 2
    places = (jnp.arange(token_count) % SEQUENCE_TOKENS).astype(jnp.float32)
    rates = jnp.exp(jnp.arange(half, dtype=jnp.float32) * (-2.0 * math.log(10000.0) / HEAD_SIZE))
    angles = places[:, None] * rates[None, :]
    cosine, sine = jnp.cos(angles), jnp.sin(angles)
    return (
        jnp.concatenate([cosine] * 4, 1),
        jnp.concatenate([-sine, sine] * 2, 1),
    )


def contract(left, right, left_dim, right_dim):
    return lax.dot_general(
        left, right, (((left_dim,), (right_dim,)), ((), ())), preferred_element_type=jnp.float32
    )


def whole(array):
    return pl.BlockSpec(
        array.shape, lambda *_: (0,) * array.ndim, pipeline_mode=pl.Buffered(1)
    )


def each(array):
    return pl.BlockSpec((1,) + array.shape[1:], lambda e, *_: (e,) + (0,) * (array.ndim - 1))


VMEM_BYTES = 56 * 2**20


def expert_kernel(tile, h0, h1, c0, c1, gates0, gates1, w_gate, w_up, w_down, gh, dg, du, d_router0, d_router1):
    e = pl.program_id(0)
    tokens, lanes = gates0.shape
    expert = lax.axis_index("ep") * pl.num_programs(0) + e
    lane = lax.broadcasted_iota(jnp.int32, (tile, lanes), 1)

    @pl.when(e == 0)
    def _():
        d_router0[...] = jnp.zeros_like(d_router0)
        d_router1[...] = jnp.zeros_like(d_router1)

    for base, rows_h, rows_c, gates, d_router in (
        (0, h0, c0, gates0, d_router0),
        (tokens, h1, c1, gates1, d_router1),
    ):
        for start in range(0, tokens, tile):
            rows = slice(start, start + tile)
            out = slice(base + start, base + start + tile)
            entries = rows_h[rows, :]
            gate_pre = contract(entries, w_gate[0], 1, 0)
            up_pre = contract(entries, w_up[0], 1, 0)
            back = contract(rows_c[rows, :], w_down[0], 1, 1)
            column = jnp.sum(jnp.where(lane == expert, gates[rows, :], 0.0), 1, keepdims=True)
            sigma = jax.nn.sigmoid(gate_pre)
            swish = gate_pre * sigma
            hidden = (swish * up_pre).astype(jnp.bfloat16).astype(jnp.float32)
            d_router[rows, :] = jnp.where(
                lane == expert, jnp.sum(hidden * back, 1, keepdims=True), d_router[rows, :]
            )
            d_hidden = column * back
            dg[0, out, :] = (
                d_hidden * up_pre * (sigma * (1.0 + gate_pre * (1.0 - sigma)))
            ).astype(jnp.bfloat16)
            du[0, out, :] = (d_hidden * swish).astype(jnp.bfloat16)
            gh[0, out, :] = (column * hidden).astype(jnp.bfloat16)


def expert_pass(hs, cots, gates, w_gate, w_up, w_down):
    count, width = hs[0].shape
    tokens = 2 * count
    held, _, hidden_units = w_gate.shape
    part = jax.ShapeDtypeStruct((held, tokens, hidden_units), jnp.bfloat16)
    gate_shape = gates[0].shape
    return pl.pallas_call(
        functools.partial(expert_kernel, 256),
        grid=(held,),
        in_specs=[whole(a) for a in (*hs, *cots, *gates)] + [each(a) for a in (w_gate, w_up, w_down)],
        out_specs=[each(part)] * 3 + [pl.BlockSpec(gate_shape, lambda e: (0, 0))] * 2,
        out_shape=[part] * 3 + [jax.ShapeDtypeStruct(gate_shape, jnp.float32)] * 2,
        compiler_params=pltpu.CompilerParams(vmem_limit_bytes=VMEM_BYTES),
        cost_estimate=pl.CostEstimate(
            flops=6 * held * tokens * width * hidden_units,
            bytes_accessed=6 * held * width * hidden_units,
            transcendentals=held * tokens * hidden_units,
        ),
        name="expert_pass",
    )(*hs, *cots, *gates, w_gate, w_up, w_down)


def weight_kernel(*refs):
    hs, cots, passes, unit = refs[:4], refs[4:8], refs[8:14], refs[14]
    kind = pl.program_id(1)

    def put(lefts, rights):
        count = lefts[0].shape[0]
        result = sum(
            contract(lefts[k][...], rights[k // 2][0, (k % 2) * count : (k % 2 + 1) * count], 0, 0)
            for k in range(4)
        ).astype(jnp.bfloat16)
        rows = unit.shape[3]
        for j in range(unit.shape[1]):
            unit[0, j, 0] = result[j * rows : (j + 1) * rows]

    pl.when(kind == 0)(lambda: put(hs, passes[2:4]))
    pl.when(kind == 1)(lambda: put(hs, passes[4:6]))
    pl.when(kind == 2)(lambda: put(cots, passes[:2]))


def weight_grads(count, first, many, hs, cots, ghs, dgs, dus):
    width = hs[0].shape[1]
    _, tokens, hidden_units = dgs[0].shape
    entry = pl.BlockSpec((1, tokens, hidden_units), lambda e, k: (e + first, 0, 0))
    unit = pl.pallas_call(
        weight_kernel,
        grid=(many, 3),
        in_specs=[whole(hs[0])] * 8 + [entry] * 6,
        out_specs=pl.BlockSpec((1, count, 1, width // count, hidden_units), lambda e, k: (e, 0, k, 0, 0)),
        out_shape=jax.ShapeDtypeStruct((many, count, 3, width // count, hidden_units), jnp.bfloat16),
        compiler_params=pltpu.CompilerParams(vmem_limit_bytes=VMEM_BYTES),
        cost_estimate=pl.CostEstimate(
            flops=12 * many * tokens * width * hidden_units,
            bytes_accessed=6 * many * (width + 2 * tokens) * hidden_units,
            transcendentals=0,
        ),
        name="weight_grads",
    )(*hs, *cots, *ghs, *dgs, *dus)
    return unit.reshape(many, count, 3 * (width // count), hidden_units)


def sum_kernel(right_dim, pairs, *refs):
    lefts, rights, outs, total = refs[:pairs], refs[pairs : 2 * pairs], refs[-3:-1], refs[-1]
    e = pl.program_id(0)
    term = sum(contract(left[0], right[0], 1, right_dim) for left, right in zip(lefts, rights))

    @pl.when(e == 0)
    def _():
        total[...] = term

    @pl.when(e > 0)
    def _():
        total[...] += term

    @pl.when(e == pl.num_programs(0) - 1)
    def _():
        for k, out in enumerate(outs):
            count = out.shape[0]
            out[...] = total[k * count : (k + 1) * count].astype(out.dtype)


def sum_over_experts(lefts, rights, right_dim):
    held, tokens, inner = lefts[0].shape
    width = rights[0].shape[2 - right_dim]
    return pl.pallas_call(
        functools.partial(sum_kernel, right_dim, len(lefts)),
        grid=(held,),
        in_specs=[each(a) for a in lefts] + [each(a) for a in rights],
        out_specs=[pl.BlockSpec((tokens // 2, width), lambda e: (0, 0))] * 2,
        out_shape=[jax.ShapeDtypeStruct((tokens // 2, width), jnp.bfloat16)] * 2,
        scratch_shapes=[pltpu.VMEM((tokens, width), jnp.float32)],
        compiler_params=pltpu.CompilerParams(vmem_limit_bytes=VMEM_BYTES),
        cost_estimate=pl.CostEstimate(
            flops=2 * len(lefts) * held * tokens * width * inner,
            bytes_accessed=2 * len(lefts) * held * (tokens + width) * inner,
            transcendentals=0,
        ),
        name="sum_over_experts",
    )(*lefts, *rights)


def rotate(values, cosine, sine, way):
    lane = lax.broadcasted_iota(jnp.int32, cosine.shape, 1)
    first = lane % HEAD_SIZE < HEAD_SIZE // 2
    lanes = cosine.shape[1]
    half = HEAD_SIZE // 2
    pieces = []
    for start in range(0, values.shape[1], lanes):
        piece = values[:, start : start + lanes]
        other = jnp.where(first, pltpu.roll(piece, lanes - half, 1), pltpu.roll(piece, half, 1))
        pieces.append(piece * cosine + way * (other * sine))
    return jnp.concatenate(pieces, 1)


def heads_of(array, group, rows, queries):
    return jnp.concatenate(
        [
            array[rows, (group * queries + j) * HEAD_SIZE : (group * queries + j + 1) * HEAD_SIZE]
            for j in range(queries)
        ],
        0,
    )


def chosen_of(routes, shape):
    expert = lax.broadcasted_iota(jnp.int32, shape, 1)
    picks = routes[...].T
    chosen = picks[:, :1] == expert
    for k in range(1, picks.shape[1]):
        chosen = chosen | (picks[:, k : k + 1] == expert)
    return chosen


def attention_kernel(
    tokens, norm_attn, w_query, w_key, w_value, cosine, sine, w_out, norm_ffn, w_router, routes,
    normed, queries, keys, values, log_totals, attn, resid, h_two, probs, combine,
):
    count, width = tokens.shape
    field = tokens[...].astype(jnp.float32)
    inverse = lax.rsqrt(jnp.mean(field * field, -1, keepdims=True) + epsilon)
    first = (field * inverse * norm_attn[...].astype(jnp.float32)).astype(jnp.bfloat16)
    normed[...] = first
    queries[...] = rotate(contract(first, w_query[...], 1, 0), cosine[...], sine[...], 1).astype(jnp.bfloat16)
    keys[...] = rotate(contract(first, w_key[...], 1, 0), cosine[...], sine[...], 1).astype(jnp.bfloat16)
    values[...] = contract(first, w_value[...], 1, 0).astype(jnp.bfloat16)
    groups = keys.shape[1] // HEAD_SIZE
    per_group = queries.shape[1] // keys.shape[1]
    lane = lax.broadcasted_iota(jnp.int32, (BLOCK, log_totals.shape[1]), 1)
    for block in range(count // BLOCK):
        rows = slice(block * BLOCK, (block + 1) * BLOCK)
        seen = slice(0, (block + 1) * BLOCK)
        logs = jnp.zeros((BLOCK, log_totals.shape[1]), jnp.float32)
        for group in range(groups):
            cut = slice(group * HEAD_SIZE, (group + 1) * HEAD_SIZE)
            scores = contract(heads_of(queries, group, rows, per_group), keys[seen, cut], 1, 1)
            scores = scores * HEAD_SIZE ** (-0.5)
            highest = jnp.max(scores, -1, keepdims=True)
            shifted = jnp.exp(scores - highest)
            sums = jnp.sum(shifted, -1, keepdims=True)
            probs_bf = (shifted * (1.0 / sums)).astype(jnp.bfloat16)
            mix = contract(probs_bf, values[seen, cut], 1, 0).astype(jnp.bfloat16)
            log_sum = highest + jnp.log(sums)
            for j in range(per_group):
                head = group * per_group + j
                part = slice(j * BLOCK, (j + 1) * BLOCK)
                attn[rows, head * HEAD_SIZE : (head + 1) * HEAD_SIZE] = mix[part]
                logs = jnp.where(lane == head, log_sum[part], logs)
        log_totals[rows, :] = logs
    total = field + contract(attn[...], w_out[...], 1, 0)
    resid[...] = total
    inverse = lax.rsqrt(jnp.mean(total * total, -1, keepdims=True) + epsilon)
    second = (total * inverse * norm_ffn[...].astype(jnp.float32)).astype(jnp.bfloat16)
    h_two[...] = second
    logits = contract(second, w_router[...], 1, 1)
    shifted = jnp.exp(logits - jnp.max(logits, -1, keepdims=True))
    soft = shifted / jnp.sum(shifted, -1, keepdims=True)
    probs[...] = soft
    combine[...] = jnp.where(chosen_of(routes, logits.shape), soft, 0.0)


LANES = 128


def attention_forward(tokens, norm_attn, w_query, w_key, w_value, cosine, sine, w_out, norm_ffn, w_router, routes):
    count, width = tokens.shape
    experts = w_router.shape[1]
    key_width = w_key.shape[1]
    shape = jax.ShapeDtypeStruct
    return pl.pallas_call(
        attention_kernel,
        out_shape=[
            shape((count, width), jnp.bfloat16),
            shape((count, width), jnp.bfloat16),
            shape((count, key_width), jnp.bfloat16),
            shape((count, key_width), jnp.bfloat16),
            shape((count, LANES), jnp.float32),
            shape((count, width), jnp.bfloat16),
            shape((count, width), jnp.float32),
            shape((count, width), jnp.bfloat16),
            shape((count, experts), jnp.float32),
            shape((count, experts), jnp.float32),
        ],
        compiler_params=pltpu.CompilerParams(vmem_limit_bytes=VMEM_BYTES),
        cost_estimate=pl.CostEstimate(
            flops=6 * count * width * width, bytes_accessed=8 * width * width, transcendentals=24 * count * count
        ),
        name="attention_forward",
    )(
        tokens, norm_attn[None], w_query, w_key, w_value, cosine, sine, w_out, norm_ffn[None], w_router.T, routes.T
    )


def as_lane(row):
    first = lax.broadcasted_iota(jnp.int32, (LANES, row.shape[1]), 0) == 0
    return jnp.where(first, row, 0.0).T.astype(jnp.bfloat16)


def attention_back_kernel(
    dh_own, dh_near, dh_far, router_own, router_near, router_far, routes, probs, resid, norm_ffn, cotangent, w_router, w_out, h_two, attn,
    queries, keys, values, log_totals, cosine, sine,
    d_resid, d_pre, grad_out, d_branch, d_attn, d_queries, d_keys, d_values,
):
    count, width = resid.shape
    experts = probs.shape[1]
    soft = probs[...]
    to_router = jnp.where(
        chosen_of(routes, soft.shape), router_own[...] + router_near[...] + router_far[...], 0.0
    )
    d_logits = (soft * (to_router - jnp.sum(soft * to_router, -1, keepdims=True))).astype(jnp.bfloat16)
    d_normed = (
        dh_own[...].astype(jnp.float32)
        + dh_near[...].astype(jnp.float32)
        + dh_far[...].astype(jnp.float32)
        + contract(d_logits, w_router[...], 1, 0)
    )
    total = resid[...]
    inverse = lax.rsqrt(jnp.mean(total * total, -1, keepdims=True) + epsilon)
    normal = total * inverse
    scaled = d_normed * norm_ffn[...].astype(jnp.float32)
    back = cotangent[...].astype(jnp.float32) + inverse * (
        scaled - normal * jnp.mean(scaled * normal, -1, keepdims=True)
    )
    d_resid[...] = back
    d_branch[...] = back.astype(jnp.bfloat16)
    grad_out[:, :width] = contract(attn[...], d_branch[...], 0, 0).astype(jnp.bfloat16)
    d_logits = jnp.concatenate([d_logits, jnp.zeros((count, LANES - experts), jnp.bfloat16)], 1)
    grad_out[:, width : width + LANES] = contract(h_two[...], d_logits, 0, 0).astype(jnp.bfloat16)
    grad_out[:, width + LANES :] = as_lane(jnp.sum(d_normed * normal, 0, keepdims=True))
    d_attn[...] = contract(d_branch[...], w_out[...], 1, 1).astype(jnp.bfloat16)
    groups = keys.shape[1] // HEAD_SIZE
    per_group = queries.shape[1] // keys.shape[1]
    factor = HEAD_SIZE ** (-0.5)
    lane = lax.broadcasted_iota(jnp.int32, (BLOCK, log_totals.shape[1]), 1)
    for block in reversed(range(count // BLOCK)):
        rows = slice(block * BLOCK, (block + 1) * BLOCK)
        seen = slice(0, (block + 1) * BLOCK)
        logs = log_totals[rows, :]
        for group in range(groups):
            cut = slice(group * HEAD_SIZE, (group + 1) * HEAD_SIZE)
            part_q = heads_of(queries, group, rows, per_group)
            part_d = heads_of(d_attn, group, rows, per_group)
            log_sum = jnp.concatenate(
                [
                    jnp.sum(jnp.where(lane == group * per_group + j, logs, 0.0), 1, keepdims=True)
                    for j in range(per_group)
                ],
                0,
            )
            part_k, part_v = keys[seen, cut], values[seen, cut]
            probs_f = jnp.exp(contract(part_q, part_k, 1, 1) * factor - log_sum)
            d_probs = contract(part_d, part_v, 1, 1)
            centre = jnp.sum(probs_f * d_probs, -1, keepdims=True)
            d_scores = (probs_f * (d_probs - centre)).astype(jnp.bfloat16)
            turned = contract(d_scores, part_k, 1, 0) * factor
            for j in range(per_group):
                head = group * per_group + j
                d_queries[rows, head * HEAD_SIZE : (head + 1) * HEAD_SIZE] = turned[j * BLOCK : (j + 1) * BLOCK]
            new_k = contract(d_scores, part_q, 0, 0) * factor
            new_v = contract(probs_f.astype(jnp.bfloat16), part_d, 0, 0)
            if block == count // BLOCK - 1:
                d_keys[seen, cut] = new_k
                d_values[seen, cut] = new_v
            else:
                d_keys[seen, cut] += new_k
                d_values[seen, cut] += new_v
    key_width = keys.shape[1]
    d_pre[:, :width] = rotate(d_queries[...], cosine[...], sine[...], -1).astype(jnp.bfloat16)
    d_pre[:, width : width + key_width] = rotate(d_keys[...], cosine[...], sine[...], -1).astype(jnp.bfloat16)
    d_pre[:, width + key_width :] = d_values[...].astype(jnp.bfloat16)


def attention_back(dh_own, dh_near, dh_far, router_own, router_near, router_far, routes, probs, resid, norm_ffn, cotangent, w_router, w_out, h_two, attn,
                   queries, keys, values, log_totals, cosine, sine):
    count, width = resid.shape
    key_width = keys.shape[1]
    shape = jax.ShapeDtypeStruct
    return pl.pallas_call(
        attention_back_kernel,
        out_shape=[
            shape((count, width), jnp.float32),
            shape((count, width + 2 * key_width), jnp.bfloat16),
            shape((width, width + 2 * LANES), jnp.bfloat16),
        ],
        scratch_shapes=[
            pltpu.VMEM((count, width), jnp.bfloat16),
            pltpu.VMEM((count, width), jnp.bfloat16),
            pltpu.VMEM((count, width), jnp.float32),
            pltpu.VMEM((count, key_width), jnp.float32),
            pltpu.VMEM((count, key_width), jnp.float32),
        ],
        compiler_params=pltpu.CompilerParams(vmem_limit_bytes=VMEM_BYTES),
        cost_estimate=pl.CostEstimate(
            flops=10 * count * width * width, bytes_accessed=8 * width * width, transcendentals=24 * count * count
        ),
        name="attention_back",
    )(
        dh_own, dh_near, dh_far, router_own, router_near, router_far, routes.T, probs, resid, norm_ffn[None], cotangent,
        w_router.T, w_out, h_two, attn, queries, keys, values, log_totals, cosine, sine,
    )


def input_kernel(d_pre, normed, tokens, norm_attn, d_resid, w_query, w_key, w_value, d_input, grads):
    width, key_width = w_query.shape[1], w_key.shape[1]
    entries = d_pre[...]
    d_normed = (
        contract(entries[:, :width], w_query[...], 1, 1)
        + contract(entries[:, width : width + key_width], w_key[...], 1, 1)
        + contract(entries[:, width + key_width :], w_value[...], 1, 1)
    )
    field = tokens[...].astype(jnp.float32)
    inverse = lax.rsqrt(jnp.mean(field * field, -1, keepdims=True) + epsilon)
    normal = field * inverse
    scaled = d_normed * norm_attn[...].astype(jnp.float32)
    d_input[...] = d_resid[...] + inverse * (scaled - normal * jnp.mean(scaled * normal, -1, keepdims=True))
    wide = entries.shape[1]
    grads[:, :wide] = contract(normed[...], entries, 0, 0).astype(jnp.bfloat16)
    grads[:, wide : wide + LANES] = as_lane(jnp.sum(d_normed * normal, 0, keepdims=True))
    grads[:, wide + LANES :] = jnp.zeros((width, LANES), jnp.bfloat16)


def input_back(d_pre, normed, tokens, norm_attn, d_resid, w_query, w_key, w_value):
    count, width = tokens.shape
    shape = jax.ShapeDtypeStruct
    return pl.pallas_call(
        input_kernel,
        out_shape=[
            shape((count, width), jnp.float32),
            shape((width, d_pre.shape[1] + 2 * LANES), jnp.bfloat16),
        ],
        compiler_params=pltpu.CompilerParams(vmem_limit_bytes=VMEM_BYTES),
        cost_estimate=pl.CostEstimate(
            flops=8 * count * width * width, bytes_accessed=12 * width * width, transcendentals=0
        ),
        name="input_back",
    )(d_pre, normed, tokens, norm_attn[None], d_resid, w_query, w_key, w_value)


SLOTS = 3


def ring_device(place, count):
    back = place // (count // 2)
    return (1 - back) * 2 * place + back * (2 * (count - 1 - place) + 1)


def ring_place(count):
    here = lax.axis_index("rep")
    odd = here % 2
    rank = here // 2 + odd * (count - 1 - 2 * (here // 2))
    after = ring_device((rank + 1) % count, count)
    before = ring_device((rank + count - 1) % count, count)
    return rank, after, before


def group_places():
    holder = lax.axis_index("ep")
    core = holder + 1 - 2 * (holder % 2)
    return holder, core, (holder + 2) % 4, (core + 2) % 4


def greet(after, before, core, chip):
    barrier = pltpu.get_barrier_semaphore()
    for neighbour in (before, after):
        pl.semaphore_signal(barrier, inc=1, device_id={"rep": neighbour})
    for neighbour in (core, chip):
        pl.semaphore_signal(barrier, inc=1, device_id={"ep": neighbour})
    pl.semaphore_wait(barrier, 4)


def ring_tools(count, shapes, sources, sums, held, terms, semaphores):
    arrived, sent, loaded, stored, credit = semaphores
    rank, after, before = ring_place(count)
    hops = 2 * (count - 1)

    def columns(index, way):
        half = shapes[index][1] // 2
        return pl.ds(way * half, half)

    def send(index, way, hop):
        stream = 2 * index + way
        source = (hop + SLOTS - 1) % SLOTS
        slot = hop % SLOTS
        return pltpu.make_async_remote_copy(
            src_ref=held[index].at[way, source],
            dst_ref=held[index].at[way, slot],
            send_sem=sent.at[stream, slot],
            recv_sem=arrived.at[stream, slot],
            device_id={"rep": before if way else after},
        )

    def load(index, way, hop):
        step = hop + 2
        chunk = (rank + step) % count if way else (rank + 2 * count - step) % count
        return pltpu.make_async_copy(
            sources[index].at[chunk, :, columns(index, way)],
            terms[index].at[way, hop % 2],
            loaded.at[2 * index + way, hop % 2],
        )

    def first(index, way):
        chunk = (rank + 1) % count if way else (rank + count - 1) % count
        return pltpu.make_async_copy(
            sources[index].at[chunk, :, columns(index, way)],
            held[index].at[way, SLOTS - 1],
            stored.at[2 * index + way, SLOTS - 1],
        )

    def store(index, way, hop):
        step = hop - (count - 2)
        chunk = (rank + step) % count if way else (rank + count - step) % count
        return pltpu.make_async_copy(
            held[index].at[way, hop % SLOTS],
            sums[index].at[chunk, :, columns(index, way)],
            stored.at[2 * index + way, hop % SLOTS],
        )

    def release(index, way):
        pl.semaphore_signal(
            credit.at[2 * index + way], inc=1, device_id={"rep": after if way else before}
        )

    def begin(streams):
        for index, way in streams:
            first(index, way).start()
        for index, way in streams:
            load(index, way, 0).start()
            load(index, way, 1).start()
        for index, way in streams:
            first(index, way).wait()
            send(index, way, 0).start()

    def take(index, way, hop):
        send(index, way, hop).wait_recv()
        send(index, way, hop).wait_send()

    def pass_on(index, way, hop):
        @pl.when(hop + 1 >= 2)
        def _():
            pl.semaphore_wait(credit.at[2 * index + way], 1)

        send(index, way, hop + 1).start()

    def add_step(streams, hop):
        for index, way in streams:
            take(index, way, hop)

            @pl.when(hop <= hops - 3)
            def _():
                release(index, way)

            load(index, way, hop).wait()
            slot = hop % SLOTS
            held[index][way, slot] = (
                held[index][way, slot].astype(jnp.float32)
                + terms[index][way, hop % 2].astype(jnp.float32)
            ).astype(jnp.bfloat16)
            pass_on(index, way, hop)

            @pl.when(hop + 2 <= count - 2)
            def _():
                load(index, way, hop + 2).start()

            @pl.when(hop == count - 2)
            def _():
                store(index, way, hop).start()

    def hand_step(streams, hop):
        for index, way in streams:
            take(index, way, hop)
            store(index, way, hop - 1).wait()

            @pl.when(hop <= hops - 3)
            def _():
                release(index, way)

            @pl.when(hop + 1 < hops)
            def _():
                pass_on(index, way, hop)

            store(index, way, hop).start()

    def end(streams):
        for index, way in streams:
            store(index, way, hops - 1).wait()

    return begin, add_step, hand_step, end


def both_ways(indices):
    return [(index, way) for index in indices for way in (0, 1)]


def ring_kernel(count, many, lag, shapes, *refs):
    dense = len(shapes) - many
    inputs, outputs, rest = refs[: 1 + dense], refs[1 + dense : 2 + 2 * dense], refs[2 + 2 * dense :]
    total = len(shapes)
    held, terms, rest = rest[:total], rest[total : 2 * total], rest[2 * total :]
    own, near, far, joined, rest = (
        rest[:dense], rest[dense : 2 * dense], rest[2 * dense : 3 * dense], rest[3 * dense : 4 * dense], rest[4 * dense :]
    )
    near_sent, near_arrived, own_loaded, far_sent, far_arrived = rest[:5]
    sources = [inputs[0].at[k] for k in range(many)] + list(joined)
    sums = [outputs[0].at[k] for k in range(many)] + list(outputs[1:])
    _, after, before = ring_place(count)
    holder, core, chip, far_core = group_places()
    hops = 2 * (count - 1)
    greet(after, before, core, chip)
    begin, add_step, hand_step, end = ring_tools(count, shapes, sources, sums, held, terms, rest[5:])

    def block(k, index):
        rows = own[k].shape[1]
        return inputs[1 + k].at[pl.ds(pl.multiple_of(index * rows, 8), rows), :]

    def to_core(k, part):
        return pltpu.make_async_remote_copy(
            src_ref=block(k, far_core if part else core),
            dst_ref=near[k].at[part],
            send_sem=near_sent.at[k, part],
            recv_sem=near_arrived.at[k, part],
            device_id={"ep": core},
        )

    def own_block(k, part):
        return pltpu.make_async_copy(
            block(k, chip if part else holder), own[k].at[part], own_loaded.at[k, part]
        )

    def to_chip(k):
        return pltpu.make_async_remote_copy(
            src_ref=own[k].at[1],
            dst_ref=far[k],
            send_sem=far_sent.at[k],
            recv_sem=far_arrived.at[k],
            device_id={"ep": chip},
        )

    pieces = 8

    def send_far():
        for k in range(dense):
            to_core(k, 1).wait_recv()
            own_block(k, 1).wait()
            rows = own[k].shape[1] // pieces
            for j in range(pieces):
                cut = slice(j * rows, (j + 1) * rows)
                own[k][1, cut] = (
                    own[k][1, cut].astype(jnp.float32) + near[k][1, cut].astype(jnp.float32)
                ).astype(jnp.bfloat16)
            to_chip(k).start()

    def join():
        for k in range(dense):
            to_core(k, 0).wait_recv()
            own_block(k, 0).wait()
            to_chip(k).wait_recv()
            to_chip(k).wait_send()
            for part in (0, 1):
                to_core(k, part).wait_send()
            rows = joined[k].shape[1]
            for j in range(count):
                if j * rows < own[k].shape[1]:
                    cut = slice(j * rows, (j + 1) * rows)
                    joined[k][j] = (
                        own[k][0, cut].astype(jnp.float32)
                        + near[k][0, cut].astype(jnp.float32)
                        + far[k][cut].astype(jnp.float32)
                    ).astype(jnp.bfloat16)
                else:
                    joined[k][j] = jnp.zeros(joined[k].shape[1:], jnp.bfloat16)

    early_streams, late_streams = both_ways(range(many)), both_ways(range(many, total))
    for k in range(dense):
        for part in (1, 0):
            to_core(k, part).start()
            own_block(k, part).start()
    begin(early_streams)
    ends = sorted({0, 1, lag, count - 1, hops, lag + count - 1, lag + hops})
    for low, high in zip(ends[:-1], ends[1:]):
        if low == 1:
            send_far()
        if low == lag:
            join()
            begin(late_streams)

        def ticks(tick, carry, low=low):
            for streams, start in ((early_streams, 0), (late_streams, lag)):
                if start <= low < start + count - 1:
                    add_step(streams, tick - start)
                elif start + count - 1 <= low < start + hops:
                    hand_step(streams, tick - start)
            return carry

        lax.fori_loop(low, high, ticks, 0)
    end(early_streams + late_streams)


def ring_sum(late, partials):
    many, count = late.shape[:2]
    quarters = [(partial.shape[0] // 4, partial.shape[1]) for partial in partials]
    cuts = [(-(-rows // (8 * count)) * 8, columns) for rows, columns in quarters]
    shapes = [late.shape[2:]] * many + cuts
    total, dense = len(shapes), len(partials)
    halves = [(rows, columns // 2) for rows, columns in shapes]
    size = late.size + sum(partial.size for partial in partials)
    dma = pltpu.SemaphoreType.DMA
    return pl.pallas_call(
        functools.partial(ring_kernel, count, many, 5, shapes),
        out_shape=[jax.ShapeDtypeStruct(late.shape, late.dtype)]
        + [jax.ShapeDtypeStruct((count,) + cut, late.dtype) for cut in cuts],
        in_specs=[pl.BlockSpec(memory_space=pl.ANY)] * (1 + dense),
        out_specs=[pl.BlockSpec(memory_space=pl.ANY)] * (1 + dense),
        scratch_shapes=[pltpu.VMEM((2, SLOTS) + half, jnp.bfloat16) for half in halves]
        + [pltpu.VMEM((2, 2) + half, jnp.bfloat16) for half in halves]
        + [pltpu.VMEM((2,) + quarter, jnp.bfloat16) for quarter in quarters]
        + [pltpu.VMEM((2,) + quarter, jnp.bfloat16) for quarter in quarters]
        + [pltpu.VMEM(quarter, jnp.bfloat16) for quarter in quarters]
        + [pltpu.VMEM((count,) + cut, jnp.bfloat16) for cut in cuts]
        + [
            dma((dense, 2)),
            dma((dense, 2)),
            dma((dense, 2)),
            dma((dense,)),
            dma((dense,)),
            dma((2 * total, SLOTS)),
            dma((2 * total, SLOTS)),
            dma((2 * total, 2)),
            dma((2 * total, SLOTS)),
            pltpu.SemaphoreType.REGULAR((2 * total,)),
        ],
        compiler_params=pltpu.CompilerParams(
            collective_id=0, has_side_effects=True, vmem_limit_bytes=VMEM_BYTES
        ),
        cost_estimate=pl.CostEstimate(flops=2 * size, bytes_accessed=8 * size, transcendentals=0),
        name="ring_sum",
    )(late, *partials)


def overlap_kernel(count, first, shapes, *refs):
    unit, near, far, (w_gate, w_up, w_down), hs, cots = (
        refs[0], refs[1:4], refs[4:7], refs[7:10], refs[10:14], refs[14:18]
    )
    unit_sum, grads, outs, refs = refs[18], refs[19], refs[20:26], refs[26:]
    many = len(shapes)
    held_slots, terms, refs = refs[:many], refs[many : 2 * many], refs[2 * many :]
    (
        left_a, left_b, right_a, right_b, right_c, total, total_w, stage, stage_w, from_core, from_chip,
        ready, core_sent, core_arrived, chip_sent, chip_arrived, out_done, grads_done,
    ) = refs[:18]
    held = w_gate.shape[0]
    tokens = hs[0].shape[0]
    _, after, before = ring_place(count)
    holder, core, chip, _ = group_places()
    hops = 2 * (count - 1)
    greet(after, before, core, chip)
    streams = both_ways(range(many))
    begin, add_step, hand_step, end = ring_tools(
        count,
        shapes,
        [unit.at[k] for k in range(many)],
        [unit_sum.at[k] for k in range(many)],
        held_slots,
        terms,
        refs[18:],
    )

    def tick(hop):
        pl.when(hop < count - 1)(lambda: add_step(streams, hop))
        pl.when((hop >= count - 1) & (hop < hops))(lambda: hand_step(streams, hop))

    def copies(bank, *pairs):
        return [pltpu.make_async_copy(source, target, ready.at[bank, k]) for source, target, k in pairs]

    def load_dh(side, e, bank):
        return copies(
            bank,
            (side[1].at[e], left_a.at[bank], 0),
            (side[2].at[e], left_b.at[bank], 1),
            (w_gate.at[e], right_a.at[bank], 2),
            (w_up.at[e], right_b.at[bank], 3),
        )

    def load_y(side, e, bank):
        return copies(bank, (side[0].at[e], left_a.at[bank], 0), (w_down.at[e], right_c.at[bank], 4))

    def load_w(e, kind, part, bank):
        side = (near, far)[part // 2]
        rows = pl.ds((part % 2) * tokens, tokens)
        right = side[(1, 2, 0)[kind]].at[e, rows, :]
        left = (hs, hs, cots)[kind][part]
        return copies(bank, (right, left_a.at[bank, pl.ds(0, tokens), :], 0), (left, right_c.at[bank], 4))

    def begin_all(made):
        for copy in made:
            copy.start()

    def await_all(made):
        for copy in made:
            copy.wait()

    def to_core(k):
        return pltpu.make_async_remote_copy(
            src_ref=stage.at[k % 2, 1],
            dst_ref=from_core.at[k],
            send_sem=core_sent.at[k],
            recv_sem=core_arrived.at[k],
            device_id={"ep": core},
        )

    def to_chip(k):
        return pltpu.make_async_remote_copy(
            src_ref=stage.at[0, 0],
            dst_ref=from_chip.at[k // 2],
            send_sem=chip_sent.at[k // 2],
            recv_sem=chip_arrived.at[k // 2],
            device_id={"ep": chip},
        )

    def send_chip(k):
        to_core(k).wait_recv()
        stage[0, 0] = (stage[0, 0].astype(jnp.float32) + from_core[k].astype(jnp.float32)).astype(jnp.bfloat16)
        to_chip(k).start()

    def own_out(k):
        return pltpu.make_async_copy(stage.at[1, 0], outs[3 * (k // 2)], out_done.at[3 * (k // 2)])

    def near_out(k):
        return pltpu.make_async_copy(from_core.at[k], outs[3 * (k // 2) + 1], out_done.at[3 * (k // 2) + 1])

    def far_out(k):
        return pltpu.make_async_copy(from_chip.at[k // 2], outs[3 * (k // 2) + 2], out_done.at[3 * (k // 2) + 2])

    plans = [(load_dh, far), (load_dh, near), (load_y, far), (load_y, near)]
    begin_all(load_dh(far, 0, 0))
    begin(streams)
    hop = 0
    for k, (loader, side) in enumerate(plans):
        base = k * held

        def next_first(bank, k=k):
            if k + 1 < len(plans):
                begin_all(plans[k + 1][0](plans[k + 1][1], 0, bank))
            else:
                begin_all(load_w(first, 0, 0, bank))

        every = 2 if loader is load_dh else 3

        def piece(e, carry, k=k, loader=loader, side=side, base=base, hop=hop, every=every, next_first=next_first):
            bank = (base + e) % 2
            await_all(loader(side, e, bank))

            @pl.when(e + 1 < held)
            def _():
                begin_all(loader(side, e + 1, 1 - bank))

            @pl.when(e + 1 == held)
            def _():
                next_first(1 - bank)

            if loader is load_dh:
                term = contract(left_a[bank], right_a[bank], 1, 1) + contract(left_b[bank], right_b[bank], 1, 1)
            else:
                term = contract(left_a[bank], right_c[bank], 1, 0)

            @pl.when(e == 0)
            def _():
                total[...] = term

            @pl.when(e > 0)
            def _():
                total[...] += term

            @pl.when((e + 1) % every == 0)
            def _():
                tick(hop + e // every)

            if k % 2 == 1:

                @pl.when(e == 1)
                def _():
                    send_chip(k - 1)

            return carry

        lax.fori_loop(0, held, piece, 0)
        hop += held // every
        if k >= 2:
            to_core(k - 2).wait_send()
            if k == 2:
                to_chip(0).wait_send()
            else:
                own_out(1).wait()
        for half in (0, 1):
            stage[k % 2, half] = total[half * tokens : (half + 1) * tokens].astype(jnp.bfloat16)
        to_core(k).start()
        if k % 2 == 1:
            own_out(k).start()
        tick(hop)
        hop += 1

    kinds = 3
    base = len(plans) * held

    def grads_out(e, kind):
        slot = (kinds * e + kind) % 2
        return pltpu.make_async_copy(stage_w.at[slot], grads.at[e, :, kind], grads_done.at[slot])

    def expert(e, carry):
        for kind in range(kinds):
            for part in range(4):
                bank = (base + 4 * kind + part) % 2
                await_all(load_w(e + first, kind, part, bank))
                if part < 3:
                    begin_all(load_w(e + first, kind, part + 1, 1 - bank))
                elif kind < kinds - 1:
                    begin_all(load_w(e + first, kind + 1, 0, 1 - bank))
                else:

                    @pl.when(e + first + 1 < held)
                    def _():
                        begin_all(load_w(e + first + 1, 0, 0, 1 - bank))

                term = contract(right_c[bank], left_a[bank, :tokens], 0, 0)
                if part == 0:
                    total_w[...] = term
                else:
                    total_w[...] += term

            @pl.when(kinds * e + kind >= 2)
            def _():
                grads_out(e, kind).wait()

            slot = (kinds * e + kind) % 2
            rows = stage_w.shape[2]
            for j in range(count):
                stage_w[slot, j] = total_w[j * rows : (j + 1) * rows].astype(jnp.bfloat16)
            grads_out(e, kind).start()
            if kind != 1:
                tick(hop + 2 * e + kind // 2)
        return carry

    late = held - first
    lax.fori_loop(0, late, expert, 0)
    hop += 2 * late

    def drain(step, carry):
        tick(step)
        return carry

    lax.fori_loop(hop, max(hop, hops), drain, 0)
    end(streams)
    for k in (1, 3):
        to_core(k).wait_recv()
        near_out(k).start()
    for k in (0, 2):
        to_chip(k).wait_recv()
        far_out(k).start()
    for kind in (kinds - 2, kinds - 1):
        grads_out(late - 1, kind).wait()
    own_out(3).wait()
    to_chip(2).wait_send()
    for k in (2, 3):
        to_core(k).wait_send()
    for k in (1, 3):
        near_out(k).wait()
    for k in (0, 2):
        far_out(k).wait()


def overlap(unit, near, far, w_gate, w_up, w_down, hs, cots, first):
    many, count, rows3, columns = unit.shape
    tokens, width = hs[0].shape
    held = w_gate.shape[0]
    shape, half = (rows3, columns), (rows3, columns // 2)
    block = jax.ShapeDtypeStruct((tokens, width), jnp.bfloat16)
    dma = pltpu.SemaphoreType.DMA

    def buffers(*shape):
        return pltpu.VMEM(shape, jnp.bfloat16)

    flops = 2 * tokens * width * columns * (4 * 3 * held + 12 * (held - first))
    inputs = [unit, *near, *far, w_gate, w_up, w_down, *hs, *cots]
    unit_sum, grads, *blocks = pl.pallas_call(
        functools.partial(overlap_kernel, count, first, [shape] * many),
        out_shape=[
            jax.ShapeDtypeStruct(unit.shape, unit.dtype),
            jax.ShapeDtypeStruct((held - first, count, 3, rows3 // 3, columns), jnp.bfloat16),
        ]
        + [block] * 6,
        in_specs=[pl.BlockSpec(memory_space=pl.ANY)] * len(inputs),
        out_specs=[pl.BlockSpec(memory_space=pl.ANY)] * 8,
        scratch_shapes=[
            *[buffers(2, SLOTS, *half)] * many,
            *[buffers(2, 2, *half)] * many,
            buffers(2, 2 * tokens, columns),
            buffers(2, 2 * tokens, columns),
            buffers(2, width, columns),
            buffers(2, width, columns),
            buffers(2, columns, width),
            pltpu.VMEM((2 * tokens, width), jnp.float32),
            pltpu.VMEM((width, columns), jnp.float32),
            buffers(2, 2, tokens, width),
            buffers(2, count, rows3 // 3, columns),
            buffers(4, tokens, width),
            buffers(2, tokens, width),
            dma((2, 5)),
            dma((4,)),
            dma((4,)),
            dma((2,)),
            dma((2,)),
            dma((6,)),
            dma((2,)),
            dma((2 * many, SLOTS)),
            dma((2 * many, SLOTS)),
            dma((2 * many, 2)),
            dma((2 * many, SLOTS)),
            pltpu.SemaphoreType.REGULAR((2 * many,)),
        ],
        compiler_params=pltpu.CompilerParams(
            collective_id=1, has_side_effects=True, vmem_limit_bytes=VMEM_BYTES
        ),
        cost_estimate=pl.CostEstimate(flops=flops, bytes_accessed=8 * unit.size, transcendentals=0),
        name="overlap",
    )(*inputs)
    grads = grads.reshape(held - first, count, rows3, columns)
    return unit_sum, grads, blocks[:3], blocks[3:]


def finish_kernel(firsts, *refs):
    units, (dense_o, dense_qkv) = refs[: len(firsts) - 1], refs[len(firsts) - 1 : len(firsts) + 1]
    gate, up, down, out, query, key, value, extra_o, extra_qkv = refs[len(firsts) + 1 :]

    @pl.when((pl.program_id(0) == 0) & (pl.program_id(1) == 0))
    def _():
        for dense, parts in ((dense_o, (out, extra_o)), (dense_qkv, (query, key, value, extra_qkv))):
            start = 0
            for part in parts:
                columns = part.shape[1]
                rows = dense.shape[1]
                for j in range(part.shape[0] // rows):
                    part[j * rows : (j + 1) * rows] = dense[j, :, start : start + columns].astype(jnp.float32)
                start += columns

    for index, unit in enumerate(units):
        e = pl.program_id(0)

        @pl.when((e >= firsts[index]) & (e < firsts[index + 1]))
        def _():
            rows = unit.shape[2] // 3
            for k in range(unit.shape[1]):
                gate[0, k * rows : (k + 1) * rows] = unit[0, k, :rows].astype(jnp.float32)
                up[0, k * rows : (k + 1) * rows] = unit[0, k, rows : 2 * rows].astype(jnp.float32)
            turned = jnp.concatenate([unit[0, k, 2 * rows :] for k in range(unit.shape[1])], 0)
            down[0] = turned.astype(jnp.float32).T


def finish(units, dense, width, key_width):
    count, rows3, columns = units[0].shape[1:]
    rows = rows3 // 3
    pair = count // 4
    small = [
        jax.ShapeDtypeStruct((width // 4, part), jnp.float32)
        for part in (width, width, key_width, key_width, 2 * LANES, 2 * LANES)
    ]
    firsts = [0]
    for unit in units:
        firsts.append(firsts[-1] + unit.shape[0])
    experts = firsts[-1]

    def place(index):
        first, end = firsts[index], firsts[index + 1]

        def chunk(e, c):
            inside = jnp.clip(e, first, end - 1)
            return (inside - first, jnp.where(e < first, 0, jnp.where(e >= end, 3, c)), 0, 0)

        return chunk

    return pl.pallas_call(
        functools.partial(finish_kernel, firsts),
        grid=(experts, 4),
        in_specs=[pl.BlockSpec((1, pair, rows3, columns), place(index)) for index in range(len(units))]
        + [whole(part) for part in dense],
        out_specs=[
            pl.BlockSpec((1, pair * rows, columns), lambda e, c: (e, c, 0)),
            pl.BlockSpec((1, pair * rows, columns), lambda e, c: (e, c, 0)),
            pl.BlockSpec((1, columns, pair * rows), lambda e, c: (e, 0, c)),
        ]
        + [whole(part) for part in small],
        out_shape=[
            jax.ShapeDtypeStruct((experts, width, columns), jnp.float32),
            jax.ShapeDtypeStruct((experts, width, columns), jnp.float32),
            jax.ShapeDtypeStruct((experts, columns, width), jnp.float32),
        ]
        + small,
        name="finish",
        compiler_params=pltpu.CompilerParams(vmem_limit_bytes=VMEM_BYTES),
    )(*units, *dense)


def swap_core(value):
    return lax.ppermute(value, "ep", [(0, 1), (1, 0), (2, 3), (3, 2)])


def swap_chip(value):
    return lax.ppermute(value, "ep", [(0, 2), (2, 0), (1, 3), (3, 1)])


def add_bf(a, b):
    return (a.astype(jnp.float32) + b.astype(jnp.float32)).astype(jnp.bfloat16)


def per_device(
    tokens,
    norm_attn,
    w_query,
    key_projection,
    value_projection,
    w_out,
    norm_ffn,
    w_router,
    w_gate,
    w_up,
    w_down,
    routes,
    cotangent,
):
    token_count, width = tokens.shape
    experts_all = w_router.shape[1]
    held = w_gate.shape[0]
    replicas = lax.axis_size("rep")
    cot_near = (cotangent, swap_core(cotangent))
    cot_far = swap_chip(cotangent)
    cosine, sine = rope_tables(token_count)
    normed, queries, keys, values, log_totals, attn, resid, h_two, probs, combine = attention_forward(
        tokens, norm_attn, w_query, key_projection, value_projection, cosine, sine, w_out, norm_ffn, w_router, routes
    )
    h_two, combine, cot_far = lax.optimization_barrier((h_two, combine, cot_far))
    h_near = (h_two, swap_core(h_two))
    gates_near = (combine, swap_core(combine))
    h_far, gates_far = swap_chip(h_two), swap_chip(combine)
    near = expert_pass(h_near, cot_near, gates_near, w_gate, w_up, w_down)
    near, h_far, gates_far = lax.optimization_barrier((near, h_far, gates_far))
    h_far = (h_far, swap_core(h_far))
    cot_far = (cot_far, swap_core(cot_far))
    gates_far = (gates_far, swap_core(gates_far))
    far = expert_pass(h_far, cot_far, gates_far, w_gate, w_up, w_down)
    ghs, dgs, dus = zip(near[:3], far[:3])
    hs, cots = h_near + h_far, cot_near + cot_far

    router_own, router_near = near[3], swap_core(near[4])
    router_far = swap_chip(far[3] + swap_core(far[4]))
    early = weight_grads(replicas, 0, EARLY, hs, cots, ghs, dgs, dus)
    early, late, (dh_own, dh_near, dh_far), (y_own, y_near, y_far) = overlap(
        early, near[:3], far[:3], w_gate, w_up, w_down, hs, cots, EARLY
    )
    d_resid, d_pre, grad_out = attention_back(
        dh_own, dh_near, dh_far, router_own, router_near, router_far, routes, probs, resid, norm_ffn, cotangent, w_router, w_out, h_two, attn,
        queries, keys, values, log_totals, cosine, sine,
    )
    d_input, grad_qkv = input_back(
        d_pre, normed, tokens, norm_attn, d_resid, w_query, key_projection, value_projection
    )
    mixed = (
        resid + y_own.astype(jnp.float32) + y_near.astype(jnp.float32) + y_far.astype(jnp.float32)
    ).astype(jnp.bfloat16)
    late, sum_o, sum_qkv = ring_sum(late, [grad_out, grad_qkv])
    full_gate, full_up, full_down, sum_o, sum_q, sum_k, sum_v, extra_o, extra_qkv = finish(
        [early, late], [sum_o, sum_qkv], width, key_projection.shape[1]
    )
    sum_r, sum_nf, sum_na = extra_o[:, :experts_all], extra_o[:, LANES], extra_qkv[:, 0]
    return (
        mixed,
        d_input,
        sum_na,
        sum_q,
        sum_k,
        sum_v,
        sum_o,
        sum_nf,
        sum_r,
        full_gate,
        full_up,
        full_down,
    )


def solution(mesh):
    placed = (
        P(("rep", "ep"), None),
        P(),
        P(),
        P(),
        P(),
        P(),
        P(),
        P(),
        P("ep", None, None),
        P("ep", None, None),
        P("ep", None, None),
        P(("rep", "ep"), None),
        P(("rep", "ep"), None),
    )
    return jax.shard_map(
        per_device,
        mesh=mesh,
        in_specs=placed,
        out_specs=(
            P(("rep", "ep"), None),
            P(("rep", "ep"), None),
            P("ep"),
            P("ep", None),
            P("ep", None),
            P("ep", None),
            P("ep", None),
            P("ep"),
            P("ep", None),
            P("ep", None, None),
            P("ep", None, None),
            P("ep", None, None),
        ),
        check_vma=False,
    )
```

```python
import functools
import math

import jax
import jax.numpy as jnp
from jax import lax
from jax.experimental import pallas as pl
from jax.experimental.pallas import tpu as pltpu
from jax.sharding import PartitionSpec as P

QUERY_HEADS = 24
KEY_VALUE_HEADS = 8
HEAD_SIZE = 64
TOPK = 8
SEQUENCE_TOKENS = 512
BLOCK = 256
EARLY = 2


epsilon = 1e-06
masked_value = -1e30


def rope_tables(token_count):
    half = HEAD_SIZE // 2
    places = (jnp.arange(token_count) % SEQUENCE_TOKENS).astype(jnp.float32)
    rates = jnp.exp(jnp.arange(half, dtype=jnp.float32) * (-2.0 * math.log(10000.0) / HEAD_SIZE))
    angles = places[:, None] * rates[None, :]
    cosine, sine = jnp.cos(angles), jnp.sin(angles)
    return (
        jnp.concatenate([cosine] * 4, 1),
        jnp.concatenate([-sine, sine] * 2, 1),
    )


def contract(left, right, left_dim, right_dim):
    return lax.dot_general(
        left, right, (((left_dim,), (right_dim,)), ((), ())), preferred_element_type=jnp.float32
    )


def whole(array):
    return pl.BlockSpec(
        array.shape, lambda *_: (0,) * array.ndim, pipeline_mode=pl.Buffered(1)
    )


def each(array):
    return pl.BlockSpec((1,) + array.shape[1:], lambda e, *_: (e,) + (0,) * (array.ndim - 1))


VMEM_BYTES = 56 * 2**20


def expert_tile(entries, cotangents, gates, mine, w_gate, w_up, w_down):
    gate_pre = contract(entries, w_gate, 1, 0)
    up_pre = contract(entries, w_up, 1, 0)
    back = contract(cotangents, w_down, 1, 1)
    column = jnp.sum(jnp.where(mine, gates, 0.0), 1, keepdims=True)
    sigma = jax.nn.sigmoid(gate_pre)
    swish = gate_pre * sigma
    hidden = (swish * up_pre).astype(jnp.bfloat16).astype(jnp.float32)
    d_hidden = column * back
    return (
        (column * hidden).astype(jnp.bfloat16),
        (d_hidden * up_pre * (sigma * (1.0 + gate_pre * (1.0 - sigma)))).astype(jnp.bfloat16),
        (d_hidden * swish).astype(jnp.bfloat16),
        jnp.sum(hidden * back, 1, keepdims=True),
    )


def expert_kernel(tile, held, h0, h1, c0, c1, gates0, gates1, w_gate, w_up, w_down, gh, dg, du, d_router0, d_router1):
    e = pl.program_id(0)
    tokens, lanes = gates0.shape
    expert = lax.axis_index("ep") * held + e
    lane = lax.broadcasted_iota(jnp.int32, (tile, lanes), 1)

    @pl.when(e == 0)
    def _():
        d_router0[...] = jnp.zeros_like(d_router0)
        d_router1[...] = jnp.zeros_like(d_router1)

    for base, rows_h, rows_c, gates, d_router in (
        (0, h0, c0, gates0, d_router0),
        (tokens, h1, c1, gates1, d_router1),
    ):
        for start in range(0, tokens, tile):
            rows = slice(start, start + tile)
            out = slice(base + start, base + start + tile)
            results = expert_tile(
                rows_h[rows, :], rows_c[rows, :], gates[rows, :], lane == expert, w_gate[0], w_up[0], w_down[0]
            )
            gh[0, out, :], dg[0, out, :], du[0, out, :] = results[:3]
            d_router[rows, :] = jnp.where(lane == expert, results[3], d_router[rows, :])


def expert_pass(many, hs, cots, gates, w_gate, w_up, w_down):
    count, width = hs[0].shape
    tokens = 2 * count
    held, _, hidden_units = w_gate.shape
    part = jax.ShapeDtypeStruct((many, tokens, hidden_units), jnp.bfloat16)
    gate_shape = gates[0].shape
    return pl.pallas_call(
        functools.partial(expert_kernel, 256, held),
        grid=(many,),
        in_specs=[whole(a) for a in (*hs, *cots, *gates)] + [each(a) for a in (w_gate, w_up, w_down)],
        out_specs=[each(part)] * 3 + [pl.BlockSpec(gate_shape, lambda e: (0, 0))] * 2,
        out_shape=[part] * 3 + [jax.ShapeDtypeStruct(gate_shape, jnp.float32)] * 2,
        compiler_params=pltpu.CompilerParams(vmem_limit_bytes=VMEM_BYTES),
        cost_estimate=pl.CostEstimate(
            flops=6 * many * tokens * width * hidden_units,
            bytes_accessed=6 * many * width * hidden_units,
            transcendentals=many * tokens * hidden_units,
        ),
        name="expert_pass",
    )(*hs, *cots, *gates, w_gate, w_up, w_down)


def weight_kernel(*refs):
    hs, cots, passes, unit = refs[:4], refs[4:8], refs[8:14], refs[14]
    kind = pl.program_id(1)

    def put(lefts, rights):
        count = lefts[0].shape[0]
        result = sum(
            contract(lefts[k][...], rights[k // 2][0, (k % 2) * count : (k % 2 + 1) * count], 0, 0)
            for k in range(4)
        ).astype(jnp.bfloat16)
        rows = unit.shape[3]
        for j in range(unit.shape[1]):
            unit[0, j, 0] = result[j * rows : (j + 1) * rows]

    pl.when(kind == 0)(lambda: put(hs, passes[2:4]))
    pl.when(kind == 1)(lambda: put(hs, passes[4:6]))
    pl.when(kind == 2)(lambda: put(cots, passes[:2]))


def weight_grads(count, first, many, hs, cots, ghs, dgs, dus):
    width = hs[0].shape[1]
    _, tokens, hidden_units = dgs[0].shape
    entry = pl.BlockSpec((1, tokens, hidden_units), lambda e, k: (e + first, 0, 0))
    unit = pl.pallas_call(
        weight_kernel,
        grid=(many, 3),
        in_specs=[whole(hs[0])] * 8 + [entry] * 6,
        out_specs=pl.BlockSpec((1, count, 1, width // count, hidden_units), lambda e, k: (e, 0, k, 0, 0)),
        out_shape=jax.ShapeDtypeStruct((many, count, 3, width // count, hidden_units), jnp.bfloat16),
        compiler_params=pltpu.CompilerParams(vmem_limit_bytes=VMEM_BYTES),
        cost_estimate=pl.CostEstimate(
            flops=12 * many * tokens * width * hidden_units,
            bytes_accessed=6 * many * (width + 2 * tokens) * hidden_units,
            transcendentals=0,
        ),
        name="weight_grads",
    )(*hs, *cots, *ghs, *dgs, *dus)
    return unit.reshape(many, count, 3 * (width // count), hidden_units)


def sum_kernel(right_dim, pairs, *refs):
    lefts, rights, outs, total = refs[:pairs], refs[pairs : 2 * pairs], refs[-3:-1], refs[-1]
    e = pl.program_id(0)
    term = sum(contract(left[0], right[0], 1, right_dim) for left, right in zip(lefts, rights))

    @pl.when(e == 0)
    def _():
        total[...] = term

    @pl.when(e > 0)
    def _():
        total[...] += term

    @pl.when(e == pl.num_programs(0) - 1)
    def _():
        for k, out in enumerate(outs):
            count = out.shape[0]
            out[...] = total[k * count : (k + 1) * count].astype(out.dtype)


def sum_over_experts(lefts, rights, right_dim):
    held, tokens, inner = lefts[0].shape
    width = rights[0].shape[2 - right_dim]
    return pl.pallas_call(
        functools.partial(sum_kernel, right_dim, len(lefts)),
        grid=(held,),
        in_specs=[each(a) for a in lefts] + [each(a) for a in rights],
        out_specs=[pl.BlockSpec((tokens // 2, width), lambda e: (0, 0))] * 2,
        out_shape=[jax.ShapeDtypeStruct((tokens // 2, width), jnp.bfloat16)] * 2,
        scratch_shapes=[pltpu.VMEM((tokens, width), jnp.float32)],
        compiler_params=pltpu.CompilerParams(vmem_limit_bytes=VMEM_BYTES),
        cost_estimate=pl.CostEstimate(
            flops=2 * len(lefts) * held * tokens * width * inner,
            bytes_accessed=2 * len(lefts) * held * (tokens + width) * inner,
            transcendentals=0,
        ),
        name="sum_over_experts",
    )(*lefts, *rights)


def rotate(values, cosine, sine, way):
    lane = lax.broadcasted_iota(jnp.int32, cosine.shape, 1)
    first = lane % HEAD_SIZE < HEAD_SIZE // 2
    lanes = cosine.shape[1]
    half = HEAD_SIZE // 2
    pieces = []
    for start in range(0, values.shape[1], lanes):
        piece = values[:, start : start + lanes]
        other = jnp.where(first, pltpu.roll(piece, lanes - half, 1), pltpu.roll(piece, half, 1))
        pieces.append(piece * cosine + way * (other * sine))
    return jnp.concatenate(pieces, 1)


def heads_of(array, group, rows, queries):
    return jnp.concatenate(
        [
            array[rows, (group * queries + j) * HEAD_SIZE : (group * queries + j + 1) * HEAD_SIZE]
            for j in range(queries)
        ],
        0,
    )


IN_VMEM = pl.BlockSpec(memory_space=pltpu.VMEM)
IN_PLACE = pl.BlockSpec(memory_space=pl.ANY)


def moves(semaphores, *pairs):
    return [pltpu.make_async_copy(source, target, semaphores.at[k]) for k, (source, target) in enumerate(pairs)]


def chosen_of(routes, shape):
    expert = lax.broadcasted_iota(jnp.int32, shape, 1)
    picks = routes[...].T
    chosen = picks[:, :1] == expert
    for k in range(1, picks.shape[1]):
        chosen = chosen | (picks[:, k : k + 1] == expert)
    return chosen


def attention_kernel(
    tokens, norm_attn, w_query_in, w_key_in, w_value_in, cosine, sine, w_out_in, norm_ffn, w_router, routes,
    normed_out, queries_out, keys_out, values_out, log_totals, attn_out, resid_out, h_two, probs, combine,
    w_query, w_key, w_value, w_out, normed, queries, keys, values, attn, resid, arrived, left,
):
    count, width = tokens.shape
    weights = moves(
        arrived, (w_query_in, w_query), (w_key_in, w_key), (w_value_in, w_value), (w_out_in, w_out)
    )
    results = moves(
        left, (normed, normed_out), (queries, queries_out), (keys, keys_out), (values, values_out), (attn, attn_out),
        (resid, resid_out),
    )
    for weight in weights:
        weight.start()
    field = tokens[...].astype(jnp.float32)
    inverse = lax.rsqrt(jnp.mean(field * field, -1, keepdims=True) + epsilon)
    first = (field * inverse * norm_attn[...].astype(jnp.float32)).astype(jnp.bfloat16)
    normed[...] = first
    results[0].start()
    for weight in weights[:3]:
        weight.wait()
    queries[...] = rotate(contract(first, w_query[...], 1, 0), cosine[...], sine[...], 1).astype(jnp.bfloat16)
    keys[...] = rotate(contract(first, w_key[...], 1, 0), cosine[...], sine[...], 1).astype(jnp.bfloat16)
    values[...] = contract(first, w_value[...], 1, 0).astype(jnp.bfloat16)
    for result in results[1:4]:
        result.start()
    groups = keys.shape[1] // HEAD_SIZE
    per_group = queries.shape[1] // keys.shape[1]
    lane = lax.broadcasted_iota(jnp.int32, (BLOCK, log_totals.shape[1]), 1)
    for block in range(count // BLOCK):
        rows = slice(block * BLOCK, (block + 1) * BLOCK)
        seen = slice(0, (block + 1) * BLOCK)
        logs = jnp.zeros((BLOCK, log_totals.shape[1]), jnp.float32)
        for group in range(groups):
            cut = slice(group * HEAD_SIZE, (group + 1) * HEAD_SIZE)
            scores = contract(heads_of(queries, group, rows, per_group), keys[seen, cut], 1, 1)
            scores = scores * HEAD_SIZE ** (-0.5)
            highest = jnp.max(scores, -1, keepdims=True)
            shifted = jnp.exp(scores - highest)
            sums = jnp.sum(shifted, -1, keepdims=True)
            probs_bf = (shifted * (1.0 / sums)).astype(jnp.bfloat16)
            mix = contract(probs_bf, values[seen, cut], 1, 0).astype(jnp.bfloat16)
            log_sum = highest + jnp.log(sums)
            for j in range(per_group):
                head = group * per_group + j
                part = slice(j * BLOCK, (j + 1) * BLOCK)
                attn[rows, head * HEAD_SIZE : (head + 1) * HEAD_SIZE] = mix[part]
                logs = jnp.where(lane == head, log_sum[part], logs)
        log_totals[rows, :] = logs
    results[4].start()
    weights[3].wait()
    total = field + contract(attn[...], w_out[...], 1, 0)
    resid[...] = total
    results[5].start()
    inverse = lax.rsqrt(jnp.mean(total * total, -1, keepdims=True) + epsilon)
    second = (total * inverse * norm_ffn[...].astype(jnp.float32)).astype(jnp.bfloat16)
    h_two[...] = second
    logits = contract(second, w_router[...], 1, 1)
    shifted = jnp.exp(logits - jnp.max(logits, -1, keepdims=True))
    soft = shifted / jnp.sum(shifted, -1, keepdims=True)
    probs[...] = soft
    combine[...] = jnp.where(chosen_of(routes, logits.shape), soft, 0.0)
    for result in results:
        result.wait()


LANES = 128


def attention_forward(tokens, norm_attn, w_query, w_key, w_value, cosine, sine, w_out, norm_ffn, w_router, routes):
    count, width = tokens.shape
    experts = w_router.shape[1]
    key_width = w_key.shape[1]
    shape = jax.ShapeDtypeStruct
    return pl.pallas_call(
        attention_kernel,
        out_shape=[
            shape((count, width), jnp.bfloat16),
            shape((count, width), jnp.bfloat16),
            shape((count, key_width), jnp.bfloat16),
            shape((count, key_width), jnp.bfloat16),
            shape((count, LANES), jnp.float32),
            shape((count, width), jnp.bfloat16),
            shape((count, width), jnp.float32),
            shape((count, width), jnp.bfloat16),
            shape((count, experts), jnp.float32),
            shape((count, experts), jnp.float32),
        ],
        in_specs=[IN_VMEM] * 2 + [IN_PLACE] * 3 + [IN_VMEM] * 2 + [IN_PLACE] + [IN_VMEM] * 3,
        out_specs=[IN_PLACE] * 4 + [IN_VMEM] + [IN_PLACE] * 2 + [IN_VMEM] * 3,
        scratch_shapes=[
            pltpu.VMEM(weight.shape, weight.dtype) for weight in (w_query, w_key, w_value, w_out)
        ]
        + [
            pltpu.VMEM((count, width), jnp.bfloat16),
            pltpu.VMEM((count, width), jnp.bfloat16),
            pltpu.VMEM((count, key_width), jnp.bfloat16),
            pltpu.VMEM((count, key_width), jnp.bfloat16),
            pltpu.VMEM((count, width), jnp.bfloat16),
            pltpu.VMEM((count, width), jnp.float32),
            pltpu.SemaphoreType.DMA((4,)),
            pltpu.SemaphoreType.DMA((6,)),
        ],
        compiler_params=pltpu.CompilerParams(vmem_limit_bytes=VMEM_BYTES),
        cost_estimate=pl.CostEstimate(
            flops=6 * count * width * width, bytes_accessed=8 * width * width, transcendentals=24 * count * count
        ),
        name="attention_forward",
    )(
        tokens, norm_attn[None], w_query, w_key, w_value, cosine, sine, w_out, norm_ffn[None], w_router.T, routes.T
    )


def as_lane(row):
    first = lax.broadcasted_iota(jnp.int32, (LANES, row.shape[1]), 0) == 0
    return jnp.where(first, row, 0.0).T.astype(jnp.bfloat16)


def branch_back_kernel(
    dh_own, dh_near, dh_far, router_own, router_near, router_far, routes, probs, resid, norm_ffn, cotangent, w_router, w_out_in, h_two_in, attn_in,
    d_resid_out, grad_out_out, d_attn, w_out, h_two, attn, d_resid, grad_out, d_branch, arrived, left,
):
    count, width = resid.shape
    experts = probs.shape[1]
    inputs = moves(arrived, (w_out_in, w_out), (h_two_in, h_two), (attn_in, attn))
    results = moves(left, (d_resid, d_resid_out), (grad_out, grad_out_out))
    for copy in inputs:
        copy.start()
    soft = probs[...]
    to_router = jnp.where(
        chosen_of(routes, soft.shape), router_own[...] + router_near[...] + router_far[...], 0.0
    )
    d_logits = (soft * (to_router - jnp.sum(soft * to_router, -1, keepdims=True))).astype(jnp.bfloat16)
    d_normed = (
        dh_own[...].astype(jnp.float32)
        + dh_near[...].astype(jnp.float32)
        + dh_far[...].astype(jnp.float32)
        + contract(d_logits, w_router[...], 1, 0)
    )
    total = resid[...]
    inverse = lax.rsqrt(jnp.mean(total * total, -1, keepdims=True) + epsilon)
    normal = total * inverse
    scaled = d_normed * norm_ffn[...].astype(jnp.float32)
    back = cotangent[...].astype(jnp.float32) + inverse * (
        scaled - normal * jnp.mean(scaled * normal, -1, keepdims=True)
    )
    d_resid[...] = back
    results[0].start()
    d_branch[...] = back.astype(jnp.bfloat16)
    for copy in inputs:
        copy.wait()
    grad_out[:, :width] = contract(attn[...], d_branch[...], 0, 0).astype(jnp.bfloat16)
    d_logits = jnp.concatenate([d_logits, jnp.zeros((count, LANES - experts), jnp.bfloat16)], 1)
    grad_out[:, width : width + LANES] = contract(h_two[...], d_logits, 0, 0).astype(jnp.bfloat16)
    grad_out[:, width + LANES :] = as_lane(jnp.sum(d_normed * normal, 0, keepdims=True))
    results[1].start()
    d_attn[...] = contract(d_branch[...], w_out[...], 1, 1).astype(jnp.bfloat16)
    for copy in results:
        copy.wait()


def attention_back_kernel(
    d_attn, queries, keys, values, log_totals, cosine, sine, d_pre, d_queries, d_keys, d_values
):
    count, width = queries.shape
    groups = keys.shape[1] // HEAD_SIZE
    per_group = queries.shape[1] // keys.shape[1]
    factor = HEAD_SIZE ** (-0.5)
    lane = lax.broadcasted_iota(jnp.int32, (BLOCK, log_totals.shape[1]), 1)
    for block in reversed(range(count // BLOCK)):
        rows = slice(block * BLOCK, (block + 1) * BLOCK)
        seen = slice(0, (block + 1) * BLOCK)
        logs = log_totals[rows, :]
        for group in range(groups):
            cut = slice(group * HEAD_SIZE, (group + 1) * HEAD_SIZE)
            part_q = heads_of(queries, group, rows, per_group)
            part_d = heads_of(d_attn, group, rows, per_group)
            log_sum = jnp.concatenate(
                [
                    jnp.sum(jnp.where(lane == group * per_group + j, logs, 0.0), 1, keepdims=True)
                    for j in range(per_group)
                ],
                0,
            )
            part_k, part_v = keys[seen, cut], values[seen, cut]
            probs_f = jnp.exp(contract(part_q, part_k, 1, 1) * factor - log_sum)
            d_probs = contract(part_d, part_v, 1, 1)
            centre = jnp.sum(probs_f * d_probs, -1, keepdims=True)
            d_scores = (probs_f * (d_probs - centre)).astype(jnp.bfloat16)
            turned = contract(d_scores, part_k, 1, 0) * factor
            for j in range(per_group):
                head = group * per_group + j
                d_queries[rows, head * HEAD_SIZE : (head + 1) * HEAD_SIZE] = turned[j * BLOCK : (j + 1) * BLOCK]
            new_k = contract(d_scores, part_q, 0, 0) * factor
            new_v = contract(probs_f.astype(jnp.bfloat16), part_d, 0, 0)
            if block == count // BLOCK - 1:
                d_keys[seen, cut] = new_k
                d_values[seen, cut] = new_v
            else:
                d_keys[seen, cut] += new_k
                d_values[seen, cut] += new_v
    key_width = keys.shape[1]
    d_pre[:, :width] = rotate(d_queries[...], cosine[...], sine[...], -1).astype(jnp.bfloat16)
    d_pre[:, width : width + key_width] = rotate(d_keys[...], cosine[...], sine[...], -1).astype(jnp.bfloat16)
    d_pre[:, width + key_width :] = d_values[...].astype(jnp.bfloat16)


def branch_back(dh_own, dh_near, dh_far, router_own, router_near, router_far, routes, probs, resid, norm_ffn, cotangent,
                w_router, w_out, h_two, attn):
    count, width = resid.shape
    shape = jax.ShapeDtypeStruct
    return pl.pallas_call(
        branch_back_kernel,
        out_shape=[
            shape((count, width), jnp.float32),
            shape((width, width + 2 * LANES), jnp.bfloat16),
            shape((count, width), jnp.bfloat16),
        ],
        in_specs=[IN_VMEM] * 12 + [IN_PLACE] * 3,
        out_specs=[IN_PLACE] * 2 + [IN_VMEM],
        scratch_shapes=[
            pltpu.VMEM(w_out.shape, jnp.bfloat16),
            pltpu.VMEM((count, width), jnp.bfloat16),
            pltpu.VMEM((count, width), jnp.bfloat16),
            pltpu.VMEM((count, width), jnp.float32),
            pltpu.VMEM((width, width + 2 * LANES), jnp.bfloat16),
            pltpu.VMEM((count, width), jnp.bfloat16),
            pltpu.SemaphoreType.DMA((3,)),
            pltpu.SemaphoreType.DMA((2,)),
        ],
        compiler_params=pltpu.CompilerParams(vmem_limit_bytes=VMEM_BYTES),
        cost_estimate=pl.CostEstimate(
            flops=4 * count * width * width, bytes_accessed=8 * width * width, transcendentals=0
        ),
        name="branch_back",
    )(
        dh_own, dh_near, dh_far, router_own, router_near, router_far, routes.T, probs, resid, norm_ffn[None], cotangent,
        w_router.T, w_out, h_two, attn,
    )


def attention_back(d_attn, queries, keys, values, log_totals, cosine, sine):
    count, width = queries.shape
    key_width = keys.shape[1]
    return pl.pallas_call(
        attention_back_kernel,
        out_shape=jax.ShapeDtypeStruct((count, width + 2 * key_width), jnp.bfloat16),
        scratch_shapes=[
            pltpu.VMEM((count, width), jnp.float32),
            pltpu.VMEM((count, key_width), jnp.float32),
            pltpu.VMEM((count, key_width), jnp.float32),
        ],
        compiler_params=pltpu.CompilerParams(vmem_limit_bytes=VMEM_BYTES),
        cost_estimate=pl.CostEstimate(
            flops=8 * count * width * width, bytes_accessed=4 * width * width, transcendentals=24 * count * count
        ),
        name="attention_back",
    )(d_attn, queries, keys, values, log_totals, cosine, sine)


def input_kernel(
    d_pre, normed, tokens_in, norm_attn, d_resid_in, w_query_in, w_key_in, w_value_in, d_input, grads_out,
    tokens, d_resid, w_query, w_key, w_value, grads, arrived, left,
):
    width, key_width = w_query.shape[1], w_key.shape[1]
    inputs = moves(
        arrived, (w_query_in, w_query), (w_key_in, w_key), (w_value_in, w_value), (tokens_in, tokens), (d_resid_in, d_resid)
    )
    for copy in inputs:
        copy.start()
    wide = d_pre.shape[1]
    results = moves(
        left,
        *[
            (grads.at[:, pl.ds(start, key_width)], grads_out.at[:, pl.ds(start, key_width)])
            for start in range(0, wide, key_width)
        ],
        (grads.at[:, pl.ds(wide, 2 * LANES)], grads_out.at[:, pl.ds(wide, 2 * LANES)]),
    )
    for k, start in enumerate(range(0, wide, key_width)):
        cut = slice(start, start + key_width)
        grads[:, cut] = contract(normed[...], d_pre[:, cut], 0, 0).astype(jnp.bfloat16)
        results[k].start()
    for copy in inputs:
        copy.wait()
    d_normed = (
        contract(d_pre[:, :width], w_query[...], 1, 1)
        + contract(d_pre[:, width : width + key_width], w_key[...], 1, 1)
        + contract(d_pre[:, width + key_width :], w_value[...], 1, 1)
    )
    field = tokens[...].astype(jnp.float32)
    inverse = lax.rsqrt(jnp.mean(field * field, -1, keepdims=True) + epsilon)
    normal = field * inverse
    scaled = d_normed * norm_attn[...].astype(jnp.float32)
    grads[:, wide : wide + LANES] = as_lane(jnp.sum(d_normed * normal, 0, keepdims=True))
    grads[:, wide + LANES :] = jnp.zeros((width, LANES), jnp.bfloat16)
    results[-1].start()
    d_input[...] = d_resid[...] + inverse * (scaled - normal * jnp.mean(scaled * normal, -1, keepdims=True))
    for copy in results:
        copy.wait()


def input_back(d_pre, normed, tokens, norm_attn, d_resid, w_query, w_key, w_value):
    count, width = tokens.shape
    shape = jax.ShapeDtypeStruct
    return pl.pallas_call(
        input_kernel,
        out_shape=[
            shape((count, width), jnp.float32),
            shape((width, d_pre.shape[1] + 2 * LANES), jnp.bfloat16),
        ],
        in_specs=[IN_VMEM] * 2 + [IN_PLACE, IN_VMEM] + [IN_PLACE] * 4,
        out_specs=[IN_VMEM, IN_PLACE],
        scratch_shapes=[
            pltpu.VMEM((count, width), jnp.bfloat16),
            pltpu.VMEM((count, width), jnp.float32),
            *[pltpu.VMEM(weight.shape, jnp.bfloat16) for weight in (w_query, w_key, w_value)],
            pltpu.VMEM((width, d_pre.shape[1] + 2 * LANES), jnp.bfloat16),
            pltpu.SemaphoreType.DMA((5,)),
            pltpu.SemaphoreType.DMA((d_pre.shape[1] // w_key.shape[1] + 1,)),
        ],
        compiler_params=pltpu.CompilerParams(vmem_limit_bytes=VMEM_BYTES),
        cost_estimate=pl.CostEstimate(
            flops=8 * count * width * width, bytes_accessed=12 * width * width, transcendentals=0
        ),
        name="input_back",
    )(d_pre, normed, tokens, norm_attn[None], d_resid, w_query, w_key, w_value)


SLOTS = 3


def ring_device(place, count):
    back = place // (count // 2)
    return (1 - back) * 2 * place + back * (2 * (count - 1 - place) + 1)


def ring_place(count):
    here = lax.axis_index("rep")
    odd = here % 2
    rank = here // 2 + odd * (count - 1 - 2 * (here // 2))
    after = ring_device((rank + 1) % count, count)
    before = ring_device((rank + count - 1) % count, count)
    return rank, after, before


def group_places():
    holder = lax.axis_index("ep")
    core = holder + 1 - 2 * (holder % 2)
    return holder, core, (holder + 2) % 4, (core + 2) % 4


def greet(after, before, core, chip):
    barrier = pltpu.get_barrier_semaphore()
    for neighbour in (before, after):
        pl.semaphore_signal(barrier, inc=1, device_id={"rep": neighbour})
    for neighbour in (core, chip):
        pl.semaphore_signal(barrier, inc=1, device_id={"ep": neighbour})
    pl.semaphore_wait(barrier, 4)


def ring_tools(count, shapes, sources, sums, held, terms, semaphores, start=0, initial=()):
    arrived, sent, loaded, stored, credit = semaphores
    rank, after, before = ring_place(count)
    hops = 2 * (count - 1)

    def columns(index, way):
        half = shapes[index][1] // 2
        return pl.ds(way * half, half)

    def send(index, way, hop):
        stream = 2 * index + way
        source = (hop + SLOTS - 1) % SLOTS
        slot = hop % SLOTS
        return pltpu.make_async_remote_copy(
            src_ref=held[index].at[way, source],
            dst_ref=held[index].at[way, slot],
            send_sem=sent.at[stream, slot],
            recv_sem=arrived.at[stream, slot],
            device_id={"rep": before if way else after},
        )

    def load(index, way, hop):
        step = hop + 2
        chunk = (rank + step) % count if way else (rank + 2 * count - step) % count
        return pltpu.make_async_copy(
            sources[index].at[chunk, :, columns(index, way)],
            terms[index].at[way, hop % 2],
            loaded.at[2 * index + way, hop % 2],
        )

    started = initial[0].shape[0] if initial else 0

    def begins(index):
        return start if index < started else 0

    def first(index, way):
        chunk = (rank + 1) % count if way else (rank + count - 1) % count
        source = initial[way].at[index] if index < started else sources[index].at[chunk, :, columns(index, way)]
        slot = (begins(index) + SLOTS - 1) % SLOTS
        return pltpu.make_async_copy(source, held[index].at[way, slot], stored.at[2 * index + way, slot])

    def store(index, way, hop):
        step = hop - (count - 2)
        chunk = (rank + step) % count if way else (rank + count - step) % count
        return pltpu.make_async_copy(
            held[index].at[way, hop % SLOTS],
            sums[index].at[chunk, :, columns(index, way)],
            stored.at[2 * index + way, hop % SLOTS],
        )

    def release(index, way):
        pl.semaphore_signal(
            credit.at[2 * index + way], inc=1, device_id={"rep": after if way else before}
        )

    def begin(streams):
        for index, way in streams:
            first(index, way).start()
        for index, way in streams:
            load(index, way, begins(index)).start()
            load(index, way, begins(index) + 1).start()
        for index, way in streams:
            first(index, way).wait()
            send(index, way, begins(index)).start()

    def take(index, way, hop):
        send(index, way, hop).wait_recv()
        send(index, way, hop).wait_send()

    def pass_on(index, way, hop):
        @pl.when(hop + 1 >= begins(index) + 2)
        def _():
            pl.semaphore_wait(credit.at[2 * index + way], 1)

        send(index, way, hop + 1).start()

    def add_step(streams, hop):
        for index, way in streams:
            take(index, way, hop)

            @pl.when(hop <= hops - 3)
            def _():
                release(index, way)

            load(index, way, hop).wait()
            slot = hop % SLOTS
            held[index][way, slot] = (
                held[index][way, slot].astype(jnp.float32)
                + terms[index][way, hop % 2].astype(jnp.float32)
            ).astype(jnp.bfloat16)
            pass_on(index, way, hop)

            @pl.when(hop + 2 <= count - 2)
            def _():
                load(index, way, hop + 2).start()

            @pl.when(hop == count - 2)
            def _():
                store(index, way, hop).start()

    def hand_step(streams, hop):
        for index, way in streams:
            take(index, way, hop)
            store(index, way, hop - 1).wait()

            @pl.when(hop <= hops - 3)
            def _():
                release(index, way)

            @pl.when(hop + 1 < hops)
            def _():
                pass_on(index, way, hop)

            store(index, way, hop).start()

    def end(streams):
        for index, way in streams:
            store(index, way, hops - 1).wait()

    return begin, add_step, hand_step, end


def both_ways(indices):
    return [(index, way) for index in indices for way in (0, 1)]


def ring_kernel(count, many, lag, start, shapes, *refs):
    dense = len(shapes) - many
    inputs, initial, refs = refs[: 1 + dense], refs[1 + dense : 3 + dense], refs[3 + dense :]
    outputs, rest = refs[: 1 + dense], refs[1 + dense :]
    total = len(shapes)
    held, terms, rest = rest[:total], rest[total : 2 * total], rest[2 * total :]
    own, near, far, joined, rest = (
        rest[:dense], rest[dense : 2 * dense], rest[2 * dense : 3 * dense], rest[3 * dense : 4 * dense], rest[4 * dense :]
    )
    near_sent, near_arrived, own_loaded, far_sent, far_arrived = rest[:5]
    sources = [inputs[0].at[k] for k in range(many)] + list(joined)
    sums = [outputs[0].at[k] for k in range(many)] + list(outputs[1:])
    _, after, before = ring_place(count)
    holder, core, chip, far_core = group_places()
    hops = 2 * (count - 1)
    greet(after, before, core, chip)
    begin, add_step, hand_step, end = ring_tools(
        count, shapes, sources, sums, held, terms, rest[5:], start, initial
    )

    def block(k, index):
        rows = own[k].shape[1]
        return inputs[1 + k].at[pl.ds(pl.multiple_of(index * rows, 8), rows), :]

    def to_core(k, part):
        return pltpu.make_async_remote_copy(
            src_ref=block(k, far_core if part else core),
            dst_ref=near[k].at[part],
            send_sem=near_sent.at[k, part],
            recv_sem=near_arrived.at[k, part],
            device_id={"ep": core},
        )

    def own_block(k, part):
        return pltpu.make_async_copy(
            block(k, chip if part else holder), own[k].at[part], own_loaded.at[k, part]
        )

    def to_chip(k):
        return pltpu.make_async_remote_copy(
            src_ref=own[k].at[1],
            dst_ref=far[k],
            send_sem=far_sent.at[k],
            recv_sem=far_arrived.at[k],
            device_id={"ep": chip},
        )

    pieces = 8

    def send_far():
        for k in range(dense):
            to_core(k, 1).wait_recv()
            own_block(k, 1).wait()
            rows = own[k].shape[1] // pieces
            for j in range(pieces):
                cut = slice(j * rows, (j + 1) * rows)
                own[k][1, cut] = (
                    own[k][1, cut].astype(jnp.float32) + near[k][1, cut].astype(jnp.float32)
                ).astype(jnp.bfloat16)
            to_chip(k).start()

    def join():
        for k in range(dense):
            to_core(k, 0).wait_recv()
            own_block(k, 0).wait()
            to_chip(k).wait_recv()
            to_chip(k).wait_send()
            for part in (0, 1):
                to_core(k, part).wait_send()
            rows = joined[k].shape[1]
            for j in range(count):
                if j * rows < own[k].shape[1]:
                    cut = slice(j * rows, (j + 1) * rows)
                    joined[k][j] = (
                        own[k][0, cut].astype(jnp.float32)
                        + near[k][0, cut].astype(jnp.float32)
                        + far[k][cut].astype(jnp.float32)
                    ).astype(jnp.bfloat16)
                else:
                    joined[k][j] = jnp.zeros(joined[k].shape[1:], jnp.bfloat16)

    early_streams, late_streams = both_ways(range(many)), both_ways(range(many, total))
    for k in range(dense):
        for part in (1, 0):
            to_core(k, part).start()
            own_block(k, part).start()
    begin(early_streams)
    ends = sorted({0, 1, lag, count - 1 - start, hops - start, lag + count - 1, lag + hops})
    for low, high in zip(ends[:-1], ends[1:]):
        if low == 1:
            send_far()
        if low == lag:
            join()
            begin(late_streams)

        def ticks(tick, carry, low=low):
            for streams, zero in ((early_streams, -start), (late_streams, lag)):
                if max(zero, 0) <= low < zero + count - 1:
                    add_step(streams, tick - zero)
                elif zero + count - 1 <= low < zero + hops:
                    hand_step(streams, tick - zero)
            return carry

        lax.fori_loop(low, high, ticks, 0)
    end(early_streams + late_streams)


def ring_sum(late, partials, start, initial):
    many, count = late.shape[:2]
    quarters = [(partial.shape[0] // 4, partial.shape[1]) for partial in partials]
    cuts = [(-(-rows // (8 * count)) * 8, columns) for rows, columns in quarters]
    shapes = [late.shape[2:]] * many + cuts
    total, dense = len(shapes), len(partials)
    halves = [(rows, columns // 2) for rows, columns in shapes]
    size = late.size + sum(partial.size for partial in partials)
    dma = pltpu.SemaphoreType.DMA
    return pl.pallas_call(
        functools.partial(ring_kernel, count, many, 5, start, shapes),
        out_shape=[jax.ShapeDtypeStruct(late.shape, late.dtype)]
        + [jax.ShapeDtypeStruct((count,) + cut, late.dtype) for cut in cuts],
        in_specs=[pl.BlockSpec(memory_space=pl.ANY)] * (3 + dense),
        out_specs=[pl.BlockSpec(memory_space=pl.ANY)] * (1 + dense),
        scratch_shapes=[pltpu.VMEM((2, SLOTS) + half, jnp.bfloat16) for half in halves]
        + [pltpu.VMEM((2, 2) + half, jnp.bfloat16) for half in halves]
        + [pltpu.VMEM((2,) + quarter, jnp.bfloat16) for quarter in quarters]
        + [pltpu.VMEM((2,) + quarter, jnp.bfloat16) for quarter in quarters]
        + [pltpu.VMEM(quarter, jnp.bfloat16) for quarter in quarters]
        + [pltpu.VMEM((count,) + cut, jnp.bfloat16) for cut in cuts]
        + [
            dma((dense, 2)),
            dma((dense, 2)),
            dma((dense, 2)),
            dma((dense,)),
            dma((dense,)),
            dma((2 * total, SLOTS)),
            dma((2 * total, SLOTS)),
            dma((2 * total, 2)),
            dma((2 * total, SLOTS)),
            pltpu.SemaphoreType.REGULAR((2 * total,)),
        ],
        compiler_params=pltpu.CompilerParams(
            collective_id=0, has_side_effects=True, vmem_limit_bytes=VMEM_BYTES
        ),
        cost_estimate=pl.CostEstimate(flops=2 * size, bytes_accessed=8 * size, transcendentals=0),
        name="ring_sum",
    )(late, *partials, *initial)


def chunk_kernel(chunks, forth, back, *refs):
    for term, held, out in zip((forth, back), refs[:-2] or (None, None), refs[-2:]):
        if held is None:
            out[...] = term[:, 0]
        else:
            out[...] = (term[:, 0].astype(jnp.float32) + held[...].astype(jnp.float32)).astype(out.dtype)


def ring_chunks(units, step, held=()):
    many, count, rows, columns = units.shape
    rank, _, _ = ring_place(count)
    chunks = jnp.stack([(rank + count - step) % count, (rank + step) % count])
    half = columns // 2
    block = pl.BlockSpec((many, rows, half), lambda e, chunks: (0, 0, 0))
    return pl.pallas_call(
        chunk_kernel,
        grid_spec=pltpu.PrefetchScalarGridSpec(
            num_scalar_prefetch=1,
            grid=(1,),
            in_specs=[
                pl.BlockSpec((many, 1, rows, half), lambda e, chunks: (0, chunks[0], 0, 0)),
                pl.BlockSpec((many, 1, rows, half), lambda e, chunks: (0, chunks[1], 0, 1)),
            ]
            + [block] * len(held),
            out_specs=[block] * 2,
        ),
        out_shape=[jax.ShapeDtypeStruct((many, rows, half), units.dtype)] * 2,
        compiler_params=pltpu.CompilerParams(vmem_limit_bytes=VMEM_BYTES),
        name="ring_chunks",
    )(chunks, units, units, *held)


def ring_hop(parts, count):
    places = [ring_device(place, count) for place in range(count)]
    pairs = [(places[k], places[(k + 1) % count]) for k in range(count)]
    turned = [(b, a) for a, b in pairs]
    return lax.ppermute(parts[0], "rep", pairs), lax.ppermute(parts[1], "rep", turned)


def overlap_kernel(count, first, shapes, *refs):
    unit, near, far, (w_gate, w_up, w_down), hs, cots = (
        refs[0], refs[1:4], refs[4:7], refs[7:10], refs[10:14], refs[14:18]
    )
    gates, router_so_far, refs = refs[18:20], refs[20:22], refs[22:]
    unit_sum, grads, outs, router_far, rest_far, refs = refs[0], refs[1], refs[2:8], refs[8], refs[9:12], refs[12:]
    many = len(shapes)
    held_slots, terms, refs = refs[:many], refs[many : 2 * many], refs[2 * many :]
    (
        left_a, left_b, right_a, right_b, right_c, total, total_w, stage, stage_w, from_core, from_chip,
        gate_rows, router, router_core, router_chip,
        ready, core_sent, core_arrived, chip_sent, chip_arrived, out_done, grads_done, rows_ready, rest_done,
        router_sent, router_arrived,
    ) = refs[:26]
    held = w_gate.shape[0]
    tokens = hs[0].shape[0]
    _, after, before = ring_place(count)
    holder, core, chip, _ = group_places()
    hops = 2 * (count - 1)
    greet(after, before, core, chip)
    streams = both_ways(range(many))
    begin, add_step, hand_step, end = ring_tools(
        count,
        shapes,
        [unit.at[k] for k in range(many)],
        [unit_sum.at[k] for k in range(many)],
        held_slots,
        terms,
        refs[26:],
    )

    def tick(hop):
        pl.when(hop < count - 1)(lambda: add_step(streams, hop))
        pl.when((hop >= count - 1) & (hop < hops))(lambda: hand_step(streams, hop))

    def copies(bank, *pairs):
        return [pltpu.make_async_copy(source, target, ready.at[bank, k]) for source, target, k in pairs]

    def dh_copies(side, e, place, bank):
        return copies(
            bank,
            (side[1].at[place], left_a.at[bank], 0),
            (side[2].at[place], left_b.at[bank], 1),
            (w_gate.at[e], right_a.at[bank], 2),
            (w_up.at[e], right_b.at[bank], 3),
        )

    def y_copies(side, e, place, bank):
        return copies(bank, (side[0].at[place], left_a.at[bank], 0), (w_down.at[e], right_c.at[bank], 4))

    def load_sum(make, is_far, e, bank):
        if is_far:
            pl.when(e < first)(lambda: begin_all(make(far, e, e, bank)))
            pl.when(e >= first)(lambda: begin_all(make(rest_far, e, e - first, bank)))
        else:
            begin_all(make(near, e, e, bank))

    def load_w(e, kind, part, bank):
        rows = pl.ds((part % 2) * tokens, tokens)
        source = (1, 2, 0)[kind]
        right = rest_far[source].at[e - first, rows, :] if part // 2 else near[source].at[e, rows, :]
        left = (hs, hs, cots)[kind][part]
        return copies(bank, (right, left_a.at[bank, pl.ds(0, tokens), :], 0), (left, right_c.at[bank], 4))

    def load_expert(e, bank):
        return copies(
            bank,
            (w_gate.at[e], right_a.at[bank], 2),
            (w_up.at[e], right_b.at[bank], 3),
            (w_down.at[e], right_c.at[bank], 4),
        )

    def begin_all(made):
        for copy in made:
            copy.start()

    def await_all(made):
        for copy in made:
            copy.wait()

    def to_core(k):
        return pltpu.make_async_remote_copy(
            src_ref=stage.at[k % 2, 1],
            dst_ref=from_core.at[k],
            send_sem=core_sent.at[k],
            recv_sem=core_arrived.at[k],
            device_id={"ep": core},
        )

    def to_chip(k):
        return pltpu.make_async_remote_copy(
            src_ref=stage.at[0, 0],
            dst_ref=from_chip.at[k // 2],
            send_sem=chip_sent.at[k // 2],
            recv_sem=chip_arrived.at[k // 2],
            device_id={"ep": chip},
        )

    def send_chip(k):
        to_core(k).wait_recv()
        stage[0, 0] = (stage[0, 0].astype(jnp.float32) + from_core[k].astype(jnp.float32)).astype(jnp.bfloat16)
        to_chip(k).start()

    def own_out(k):
        return pltpu.make_async_copy(stage.at[1, 0], outs[3 * (k // 2)], out_done.at[3 * (k // 2)])

    def near_out(k):
        return pltpu.make_async_copy(from_core.at[k], outs[3 * (k // 2) + 1], out_done.at[3 * (k // 2) + 1])

    def far_out(k):
        return pltpu.make_async_copy(from_chip.at[k // 2], outs[3 * (k // 2) + 2], out_done.at[3 * (k // 2) + 2])

    far_rows = [
        pltpu.make_async_copy(source, target, rows_ready.at[k])
        for k, (source, target) in enumerate(
            [(hs[2], stage.at[0, 0]), (hs[3], stage.at[0, 1]), (cots[2], stage.at[1, 0]), (cots[3], stage.at[1, 1])]
            + [(gates[part], gate_rows.at[part]) for part in (0, 1)]
            + [(router_so_far[part], router.at[part]) for part in (0, 1)]
        )
    ]
    late = held - first
    tile = tokens // 2
    lane = lax.broadcasted_iota(jnp.int32, (tile, gates[0].shape[1]), 1)

    def rest_out(e, part, kind):
        slot = part % 2
        return pltpu.make_async_copy(
            left_b.at[slot, pl.ds(kind * tile, tile), :],
            rest_far[kind].at[e, pl.ds(part * tile, tile), :],
            rest_done.at[slot, kind],
        )

    begin_all(far_rows)
    begin_all(load_expert(first, 0))
    begin(streams)
    await_all(far_rows)
    hop = 0

    def one_expert(e, carry):
        bank = e % 2
        await_all(load_expert(e + first, bank))

        @pl.when(e + 1 < late)
        def _():
            begin_all(load_expert(e + 1 + first, 1 - bank))

        mine = lane == holder * held + first + e
        for part in range(4):
            block, rows = part // 2, slice((part % 2) * tile, (part % 2 + 1) * tile)
            results = expert_tile(
                stage[0, block, rows], stage[1, block, rows], gate_rows[block, rows], mine,
                right_a[bank], right_b[bank], right_c[bank],
            )
            router[block, rows] = jnp.where(mine, results[3], router[block, rows])
            for kind in range(3):
                if part >= 2:
                    rest_out(e, part, kind).wait()
                else:
                    pl.when(e > 0)(lambda: rest_out(e, part, kind).wait())
                left_b[part % 2, kind * tile : (kind + 1) * tile] = results[kind]
                rest_out(e, part, kind).start()

        @pl.when(e >= 1)
        def _():
            tick(hop + e - 1)

        return carry

    lax.fori_loop(0, late, one_expert, 0)
    hop += late - 1
    for part in (2, 3):
        for kind in range(3):
            rest_out(late - 1, part, kind).wait()

    def router_to_core():
        return pltpu.make_async_remote_copy(
            src_ref=router.at[1],
            dst_ref=router_core,
            send_sem=router_sent.at[0],
            recv_sem=router_arrived.at[0],
            device_id={"ep": core},
        )

    def router_to_chip():
        return pltpu.make_async_remote_copy(
            src_ref=router.at[0],
            dst_ref=router_chip,
            send_sem=router_sent.at[1],
            recv_sem=router_arrived.at[1],
            device_id={"ep": chip},
        )

    router_to_core().start()
    plans = [(dh_copies, True), (dh_copies, False), (y_copies, True), (y_copies, False)]
    load_sum(dh_copies, True, 0, 0)
    for k, (make, is_far) in enumerate(plans):
        base = k * held

        def next_first(bank, k=k):
            if k + 1 < len(plans):
                load_sum(*plans[k + 1], 0, bank)
            else:
                begin_all(load_w(first, 0, 0, bank))

        every = 3 if make is dh_copies else held + 1

        def piece(e, carry, k=k, make=make, is_far=is_far, base=base, hop=hop, every=every, next_first=next_first):
            bank = (base + e) % 2
            await_all(make(near, e, e, bank))

            @pl.when(e + 1 < held)
            def _():
                load_sum(make, is_far, e + 1, 1 - bank)

            @pl.when(e + 1 == held)
            def _():
                next_first(1 - bank)

            if make is dh_copies:
                term = contract(left_a[bank], right_a[bank], 1, 1) + contract(left_b[bank], right_b[bank], 1, 1)
            else:
                term = contract(left_a[bank], right_c[bank], 1, 0)

            @pl.when(e == 0)
            def _():
                total[...] = term

            @pl.when(e > 0)
            def _():
                total[...] += term

            @pl.when((e + 1) % every == 0)
            def _():
                tick(hop + e // every)

            if k % 2 == 1:

                @pl.when(e == 1)
                def _():
                    send_chip(k - 1)
                    if k == 1:
                        router_to_core().wait_recv()
                        router[0] += router_core[...]
                        router_to_chip().start()

            return carry

        lax.fori_loop(0, held, piece, 0)
        hop += held // every
        if k >= 2:
            to_core(k - 2).wait_send()
            if k == 2:
                to_chip(0).wait_send()
            else:
                own_out(1).wait()
        for half in (0, 1):
            stage[k % 2, half] = total[half * tokens : (half + 1) * tokens].astype(jnp.bfloat16)
        to_core(k).start()
        if k % 2 == 1:
            own_out(k).start()
        tick(hop)
        hop += 1

    kinds = 3
    base = len(plans) * held

    def grads_out(e, kind):
        slot = (kinds * e + kind) % 2
        return pltpu.make_async_copy(stage_w.at[slot], grads.at[e, :, kind], grads_done.at[slot])

    def expert(e, carry):
        for kind in range(kinds):
            for part in range(4):
                bank = (base + 4 * kind + part) % 2
                await_all(load_w(e + first, kind, part, bank))
                if part < 3:
                    begin_all(load_w(e + first, kind, part + 1, 1 - bank))
                elif kind < kinds - 1:
                    begin_all(load_w(e + first, kind + 1, 0, 1 - bank))
                else:

                    @pl.when(e + first + 1 < held)
                    def _():
                        begin_all(load_w(e + first + 1, 0, 0, 1 - bank))

                term = contract(right_c[bank], left_a[bank, :tokens], 0, 0)
                if part == 0:
                    total_w[...] = term
                else:
                    total_w[...] += term

            @pl.when(kinds * e + kind >= 2)
            def _():
                grads_out(e, kind).wait()

            slot = (kinds * e + kind) % 2
            rows = stage_w.shape[2]
            for j in range(count):
                stage_w[slot, j] = total_w[j * rows : (j + 1) * rows].astype(jnp.bfloat16)
            grads_out(e, kind).start()
            if kind != 1:
                tick(hop + 2 * e + kind // 2)
        return carry

    lax.fori_loop(0, late, expert, 0)
    hop += 2 * late

    def drain(step, carry):
        tick(step)
        return carry

    lax.fori_loop(hop, max(hop, hops), drain, 0)
    end(streams)
    for k in (1, 3):
        to_core(k).wait_recv()
        near_out(k).start()
    for k in (0, 2):
        to_chip(k).wait_recv()
        far_out(k).start()
    router_to_chip().wait_recv()
    router_out = pltpu.make_async_copy(router_chip, router_far, rows_ready.at[0])
    router_out.start()
    router_to_core().wait_send()
    router_to_chip().wait_send()
    router_out.wait()
    for kind in (kinds - 2, kinds - 1):
        grads_out(late - 1, kind).wait()
    own_out(3).wait()
    to_chip(2).wait_send()
    for k in (2, 3):
        to_core(k).wait_send()
    for k in (1, 3):
        near_out(k).wait()
    for k in (0, 2):
        far_out(k).wait()


def overlap(unit, near, far, w_gate, w_up, w_down, hs, cots, gates, router_so_far, first):
    many, count, rows3, columns = unit.shape
    tokens, width = hs[0].shape
    held = w_gate.shape[0]
    shape, half = (rows3, columns), (rows3, columns // 2)
    block = jax.ShapeDtypeStruct((tokens, width), jnp.bfloat16)
    dma = pltpu.SemaphoreType.DMA

    def buffers(*shape):
        return pltpu.VMEM(shape, jnp.bfloat16)

    flops = 2 * tokens * width * columns * (4 * 3 * held + 12 * (held - first))
    inputs = [unit, *near, *far, w_gate, w_up, w_down, *hs, *cots, *gates, *router_so_far]
    late = held - first
    small = gates[0].shape
    unit_sum, grads, *blocks, router_far, _, _, _ = pl.pallas_call(
        functools.partial(overlap_kernel, count, first, [shape] * many),
        out_shape=[
            jax.ShapeDtypeStruct(unit.shape, unit.dtype),
            jax.ShapeDtypeStruct((held - first, count, 3, rows3 // 3, columns), jnp.bfloat16),
        ]
        + [block] * 6
        + [jax.ShapeDtypeStruct(small, jnp.float32)]
        + [jax.ShapeDtypeStruct((late, 2 * tokens, columns), jnp.bfloat16)] * 3,
        in_specs=[pl.BlockSpec(memory_space=pl.ANY)] * len(inputs),
        out_specs=[pl.BlockSpec(memory_space=pl.ANY)] * 12,
        scratch_shapes=[
            *[buffers(2, SLOTS, *half)] * many,
            *[buffers(2, 2, *half)] * many,
            buffers(2, 2 * tokens, columns),
            buffers(2, 2 * tokens, columns),
            buffers(2, width, columns),
            buffers(2, width, columns),
            buffers(2, columns, width),
            pltpu.VMEM((2 * tokens, width), jnp.float32),
            pltpu.VMEM((width, columns), jnp.float32),
            buffers(2, 2, tokens, width),
            buffers(2, count, rows3 // 3, columns),
            buffers(4, tokens, width),
            buffers(2, tokens, width),
            pltpu.VMEM((2,) + small, jnp.float32),
            pltpu.VMEM((2,) + small, jnp.float32),
            pltpu.VMEM(small, jnp.float32),
            pltpu.VMEM(small, jnp.float32),
            dma((2, 5)),
            dma((4,)),
            dma((4,)),
            dma((2,)),
            dma((2,)),
            dma((6,)),
            dma((2,)),
            dma((8,)),
            dma((2, 3)),
            dma((2,)),
            dma((2,)),
            dma((2 * many, SLOTS)),
            dma((2 * many, SLOTS)),
            dma((2 * many, 2)),
            dma((2 * many, SLOTS)),
            pltpu.SemaphoreType.REGULAR((2 * many,)),
        ],
        compiler_params=pltpu.CompilerParams(
            collective_id=1, has_side_effects=True, vmem_limit_bytes=60 * 2**20
        ),
        cost_estimate=pl.CostEstimate(flops=flops, bytes_accessed=8 * unit.size, transcendentals=0),
        name="overlap",
    )(*inputs)
    grads = grads.reshape(held - first, count, rows3, columns)
    return unit_sum, grads, blocks[:3], blocks[3:], router_far


def finish_kernel(firsts, *refs):
    units, (dense_o, dense_qkv) = refs[: len(firsts) - 1], refs[len(firsts) - 1 : len(firsts) + 1]
    gate, up, down, out, query, key, value, extra_o, extra_qkv = refs[len(firsts) + 1 :]

    @pl.when((pl.program_id(0) == 0) & (pl.program_id(1) == 0))
    def _():
        for dense, parts in ((dense_o, (out, extra_o)), (dense_qkv, (query, key, value, extra_qkv))):
            start = 0
            for part in parts:
                columns = part.shape[1]
                rows = dense.shape[1]
                for j in range(part.shape[0] // rows):
                    part[j * rows : (j + 1) * rows] = dense[j, :, start : start + columns].astype(jnp.float32)
                start += columns

    for index, unit in enumerate(units):
        e = pl.program_id(0)

        @pl.when((e >= firsts[index]) & (e < firsts[index + 1]))
        def _():
            rows = unit.shape[2] // 3
            for k in range(unit.shape[1]):
                gate[0, k * rows : (k + 1) * rows] = unit[0, k, :rows].astype(jnp.float32)
                up[0, k * rows : (k + 1) * rows] = unit[0, k, rows : 2 * rows].astype(jnp.float32)
            turned = jnp.concatenate([unit[0, k, 2 * rows :] for k in range(unit.shape[1])], 0)
            down[0] = turned.astype(jnp.float32).T


def finish(units, dense, width, key_width):
    count, rows3, columns = units[0].shape[1:]
    rows = rows3 // 3
    pair = count // 4
    small = [
        jax.ShapeDtypeStruct((width // 4, part), jnp.float32)
        for part in (width, width, key_width, key_width, 2 * LANES, 2 * LANES)
    ]
    firsts = [0]
    for unit in units:
        firsts.append(firsts[-1] + unit.shape[0])
    experts = firsts[-1]

    def place(index):
        first, end = firsts[index], firsts[index + 1]

        def chunk(e, c):
            inside = jnp.clip(e, first, end - 1)
            return (inside - first, jnp.where(e < first, 0, jnp.where(e >= end, 3, c)), 0, 0)

        return chunk

    return pl.pallas_call(
        functools.partial(finish_kernel, firsts),
        grid=(experts, 4),
        in_specs=[pl.BlockSpec((1, pair, rows3, columns), place(index)) for index in range(len(units))]
        + [whole(part) for part in dense],
        out_specs=[
            pl.BlockSpec((1, pair * rows, columns), lambda e, c: (e, c, 0)),
            pl.BlockSpec((1, pair * rows, columns), lambda e, c: (e, c, 0)),
            pl.BlockSpec((1, columns, pair * rows), lambda e, c: (e, 0, c)),
        ]
        + [whole(part) for part in small],
        out_shape=[
            jax.ShapeDtypeStruct((experts, width, columns), jnp.float32),
            jax.ShapeDtypeStruct((experts, width, columns), jnp.float32),
            jax.ShapeDtypeStruct((experts, columns, width), jnp.float32),
        ]
        + small,
        name="finish",
        compiler_params=pltpu.CompilerParams(vmem_limit_bytes=VMEM_BYTES),
    )(*units, *dense)


def swap_core(value):
    return lax.ppermute(value, "ep", [(0, 1), (1, 0), (2, 3), (3, 2)])


def swap_chip(value):
    return lax.ppermute(value, "ep", [(0, 2), (2, 0), (1, 3), (3, 1)])


def add_bf(a, b):
    return (a.astype(jnp.float32) + b.astype(jnp.float32)).astype(jnp.bfloat16)


def per_device(
    tokens,
    norm_attn,
    w_query,
    key_projection,
    value_projection,
    w_out,
    norm_ffn,
    w_router,
    w_gate,
    w_up,
    w_down,
    routes,
    cotangent,
):
    token_count, width = tokens.shape
    experts_all = w_router.shape[1]
    held = w_gate.shape[0]
    replicas = lax.axis_size("rep")
    cot_near = (cotangent, swap_core(cotangent))
    cot_far = swap_chip(cotangent)
    cosine, sine = rope_tables(token_count)
    normed, queries, keys, values, log_totals, attn, resid, h_two, probs, combine = attention_forward(
        tokens, norm_attn, w_query, key_projection, value_projection, cosine, sine, w_out, norm_ffn, w_router, routes
    )
    h_two, combine, cot_far = lax.optimization_barrier((h_two, combine, cot_far))
    h_near = (h_two, swap_core(h_two))
    gates_near = (combine, swap_core(combine))
    h_far, gates_far = swap_chip(h_two), swap_chip(combine)
    near = expert_pass(held, h_near, cot_near, gates_near, w_gate, w_up, w_down)
    near, h_far, gates_far = lax.optimization_barrier((near, h_far, gates_far))
    h_far = (h_far, swap_core(h_far))
    cot_far = (cot_far, swap_core(cot_far))
    gates_far = (gates_far, swap_core(gates_far))
    far = expert_pass(EARLY, h_far, cot_far, gates_far, w_gate, w_up, w_down)
    ghs, dgs, dus = zip(near[:3], far[:3])
    hs, cots = h_near + h_far, cot_near + cot_far

    router_own, router_near = near[3], swap_core(near[4])
    early = weight_grads(replicas, 0, EARLY, hs, cots, ghs, dgs, dus)
    early, late, (dh_own, dh_near, dh_far), (y_own, y_near, y_far), router_far = overlap(
        early, near[:3], far[:3], w_gate, w_up, w_down, hs, cots, gates_far, far[3:], EARLY
    )
    sent = ring_chunks(late, 1)
    arrived = ring_hop(sent, replicas)
    dh_own, sent = lax.optimization_barrier((dh_own, sent))
    d_resid, grad_out, d_attn = branch_back(
        dh_own, dh_near, dh_far, router_own, router_near, router_far, routes, probs, resid, norm_ffn, cotangent,
        w_router, w_out, h_two, attn,
    )
    arrived, d_attn = lax.optimization_barrier((arrived, d_attn))
    sent = ring_chunks(late, 2, arrived)
    arrived = ring_hop(sent, replicas)
    sent, d_attn = lax.optimization_barrier((sent, d_attn))
    d_pre = attention_back(d_attn, queries, keys, values, log_totals, cosine, sine)
    arrived, d_pre = lax.optimization_barrier((arrived, d_pre))
    sent = ring_chunks(late, 3, arrived)
    arrived = ring_hop(sent, replicas)
    sent, d_pre = lax.optimization_barrier((sent, d_pre))
    d_input, grad_qkv = input_back(
        d_pre, normed, tokens, norm_attn, d_resid, w_query, key_projection, value_projection
    )
    arrived, grad_qkv = lax.optimization_barrier((arrived, grad_qkv))
    initial = ring_chunks(late, 4, arrived)
    mixed = (
        resid + y_own.astype(jnp.float32) + y_near.astype(jnp.float32) + y_far.astype(jnp.float32)
    ).astype(jnp.bfloat16)
    late, sum_o, sum_qkv = ring_sum(late, [grad_out, grad_qkv], 3, initial)
    full_gate, full_up, full_down, sum_o, sum_q, sum_k, sum_v, extra_o, extra_qkv = finish(
        [early, late], [sum_o, sum_qkv], width, key_projection.shape[1]
    )
    sum_r, sum_nf, sum_na = extra_o[:, :experts_all], extra_o[:, LANES], extra_qkv[:, 0]
    return (
        mixed,
        d_input,
        sum_na,
        sum_q,
        sum_k,
        sum_v,
        sum_o,
        sum_nf,
        sum_r,
        full_gate,
        full_up,
        full_down,
    )


def solution(mesh):
    placed = (
        P(("rep", "ep"), None),
        P(),
        P(),
        P(),
        P(),
        P(),
        P(),
        P(),
        P("ep", None, None),
        P("ep", None, None),
        P("ep", None, None),
        P(("rep", "ep"), None),
        P(("rep", "ep"), None),
    )
    return jax.shard_map(
        per_device,
        mesh=mesh,
        in_specs=placed,
        out_specs=(
            P(("rep", "ep"), None),
            P(("rep", "ep"), None),
            P("ep"),
            P("ep", None),
            P("ep", None),
            P("ep", None),
            P("ep", None),
            P("ep"),
            P("ep", None),
            P("ep", None, None),
            P("ep", None, None),
            P("ep", None, None),
        ),
        check_vma=False,
    )
```

```python
import functools
import math

import jax
import jax.numpy as jnp
from jax import lax
from jax.experimental import pallas as pl
from jax.experimental.pallas import tpu as pltpu
from jax.sharding import PartitionSpec as P

QUERY_HEADS = 24
KEY_VALUE_HEADS = 8
HEAD_SIZE = 64
TOPK = 8
SEQUENCE_TOKENS = 512
BLOCK = 256
EARLY = 2


epsilon = 1e-06
masked_value = -1e30


def rope_tables(token_count):
    half = HEAD_SIZE // 2
    places = (jnp.arange(token_count) % SEQUENCE_TOKENS).astype(jnp.float32)
    rates = jnp.exp(jnp.arange(half, dtype=jnp.float32) * (-2.0 * math.log(10000.0) / HEAD_SIZE))
    angles = places[:, None] * rates[None, :]
    cosine, sine = jnp.cos(angles), jnp.sin(angles)
    return (
        jnp.concatenate([cosine] * 4, 1),
        jnp.concatenate([-sine, sine] * 2, 1),
    )


def contract(left, right, left_dim, right_dim):
    return lax.dot_general(
        left, right, (((left_dim,), (right_dim,)), ((), ())), preferred_element_type=jnp.float32
    )


def whole(array):
    return pl.BlockSpec(
        array.shape, lambda *_: (0,) * array.ndim, pipeline_mode=pl.Buffered(1)
    )


def each(array):
    return pl.BlockSpec((1,) + array.shape[1:], lambda e, *_: (e,) + (0,) * (array.ndim - 1))


VMEM_BYTES = 56 * 2**20


def expert_tile(entries, cotangents, gates, mine, w_gate, w_up, w_down):
    gate_pre = contract(entries, w_gate, 1, 0)
    up_pre = contract(entries, w_up, 1, 0)
    back = contract(cotangents, w_down, 1, 1)
    column = jnp.sum(jnp.where(mine, gates, 0.0), 1, keepdims=True)
    sigma = jax.nn.sigmoid(gate_pre)
    swish = gate_pre * sigma
    hidden = (swish * up_pre).astype(jnp.bfloat16).astype(jnp.float32)
    d_hidden = column * back
    return (
        (column * hidden).astype(jnp.bfloat16),
        (d_hidden * up_pre * (sigma * (1.0 + gate_pre * (1.0 - sigma)))).astype(jnp.bfloat16),
        (d_hidden * swish).astype(jnp.bfloat16),
        jnp.sum(hidden * back, 1, keepdims=True),
    )


def expert_kernel(tile, held, h0, h1, c0, c1, gates0, gates1, w_gate, w_up, w_down, gh, dg, du, d_router0, d_router1):
    e = pl.program_id(0)
    tokens, lanes = gates0.shape
    expert = lax.axis_index("ep") * held + e
    lane = lax.broadcasted_iota(jnp.int32, (tile, lanes), 1)

    @pl.when(e == 0)
    def _():
        d_router0[...] = jnp.zeros_like(d_router0)
        d_router1[...] = jnp.zeros_like(d_router1)

    for base, rows_h, rows_c, gates, d_router in (
        (0, h0, c0, gates0, d_router0),
        (tokens, h1, c1, gates1, d_router1),
    ):
        for start in range(0, tokens, tile):
            rows = slice(start, start + tile)
            out = slice(base + start, base + start + tile)
            results = expert_tile(
                rows_h[rows, :], rows_c[rows, :], gates[rows, :], lane == expert, w_gate[0], w_up[0], w_down[0]
            )
            gh[0, out, :], dg[0, out, :], du[0, out, :] = results[:3]
            d_router[rows, :] = jnp.where(lane == expert, results[3], d_router[rows, :])


def expert_pass(many, hs, cots, gates, w_gate, w_up, w_down):
    count, width = hs[0].shape
    tokens = 2 * count
    held, _, hidden_units = w_gate.shape
    part = jax.ShapeDtypeStruct((many, tokens, hidden_units), jnp.bfloat16)
    gate_shape = gates[0].shape
    return pl.pallas_call(
        functools.partial(expert_kernel, 256, held),
        grid=(many,),
        in_specs=[whole(a) for a in (*hs, *cots, *gates)] + [each(a) for a in (w_gate, w_up, w_down)],
        out_specs=[each(part)] * 3 + [pl.BlockSpec(gate_shape, lambda e: (0, 0))] * 2,
        out_shape=[part] * 3 + [jax.ShapeDtypeStruct(gate_shape, jnp.float32)] * 2,
        compiler_params=pltpu.CompilerParams(vmem_limit_bytes=VMEM_BYTES),
        cost_estimate=pl.CostEstimate(
            flops=6 * many * tokens * width * hidden_units,
            bytes_accessed=6 * many * width * hidden_units,
            transcendentals=many * tokens * hidden_units,
        ),
        name="expert_pass",
    )(*hs, *cots, *gates, w_gate, w_up, w_down)


def weight_kernel(*refs):
    hs, cots, passes, unit = refs[:4], refs[4:8], refs[8:14], refs[14]
    kind = pl.program_id(1)

    def put(lefts, rights):
        count = lefts[0].shape[0]
        result = sum(
            contract(lefts[k][...], rights[k // 2][0, (k % 2) * count : (k % 2 + 1) * count], 0, 0)
            for k in range(4)
        ).astype(jnp.bfloat16)
        rows = unit.shape[3]
        for j in range(unit.shape[1]):
            unit[0, j, 0] = result[j * rows : (j + 1) * rows]

    pl.when(kind == 0)(lambda: put(hs, passes[2:4]))
    pl.when(kind == 1)(lambda: put(hs, passes[4:6]))
    pl.when(kind == 2)(lambda: put(cots, passes[:2]))


def weight_grads(count, first, many, hs, cots, ghs, dgs, dus):
    width = hs[0].shape[1]
    _, tokens, hidden_units = dgs[0].shape
    entry = pl.BlockSpec((1, tokens, hidden_units), lambda e, k: (e + first, 0, 0))
    unit = pl.pallas_call(
        weight_kernel,
        grid=(many, 3),
        in_specs=[whole(hs[0])] * 8 + [entry] * 6,
        out_specs=pl.BlockSpec((1, count, 1, width // count, hidden_units), lambda e, k: (e, 0, k, 0, 0)),
        out_shape=jax.ShapeDtypeStruct((many, count, 3, width // count, hidden_units), jnp.bfloat16),
        compiler_params=pltpu.CompilerParams(vmem_limit_bytes=VMEM_BYTES),
        cost_estimate=pl.CostEstimate(
            flops=12 * many * tokens * width * hidden_units,
            bytes_accessed=6 * many * (width + 2 * tokens) * hidden_units,
            transcendentals=0,
        ),
        name="weight_grads",
    )(*hs, *cots, *ghs, *dgs, *dus)
    return unit.reshape(many, count, 3 * (width // count), hidden_units)


def sum_kernel(right_dim, pairs, *refs):
    lefts, rights, outs, total = refs[:pairs], refs[pairs : 2 * pairs], refs[-3:-1], refs[-1]
    e = pl.program_id(0)
    term = sum(contract(left[0], right[0], 1, right_dim) for left, right in zip(lefts, rights))

    @pl.when(e == 0)
    def _():
        total[...] = term

    @pl.when(e > 0)
    def _():
        total[...] += term

    @pl.when(e == pl.num_programs(0) - 1)
    def _():
        for k, out in enumerate(outs):
            count = out.shape[0]
            out[...] = total[k * count : (k + 1) * count].astype(out.dtype)


def sum_over_experts(lefts, rights, right_dim):
    held, tokens, inner = lefts[0].shape
    width = rights[0].shape[2 - right_dim]
    return pl.pallas_call(
        functools.partial(sum_kernel, right_dim, len(lefts)),
        grid=(held,),
        in_specs=[each(a) for a in lefts] + [each(a) for a in rights],
        out_specs=[pl.BlockSpec((tokens // 2, width), lambda e: (0, 0))] * 2,
        out_shape=[jax.ShapeDtypeStruct((tokens // 2, width), jnp.bfloat16)] * 2,
        scratch_shapes=[pltpu.VMEM((tokens, width), jnp.float32)],
        compiler_params=pltpu.CompilerParams(vmem_limit_bytes=VMEM_BYTES),
        cost_estimate=pl.CostEstimate(
            flops=2 * len(lefts) * held * tokens * width * inner,
            bytes_accessed=2 * len(lefts) * held * (tokens + width) * inner,
            transcendentals=0,
        ),
        name="sum_over_experts",
    )(*lefts, *rights)


def rotate(values, cosine, sine, way):
    lane = lax.broadcasted_iota(jnp.int32, cosine.shape, 1)
    first = lane % HEAD_SIZE < HEAD_SIZE // 2
    lanes = cosine.shape[1]
    half = HEAD_SIZE // 2
    pieces = []
    for start in range(0, values.shape[1], lanes):
        piece = values[:, start : start + lanes]
        other = jnp.where(first, pltpu.roll(piece, lanes - half, 1), pltpu.roll(piece, half, 1))
        pieces.append(piece * cosine + way * (other * sine))
    return jnp.concatenate(pieces, 1)


def heads_of(array, group, rows, queries):
    return jnp.concatenate(
        [
            array[rows, (group * queries + j) * HEAD_SIZE : (group * queries + j + 1) * HEAD_SIZE]
            for j in range(queries)
        ],
        0,
    )


IN_VMEM = pl.BlockSpec(memory_space=pltpu.VMEM)
IN_PLACE = pl.BlockSpec(memory_space=pl.ANY)


def moves(semaphores, *pairs):
    return [pltpu.make_async_copy(source, target, semaphores.at[k]) for k, (source, target) in enumerate(pairs)]


def chosen_of(routes, shape):
    expert = lax.broadcasted_iota(jnp.int32, shape, 1)
    picks = routes[...].T
    chosen = picks[:, :1] == expert
    for k in range(1, picks.shape[1]):
        chosen = chosen | (picks[:, k : k + 1] == expert)
    return chosen


def attention_kernel(
    tokens, norm_attn, w_query_in, w_key_in, w_value_in, cosine, sine, w_out_in, norm_ffn, w_router, routes,
    normed_out, queries_out, keys_out, values_out, log_totals, attn_out, resid_out, h_two, probs, combine,
    w_query, w_key, w_value, w_out, normed, queries, keys, values, attn, resid, arrived, left,
):
    count, width = tokens.shape
    weights = moves(
        arrived, (w_query_in, w_query), (w_key_in, w_key), (w_value_in, w_value), (w_out_in, w_out)
    )
    results = moves(
        left, (normed, normed_out), (queries, queries_out), (keys, keys_out), (values, values_out), (attn, attn_out),
        (resid, resid_out),
    )
    for weight in weights:
        weight.start()
    field = tokens[...].astype(jnp.float32)
    inverse = lax.rsqrt(jnp.mean(field * field, -1, keepdims=True) + epsilon)
    first = (field * inverse * norm_attn[...].astype(jnp.float32)).astype(jnp.bfloat16)
    normed[...] = first
    results[0].start()
    for weight in weights[:3]:
        weight.wait()
    queries[...] = rotate(contract(first, w_query[...], 1, 0), cosine[...], sine[...], 1).astype(jnp.bfloat16)
    keys[...] = rotate(contract(first, w_key[...], 1, 0), cosine[...], sine[...], 1).astype(jnp.bfloat16)
    values[...] = contract(first, w_value[...], 1, 0).astype(jnp.bfloat16)
    for result in results[1:4]:
        result.start()
    groups = keys.shape[1] // HEAD_SIZE
    per_group = queries.shape[1] // keys.shape[1]
    lane = lax.broadcasted_iota(jnp.int32, (BLOCK, log_totals.shape[1]), 1)
    for block in range(count // BLOCK):
        rows = slice(block * BLOCK, (block + 1) * BLOCK)
        seen = slice(0, (block + 1) * BLOCK)
        logs = jnp.zeros((BLOCK, log_totals.shape[1]), jnp.float32)
        for group in range(groups):
            cut = slice(group * HEAD_SIZE, (group + 1) * HEAD_SIZE)
            scores = contract(heads_of(queries, group, rows, per_group), keys[seen, cut], 1, 1)
            scores = scores * HEAD_SIZE ** (-0.5)
            highest = jnp.max(scores, -1, keepdims=True)
            shifted = jnp.exp(scores - highest)
            sums = jnp.sum(shifted, -1, keepdims=True)
            probs_bf = (shifted * (1.0 / sums)).astype(jnp.bfloat16)
            mix = contract(probs_bf, values[seen, cut], 1, 0).astype(jnp.bfloat16)
            log_sum = highest + jnp.log(sums)
            for j in range(per_group):
                head = group * per_group + j
                part = slice(j * BLOCK, (j + 1) * BLOCK)
                attn[rows, head * HEAD_SIZE : (head + 1) * HEAD_SIZE] = mix[part]
                logs = jnp.where(lane == head, log_sum[part], logs)
        log_totals[rows, :] = logs
    results[4].start()
    weights[3].wait()
    total = field + contract(attn[...], w_out[...], 1, 0)
    resid[...] = total
    results[5].start()
    inverse = lax.rsqrt(jnp.mean(total * total, -1, keepdims=True) + epsilon)
    second = (total * inverse * norm_ffn[...].astype(jnp.float32)).astype(jnp.bfloat16)
    h_two[...] = second
    logits = contract(second, w_router[...], 1, 1)
    shifted = jnp.exp(logits - jnp.max(logits, -1, keepdims=True))
    soft = shifted / jnp.sum(shifted, -1, keepdims=True)
    probs[...] = soft
    combine[...] = jnp.where(chosen_of(routes, logits.shape), soft, 0.0)
    for result in results:
        result.wait()


LANES = 128


def attention_forward(tokens, norm_attn, w_query, w_key, w_value, cosine, sine, w_out, norm_ffn, w_router, routes):
    count, width = tokens.shape
    experts = w_router.shape[1]
    key_width = w_key.shape[1]
    shape = jax.ShapeDtypeStruct
    return pl.pallas_call(
        attention_kernel,
        out_shape=[
            shape((count, width), jnp.bfloat16),
            shape((count, width), jnp.bfloat16),
            shape((count, key_width), jnp.bfloat16),
            shape((count, key_width), jnp.bfloat16),
            shape((count, LANES), jnp.float32),
            shape((count, width), jnp.bfloat16),
            shape((count, width), jnp.float32),
            shape((count, width), jnp.bfloat16),
            shape((count, experts), jnp.float32),
            shape((count, experts), jnp.float32),
        ],
        in_specs=[IN_VMEM] * 2 + [IN_PLACE] * 3 + [IN_VMEM] * 2 + [IN_PLACE] + [IN_VMEM] * 3,
        out_specs=[IN_PLACE] * 4 + [IN_VMEM] + [IN_PLACE] * 2 + [IN_VMEM] * 3,
        scratch_shapes=[
            pltpu.VMEM(weight.shape, weight.dtype) for weight in (w_query, w_key, w_value, w_out)
        ]
        + [
            pltpu.VMEM((count, width), jnp.bfloat16),
            pltpu.VMEM((count, width), jnp.bfloat16),
            pltpu.VMEM((count, key_width), jnp.bfloat16),
            pltpu.VMEM((count, key_width), jnp.bfloat16),
            pltpu.VMEM((count, width), jnp.bfloat16),
            pltpu.VMEM((count, width), jnp.float32),
            pltpu.SemaphoreType.DMA((4,)),
            pltpu.SemaphoreType.DMA((6,)),
        ],
        compiler_params=pltpu.CompilerParams(vmem_limit_bytes=VMEM_BYTES),
        cost_estimate=pl.CostEstimate(
            flops=6 * count * width * width, bytes_accessed=8 * width * width, transcendentals=24 * count * count
        ),
        name="attention_forward",
    )(
        tokens, norm_attn[None], w_query, w_key, w_value, cosine, sine, w_out, norm_ffn[None], w_router.T, routes.T
    )


def as_lane(row):
    first = lax.broadcasted_iota(jnp.int32, (LANES, row.shape[1]), 0) == 0
    return jnp.where(first, row, 0.0).T.astype(jnp.bfloat16)


def branch_back_kernel(
    dh_own, dh_near, dh_far, router_own, router_near, router_far, routes, probs, resid, norm_ffn, cotangent, w_router, w_out_in, h_two_in, attn_in,
    d_resid_out, grad_out_out, d_attn, w_out, h_two, attn, d_resid, grad_out, d_branch, arrived, left,
):
    count, width = resid.shape
    experts = probs.shape[1]
    inputs = moves(arrived, (w_out_in, w_out), (h_two_in, h_two), (attn_in, attn))
    results = moves(left, (d_resid, d_resid_out), (grad_out, grad_out_out))
    for copy in inputs:
        copy.start()
    soft = probs[...]
    to_router = jnp.where(
        chosen_of(routes, soft.shape), router_own[...] + router_near[...] + router_far[...], 0.0
    )
    d_logits = (soft * (to_router - jnp.sum(soft * to_router, -1, keepdims=True))).astype(jnp.bfloat16)
    d_normed = (
        dh_own[...].astype(jnp.float32)
        + dh_near[...].astype(jnp.float32)
        + dh_far[...].astype(jnp.float32)
        + contract(d_logits, w_router[...], 1, 0)
    )
    total = resid[...]
    inverse = lax.rsqrt(jnp.mean(total * total, -1, keepdims=True) + epsilon)
    normal = total * inverse
    scaled = d_normed * norm_ffn[...].astype(jnp.float32)
    back = cotangent[...].astype(jnp.float32) + inverse * (
        scaled - normal * jnp.mean(scaled * normal, -1, keepdims=True)
    )
    d_resid[...] = back
    results[0].start()
    d_branch[...] = back.astype(jnp.bfloat16)
    for copy in inputs:
        copy.wait()
    grad_out[:, :width] = contract(attn[...], d_branch[...], 0, 0).astype(jnp.bfloat16)
    d_logits = jnp.concatenate([d_logits, jnp.zeros((count, LANES - experts), jnp.bfloat16)], 1)
    grad_out[:, width : width + LANES] = contract(h_two[...], d_logits, 0, 0).astype(jnp.bfloat16)
    grad_out[:, width + LANES :] = as_lane(jnp.sum(d_normed * normal, 0, keepdims=True))
    results[1].start()
    d_attn[...] = contract(d_branch[...], w_out[...], 1, 1).astype(jnp.bfloat16)
    for copy in results:
        copy.wait()


def attention_back_kernel(
    d_attn, queries, keys, values, log_totals, cosine, sine, d_pre, d_queries, d_keys, d_values
):
    count, width = queries.shape
    groups = keys.shape[1] // HEAD_SIZE
    per_group = queries.shape[1] // keys.shape[1]
    factor = HEAD_SIZE ** (-0.5)
    lane = lax.broadcasted_iota(jnp.int32, (BLOCK, log_totals.shape[1]), 1)
    for block in reversed(range(count // BLOCK)):
        rows = slice(block * BLOCK, (block + 1) * BLOCK)
        seen = slice(0, (block + 1) * BLOCK)
        logs = log_totals[rows, :]
        for group in range(groups):
            cut = slice(group * HEAD_SIZE, (group + 1) * HEAD_SIZE)
            part_q = heads_of(queries, group, rows, per_group)
            part_d = heads_of(d_attn, group, rows, per_group)
            log_sum = jnp.concatenate(
                [
                    jnp.sum(jnp.where(lane == group * per_group + j, logs, 0.0), 1, keepdims=True)
                    for j in range(per_group)
                ],
                0,
            )
            part_k, part_v = keys[seen, cut], values[seen, cut]
            probs_f = jnp.exp(contract(part_q, part_k, 1, 1) * factor - log_sum)
            d_probs = contract(part_d, part_v, 1, 1)
            centre = jnp.sum(probs_f * d_probs, -1, keepdims=True)
            d_scores = (probs_f * (d_probs - centre)).astype(jnp.bfloat16)
            turned = contract(d_scores, part_k, 1, 0) * factor
            for j in range(per_group):
                head = group * per_group + j
                d_queries[rows, head * HEAD_SIZE : (head + 1) * HEAD_SIZE] = turned[j * BLOCK : (j + 1) * BLOCK]
            new_k = contract(d_scores, part_q, 0, 0) * factor
            new_v = contract(probs_f.astype(jnp.bfloat16), part_d, 0, 0)
            if block == count // BLOCK - 1:
                d_keys[seen, cut] = new_k
                d_values[seen, cut] = new_v
            else:
                d_keys[seen, cut] += new_k
                d_values[seen, cut] += new_v
    key_width = keys.shape[1]
    d_pre[:, :width] = rotate(d_queries[...], cosine[...], sine[...], -1).astype(jnp.bfloat16)
    d_pre[:, width : width + key_width] = rotate(d_keys[...], cosine[...], sine[...], -1).astype(jnp.bfloat16)
    d_pre[:, width + key_width :] = d_values[...].astype(jnp.bfloat16)


def branch_back(dh_own, dh_near, dh_far, router_own, router_near, router_far, routes, probs, resid, norm_ffn, cotangent,
                w_router, w_out, h_two, attn):
    count, width = resid.shape
    shape = jax.ShapeDtypeStruct
    return pl.pallas_call(
        branch_back_kernel,
        out_shape=[
            shape((count, width), jnp.float32),
            shape((width, width + 2 * LANES), jnp.bfloat16),
            shape((count, width), jnp.bfloat16),
        ],
        in_specs=[IN_VMEM] * 12 + [IN_PLACE] * 3,
        out_specs=[IN_PLACE] * 2 + [IN_VMEM],
        scratch_shapes=[
            pltpu.VMEM(w_out.shape, jnp.bfloat16),
            pltpu.VMEM((count, width), jnp.bfloat16),
            pltpu.VMEM((count, width), jnp.bfloat16),
            pltpu.VMEM((count, width), jnp.float32),
            pltpu.VMEM((width, width + 2 * LANES), jnp.bfloat16),
            pltpu.VMEM((count, width), jnp.bfloat16),
            pltpu.SemaphoreType.DMA((3,)),
            pltpu.SemaphoreType.DMA((2,)),
        ],
        compiler_params=pltpu.CompilerParams(vmem_limit_bytes=VMEM_BYTES),
        cost_estimate=pl.CostEstimate(
            flops=4 * count * width * width, bytes_accessed=8 * width * width, transcendentals=0
        ),
        name="branch_back",
    )(
        dh_own, dh_near, dh_far, router_own, router_near, router_far, routes.T, probs, resid, norm_ffn[None], cotangent,
        w_router.T, w_out, h_two, attn,
    )


def attention_back(d_attn, queries, keys, values, log_totals, cosine, sine):
    count, width = queries.shape
    key_width = keys.shape[1]
    return pl.pallas_call(
        attention_back_kernel,
        out_shape=jax.ShapeDtypeStruct((count, width + 2 * key_width), jnp.bfloat16),
        scratch_shapes=[
            pltpu.VMEM((count, width), jnp.float32),
            pltpu.VMEM((count, key_width), jnp.float32),
            pltpu.VMEM((count, key_width), jnp.float32),
        ],
        compiler_params=pltpu.CompilerParams(vmem_limit_bytes=VMEM_BYTES),
        cost_estimate=pl.CostEstimate(
            flops=8 * count * width * width, bytes_accessed=4 * width * width, transcendentals=24 * count * count
        ),
        name="attention_back",
    )(d_attn, queries, keys, values, log_totals, cosine, sine)


def input_kernel(
    d_pre, normed, tokens_in, norm_attn, d_resid_in, w_query_in, w_key_in, w_value_in, d_input, grads_out,
    tokens, d_resid, w_query, w_key, w_value, grads, arrived, left,
):
    width, key_width = w_query.shape[1], w_key.shape[1]
    inputs = moves(
        arrived, (w_query_in, w_query), (w_key_in, w_key), (w_value_in, w_value), (tokens_in, tokens), (d_resid_in, d_resid)
    )
    for copy in inputs:
        copy.start()
    wide = d_pre.shape[1]
    results = moves(
        left,
        *[
            (grads.at[:, pl.ds(start, key_width)], grads_out.at[:, pl.ds(start, key_width)])
            for start in range(0, wide, key_width)
        ],
        (grads.at[:, pl.ds(wide, 2 * LANES)], grads_out.at[:, pl.ds(wide, 2 * LANES)]),
    )
    for k, start in enumerate(range(0, wide, key_width)):
        cut = slice(start, start + key_width)
        grads[:, cut] = contract(normed[...], d_pre[:, cut], 0, 0).astype(jnp.bfloat16)
        results[k].start()
    for copy in inputs:
        copy.wait()
    d_normed = (
        contract(d_pre[:, :width], w_query[...], 1, 1)
        + contract(d_pre[:, width : width + key_width], w_key[...], 1, 1)
        + contract(d_pre[:, width + key_width :], w_value[...], 1, 1)
    )
    field = tokens[...].astype(jnp.float32)
    inverse = lax.rsqrt(jnp.mean(field * field, -1, keepdims=True) + epsilon)
    normal = field * inverse
    scaled = d_normed * norm_attn[...].astype(jnp.float32)
    grads[:, wide : wide + LANES] = as_lane(jnp.sum(d_normed * normal, 0, keepdims=True))
    grads[:, wide + LANES :] = jnp.zeros((width, LANES), jnp.bfloat16)
    results[-1].start()
    d_input[...] = d_resid[...] + inverse * (scaled - normal * jnp.mean(scaled * normal, -1, keepdims=True))
    for copy in results:
        copy.wait()


def input_back(d_pre, normed, tokens, norm_attn, d_resid, w_query, w_key, w_value):
    count, width = tokens.shape
    shape = jax.ShapeDtypeStruct
    return pl.pallas_call(
        input_kernel,
        out_shape=[
            shape((count, width), jnp.float32),
            shape((width, d_pre.shape[1] + 2 * LANES), jnp.bfloat16),
        ],
        in_specs=[IN_VMEM] * 2 + [IN_PLACE, IN_VMEM] + [IN_PLACE] * 4,
        out_specs=[IN_VMEM, IN_PLACE],
        scratch_shapes=[
            pltpu.VMEM((count, width), jnp.bfloat16),
            pltpu.VMEM((count, width), jnp.float32),
            *[pltpu.VMEM(weight.shape, jnp.bfloat16) for weight in (w_query, w_key, w_value)],
            pltpu.VMEM((width, d_pre.shape[1] + 2 * LANES), jnp.bfloat16),
            pltpu.SemaphoreType.DMA((5,)),
            pltpu.SemaphoreType.DMA((d_pre.shape[1] // w_key.shape[1] + 1,)),
        ],
        compiler_params=pltpu.CompilerParams(vmem_limit_bytes=VMEM_BYTES),
        cost_estimate=pl.CostEstimate(
            flops=8 * count * width * width, bytes_accessed=12 * width * width, transcendentals=0
        ),
        name="input_back",
    )(d_pre, normed, tokens, norm_attn[None], d_resid, w_query, w_key, w_value)


SLOTS = 3


def ring_device(place, count):
    back = place // (count // 2)
    return (1 - back) * 2 * place + back * (2 * (count - 1 - place) + 1)


def ring_place(count):
    here = lax.axis_index("rep")
    odd = here % 2
    rank = here // 2 + odd * (count - 1 - 2 * (here // 2))
    after = ring_device((rank + 1) % count, count)
    before = ring_device((rank + count - 1) % count, count)
    return rank, after, before


def group_places():
    holder = lax.axis_index("ep")
    core = holder + 1 - 2 * (holder % 2)
    return holder, core, (holder + 2) % 4, (core + 2) % 4


def greet(after, before, core, chip):
    barrier = pltpu.get_barrier_semaphore()
    for neighbour in (before, after):
        pl.semaphore_signal(barrier, inc=1, device_id={"rep": neighbour})
    for neighbour in (core, chip):
        pl.semaphore_signal(barrier, inc=1, device_id={"ep": neighbour})
    pl.semaphore_wait(barrier, 4)


def ring_tools(count, shapes, sources, sums, held, terms, semaphores, start=0, initial=()):
    arrived, sent, loaded, stored, credit = semaphores
    rank, after, before = ring_place(count)
    hops = 2 * (count - 1)

    def columns(index, way):
        half = shapes[index][1] // 2
        return pl.ds(way * half, half)

    def send(index, way, hop):
        stream = 2 * index + way
        source = (hop + SLOTS - 1) % SLOTS
        slot = hop % SLOTS
        return pltpu.make_async_remote_copy(
            src_ref=held[index].at[way, source],
            dst_ref=held[index].at[way, slot],
            send_sem=sent.at[stream, slot],
            recv_sem=arrived.at[stream, slot],
            device_id={"rep": before if way else after},
        )

    def load(index, way, hop):
        step = hop + 2
        chunk = (rank + step) % count if way else (rank + 2 * count - step) % count
        return pltpu.make_async_copy(
            sources[index].at[chunk, :, columns(index, way)],
            terms[index].at[way, hop % 2],
            loaded.at[2 * index + way, hop % 2],
        )

    started = initial[0].shape[0] if initial else 0

    def begins(index):
        return start if index < started else 0

    def first(index, way):
        chunk = (rank + 1) % count if way else (rank + count - 1) % count
        source = initial[way].at[index] if index < started else sources[index].at[chunk, :, columns(index, way)]
        slot = (begins(index) + SLOTS - 1) % SLOTS
        return pltpu.make_async_copy(source, held[index].at[way, slot], stored.at[2 * index + way, slot])

    def store(index, way, hop):
        step = hop - (count - 2)
        chunk = (rank + step) % count if way else (rank + count - step) % count
        return pltpu.make_async_copy(
            held[index].at[way, hop % SLOTS],
            sums[index].at[chunk, :, columns(index, way)],
            stored.at[2 * index + way, hop % SLOTS],
        )

    def release(index, way):
        pl.semaphore_signal(
            credit.at[2 * index + way], inc=1, device_id={"rep": after if way else before}
        )

    def begin(streams):
        for index, way in streams:
            first(index, way).start()
        for index, way in streams:
            load(index, way, begins(index)).start()
            load(index, way, begins(index) + 1).start()
        for index, way in streams:
            first(index, way).wait()
            send(index, way, begins(index)).start()

    def take(index, way, hop):
        send(index, way, hop).wait_recv()
        send(index, way, hop).wait_send()

    def pass_on(index, way, hop):
        @pl.when(hop + 1 >= begins(index) + 2)
        def _():
            pl.semaphore_wait(credit.at[2 * index + way], 1)

        send(index, way, hop + 1).start()

    def add_step(streams, hop):
        for index, way in streams:
            take(index, way, hop)

            @pl.when(hop <= hops - 3)
            def _():
                release(index, way)

            load(index, way, hop).wait()
            slot = hop % SLOTS
            held[index][way, slot] = (
                held[index][way, slot].astype(jnp.float32)
                + terms[index][way, hop % 2].astype(jnp.float32)
            ).astype(jnp.bfloat16)
            pass_on(index, way, hop)

            @pl.when(hop + 2 <= count - 2)
            def _():
                load(index, way, hop + 2).start()

            @pl.when(hop == count - 2)
            def _():
                store(index, way, hop).start()

    def hand_step(streams, hop):
        for index, way in streams:
            take(index, way, hop)
            store(index, way, hop - 1).wait()

            @pl.when(hop <= hops - 3)
            def _():
                release(index, way)

            @pl.when(hop + 1 < hops)
            def _():
                pass_on(index, way, hop)

            store(index, way, hop).start()

    def end(streams):
        for index, way in streams:
            store(index, way, hops - 1).wait()

    return begin, add_step, hand_step, end


def both_ways(indices):
    return [(index, way) for index in indices for way in (0, 1)]


def ring_kernel(count, many, lag, start, shapes, *refs):
    dense = len(shapes) - many
    inputs, initial, refs = refs[: 1 + dense], refs[1 + dense : 3 + dense], refs[3 + dense :]
    outputs, rest = refs[: 1 + dense], refs[1 + dense :]
    total = len(shapes)
    held, terms, rest = rest[:total], rest[total : 2 * total], rest[2 * total :]
    own, near, far, joined, rest = (
        rest[:dense], rest[dense : 2 * dense], rest[2 * dense : 3 * dense], rest[3 * dense : 4 * dense], rest[4 * dense :]
    )
    near_sent, near_arrived, own_loaded, far_sent, far_arrived = rest[:5]
    sources = [inputs[0].at[k] for k in range(many)] + list(joined)
    sums = [outputs[0].at[k] for k in range(many)] + list(outputs[1:])
    _, after, before = ring_place(count)
    holder, core, chip, far_core = group_places()
    hops = 2 * (count - 1)
    greet(after, before, core, chip)
    begin, add_step, hand_step, end = ring_tools(
        count, shapes, sources, sums, held, terms, rest[5:], start, initial
    )

    def block(k, index):
        rows = own[k].shape[1]
        return inputs[1 + k].at[pl.ds(pl.multiple_of(index * rows, 8), rows), :]

    def to_core(k, part):
        return pltpu.make_async_remote_copy(
            src_ref=block(k, far_core if part else core),
            dst_ref=near[k].at[part],
            send_sem=near_sent.at[k, part],
            recv_sem=near_arrived.at[k, part],
            device_id={"ep": core},
        )

    def own_block(k, part):
        return pltpu.make_async_copy(
            block(k, chip if part else holder), own[k].at[part], own_loaded.at[k, part]
        )

    def to_chip(k):
        return pltpu.make_async_remote_copy(
            src_ref=own[k].at[1],
            dst_ref=far[k],
            send_sem=far_sent.at[k],
            recv_sem=far_arrived.at[k],
            device_id={"ep": chip},
        )

    pieces = 8

    def send_far():
        for k in range(dense):
            to_core(k, 1).wait_recv()
            own_block(k, 1).wait()
            rows = own[k].shape[1] // pieces
            for j in range(pieces):
                cut = slice(j * rows, (j + 1) * rows)
                own[k][1, cut] = (
                    own[k][1, cut].astype(jnp.float32) + near[k][1, cut].astype(jnp.float32)
                ).astype(jnp.bfloat16)
            to_chip(k).start()

    def join():
        for k in range(dense):
            to_core(k, 0).wait_recv()
            own_block(k, 0).wait()
            to_chip(k).wait_recv()
            to_chip(k).wait_send()
            for part in (0, 1):
                to_core(k, part).wait_send()
            rows = joined[k].shape[1]
            for j in range(count):
                if j * rows < own[k].shape[1]:
                    cut = slice(j * rows, (j + 1) * rows)
                    joined[k][j] = (
                        own[k][0, cut].astype(jnp.float32)
                        + near[k][0, cut].astype(jnp.float32)
                        + far[k][cut].astype(jnp.float32)
                    ).astype(jnp.bfloat16)
                else:
                    joined[k][j] = jnp.zeros(joined[k].shape[1:], jnp.bfloat16)

    early_streams, late_streams = both_ways(range(many)), both_ways(range(many, total))
    for k in range(dense):
        for part in (1, 0):
            to_core(k, part).start()
            own_block(k, part).start()
    begin(early_streams)
    ends = sorted({0, 1, lag, count - 1 - start, hops - start, lag + count - 1, lag + hops})
    for low, high in zip(ends[:-1], ends[1:]):
        if low == 1:
            send_far()
        if low == lag:
            join()
            begin(late_streams)

        def ticks(tick, carry, low=low):
            for streams, zero in ((early_streams, -start), (late_streams, lag)):
                if max(zero, 0) <= low < zero + count - 1:
                    add_step(streams, tick - zero)
                elif zero + count - 1 <= low < zero + hops:
                    hand_step(streams, tick - zero)
            return carry

        lax.fori_loop(low, high, ticks, 0)
    end(early_streams + late_streams)


def ring_sum(late, partials, start, initial):
    many, count = late.shape[:2]
    quarters = [(partial.shape[0] // 4, partial.shape[1]) for partial in partials]
    cuts = [(-(-rows // (8 * count)) * 8, columns) for rows, columns in quarters]
    shapes = [late.shape[2:]] * many + cuts
    total, dense = len(shapes), len(partials)
    halves = [(rows, columns // 2) for rows, columns in shapes]
    size = late.size + sum(partial.size for partial in partials)
    dma = pltpu.SemaphoreType.DMA
    return pl.pallas_call(
        functools.partial(ring_kernel, count, many, 5, start, shapes),
        out_shape=[jax.ShapeDtypeStruct(late.shape, late.dtype)]
        + [jax.ShapeDtypeStruct((count,) + cut, late.dtype) for cut in cuts],
        in_specs=[pl.BlockSpec(memory_space=pl.ANY)] * (3 + dense),
        out_specs=[pl.BlockSpec(memory_space=pl.ANY)] * (1 + dense),
        scratch_shapes=[pltpu.VMEM((2, SLOTS) + half, jnp.bfloat16) for half in halves]
        + [pltpu.VMEM((2, 2) + half, jnp.bfloat16) for half in halves]
        + [pltpu.VMEM((2,) + quarter, jnp.bfloat16) for quarter in quarters]
        + [pltpu.VMEM((2,) + quarter, jnp.bfloat16) for quarter in quarters]
        + [pltpu.VMEM(quarter, jnp.bfloat16) for quarter in quarters]
        + [pltpu.VMEM((count,) + cut, jnp.bfloat16) for cut in cuts]
        + [
            dma((dense, 2)),
            dma((dense, 2)),
            dma((dense, 2)),
            dma((dense,)),
            dma((dense,)),
            dma((2 * total, SLOTS)),
            dma((2 * total, SLOTS)),
            dma((2 * total, 2)),
            dma((2 * total, SLOTS)),
            pltpu.SemaphoreType.REGULAR((2 * total,)),
        ],
        compiler_params=pltpu.CompilerParams(
            collective_id=0, has_side_effects=True, vmem_limit_bytes=VMEM_BYTES
        ),
        cost_estimate=pl.CostEstimate(flops=2 * size, bytes_accessed=8 * size, transcendentals=0),
        name="ring_sum",
    )(late, *partials, *initial)


def chunk_kernel(chunks, forth, back, *refs):
    for term, held, out in zip((forth, back), refs[:-2] or (None, None), refs[-2:]):
        if held is None:
            out[...] = term[:, 0]
        else:
            out[...] = (term[:, 0].astype(jnp.float32) + held[...].astype(jnp.float32)).astype(out.dtype)


def ring_chunks(units, step, held=()):
    many, count, rows, columns = units.shape
    rank, _, _ = ring_place(count)
    chunks = jnp.stack([(rank + count - step) % count, (rank + step) % count])
    half = columns // 2
    block = pl.BlockSpec((many, rows, half), lambda e, chunks: (0, 0, 0))
    return pl.pallas_call(
        chunk_kernel,
        grid_spec=pltpu.PrefetchScalarGridSpec(
            num_scalar_prefetch=1,
            grid=(1,),
            in_specs=[
                pl.BlockSpec((many, 1, rows, half), lambda e, chunks: (0, chunks[0], 0, 0)),
                pl.BlockSpec((many, 1, rows, half), lambda e, chunks: (0, chunks[1], 0, 1)),
            ]
            + [block] * len(held),
            out_specs=[block] * 2,
        ),
        out_shape=[jax.ShapeDtypeStruct((many, rows, half), units.dtype)] * 2,
        compiler_params=pltpu.CompilerParams(vmem_limit_bytes=VMEM_BYTES),
        name="ring_chunks",
    )(chunks, units, units, *held)


def ring_hop(parts, count):
    places = [ring_device(place, count) for place in range(count)]
    pairs = [(places[k], places[(k + 1) % count]) for k in range(count)]
    turned = [(b, a) for a, b in pairs]
    return lax.ppermute(parts[0], "rep", pairs), lax.ppermute(parts[1], "rep", turned)


def overlap_kernel(count, first, shapes, *refs):
    unit, near, far, (w_gate, w_up, w_down), hs, cots = (
        refs[0], refs[1:4], refs[4:7], refs[7:10], refs[10:14], refs[14:18]
    )
    gates, router_so_far, refs = refs[18:20], refs[20:22], refs[22:]
    unit_sum, grads, outs, router_far, rest_far, refs = refs[0], refs[1], refs[2:8], refs[8], refs[9:12], refs[12:]
    many = len(shapes)
    held_slots, terms, refs = refs[:many], refs[many : 2 * many], refs[2 * many :]
    (
        left_a, left_b, right_a, right_b, right_c, total, total_w, stage, stage_w, from_core, from_chip,
        gate_rows, router, router_core, router_chip,
        ready, core_sent, core_arrived, chip_sent, chip_arrived, out_done, grads_done, rows_ready, rest_done,
        router_sent, router_arrived,
    ) = refs[:26]
    held = w_gate.shape[0]
    tokens = hs[0].shape[0]
    _, after, before = ring_place(count)
    holder, core, chip, _ = group_places()
    hops = 2 * (count - 1)
    greet(after, before, core, chip)
    streams = both_ways(range(many))
    begin, add_step, hand_step, end = ring_tools(
        count,
        shapes,
        [unit.at[k] for k in range(many)],
        [unit_sum.at[k] for k in range(many)],
        held_slots,
        terms,
        refs[26:],
    )

    def tick(step):
        hop = step // many
        for k in range(many):
            turn = step % many == k
            pl.when(turn & (hop < count - 1))(lambda: add_step(both_ways([k]), hop))
            pl.when(turn & (hop >= count - 1) & (hop < hops))(lambda: hand_step(both_ways([k]), hop))

    def copies(bank, *pairs):
        return [pltpu.make_async_copy(source, target, ready.at[bank, k]) for source, target, k in pairs]

    def dh_copies(side, e, place, bank):
        return copies(
            bank,
            (side[1].at[place], left_a.at[bank], 0),
            (side[2].at[place], left_b.at[bank], 1),
            (w_gate.at[e], right_a.at[bank], 2),
            (w_up.at[e], right_b.at[bank], 3),
        )

    def y_copies(side, e, place, bank):
        return copies(bank, (side[0].at[place], left_a.at[bank], 0), (w_down.at[e], right_c.at[bank], 4))

    def load_sum(make, is_far, e, bank):
        if is_far:
            pl.when(e < first)(lambda: begin_all(make(far, e, e, bank)))
            pl.when(e >= first)(lambda: begin_all(make(rest_far, e, e - first, bank)))
        else:
            begin_all(make(near, e, e, bank))

    def load_w(e, kind, part, bank):
        rows = pl.ds((part % 2) * tokens, tokens)
        source = (1, 2, 0)[kind]
        right = rest_far[source].at[e - first, rows, :] if part // 2 else near[source].at[e, rows, :]
        left = (hs, hs, cots)[kind][part]
        return copies(bank, (right, left_a.at[bank, pl.ds(0, tokens), :], 0), (left, right_c.at[bank], 4))

    def load_expert(e, bank):
        return copies(
            bank,
            (w_gate.at[e], right_a.at[bank], 2),
            (w_up.at[e], right_b.at[bank], 3),
            (w_down.at[e], right_c.at[bank], 4),
        )

    def begin_all(made):
        for copy in made:
            copy.start()

    def await_all(made):
        for copy in made:
            copy.wait()

    def to_core(k):
        return pltpu.make_async_remote_copy(
            src_ref=stage.at[k % 2, 1],
            dst_ref=from_core.at[k],
            send_sem=core_sent.at[k],
            recv_sem=core_arrived.at[k],
            device_id={"ep": core},
        )

    def to_chip(k):
        return pltpu.make_async_remote_copy(
            src_ref=stage.at[0, 0],
            dst_ref=from_chip.at[k // 2],
            send_sem=chip_sent.at[k // 2],
            recv_sem=chip_arrived.at[k // 2],
            device_id={"ep": chip},
        )

    def send_chip(k):
        to_core(k).wait_recv()
        stage[0, 0] = (stage[0, 0].astype(jnp.float32) + from_core[k].astype(jnp.float32)).astype(jnp.bfloat16)
        to_chip(k).start()

    def own_out(k):
        return pltpu.make_async_copy(stage.at[1, 0], outs[3 * (k // 2)], out_done.at[3 * (k // 2)])

    def near_out(k):
        return pltpu.make_async_copy(from_core.at[k], outs[3 * (k // 2) + 1], out_done.at[3 * (k // 2) + 1])

    def far_out(k):
        return pltpu.make_async_copy(from_chip.at[k // 2], outs[3 * (k // 2) + 2], out_done.at[3 * (k // 2) + 2])

    far_rows = [
        pltpu.make_async_copy(source, target, rows_ready.at[k])
        for k, (source, target) in enumerate(
            [(hs[2], stage.at[0, 0]), (hs[3], stage.at[0, 1]), (cots[2], stage.at[1, 0]), (cots[3], stage.at[1, 1])]
            + [(gates[part], gate_rows.at[part]) for part in (0, 1)]
            + [(router_so_far[part], router.at[part]) for part in (0, 1)]
        )
    ]
    late = held - first
    tile = tokens // 2
    lane = lax.broadcasted_iota(jnp.int32, (tile, gates[0].shape[1]), 1)

    def rest_out(e, part, kind):
        slot = part % 2
        return pltpu.make_async_copy(
            left_b.at[slot, pl.ds(kind * tile, tile), :],
            rest_far[kind].at[e, pl.ds(part * tile, tile), :],
            rest_done.at[slot, kind],
        )

    begin_all(far_rows)
    begin_all(load_expert(first, 0))
    begin(streams)
    await_all(far_rows)
    step = 0

    def one_expert(e, carry):
        bank = e % 2
        await_all(load_expert(e + first, bank))

        @pl.when(e + 1 < late)
        def _():
            begin_all(load_expert(e + 1 + first, 1 - bank))

        mine = lane == holder * held + first + e
        for part in range(4):
            block, rows = part // 2, slice((part % 2) * tile, (part % 2 + 1) * tile)
            results = expert_tile(
                stage[0, block, rows], stage[1, block, rows], gate_rows[block, rows], mine,
                right_a[bank], right_b[bank], right_c[bank],
            )
            router[block, rows] = jnp.where(mine, results[3], router[block, rows])
            for kind in range(3):
                if part >= 2:
                    rest_out(e, part, kind).wait()
                else:
                    pl.when(e > 0)(lambda: rest_out(e, part, kind).wait())
                left_b[part % 2, kind * tile : (kind + 1) * tile] = results[kind]
                rest_out(e, part, kind).start()
            if part % 2 == 1:

                @pl.when(e >= 1)
                def _():
                    tick(step + 2 * (e - 1) + part // 2)

        return carry

    lax.fori_loop(0, late, one_expert, 0)
    step += 2 * (late - 1)
    for part in (2, 3):
        for kind in range(3):
            rest_out(late - 1, part, kind).wait()

    def router_to_core():
        return pltpu.make_async_remote_copy(
            src_ref=router.at[1],
            dst_ref=router_core,
            send_sem=router_sent.at[0],
            recv_sem=router_arrived.at[0],
            device_id={"ep": core},
        )

    def router_to_chip():
        return pltpu.make_async_remote_copy(
            src_ref=router.at[0],
            dst_ref=router_chip,
            send_sem=router_sent.at[1],
            recv_sem=router_arrived.at[1],
            device_id={"ep": chip},
        )

    router_to_core().start()
    plans = [(dh_copies, True), (dh_copies, False), (y_copies, True), (y_copies, False)]
    load_sum(dh_copies, True, 0, 0)
    for k, (make, is_far) in enumerate(plans):
        base = k * held

        def next_first(bank, k=k):
            if k + 1 < len(plans):
                load_sum(*plans[k + 1], 0, bank)
            else:
                begin_all(load_w(first, 0, 0, bank))

        every = 1 if make is dh_copies else 2

        def piece(e, carry, k=k, make=make, is_far=is_far, base=base, step=step, every=every, next_first=next_first):
            bank = (base + e) % 2
            await_all(make(near, e, e, bank))

            @pl.when(e + 1 < held)
            def _():
                load_sum(make, is_far, e + 1, 1 - bank)

            @pl.when(e + 1 == held)
            def _():
                next_first(1 - bank)

            if make is dh_copies:
                term = contract(left_a[bank], right_a[bank], 1, 1) + contract(left_b[bank], right_b[bank], 1, 1)
            else:
                term = contract(left_a[bank], right_c[bank], 1, 0)

            @pl.when(e == 0)
            def _():
                total[...] = term

            @pl.when(e > 0)
            def _():
                total[...] += term

            @pl.when((e + 1) % every == 0)
            def _():
                tick(step + e // every)

            if k % 2 == 1:

                @pl.when(e == 1)
                def _():
                    send_chip(k - 1)
                    if k == 1:
                        router_to_core().wait_recv()
                        router[0] += router_core[...]
                        router_to_chip().start()

            return carry

        lax.fori_loop(0, held, piece, 0)
        step += held // every
        if k >= 2:
            to_core(k - 2).wait_send()
            if k == 2:
                to_chip(0).wait_send()
            else:
                own_out(1).wait()
        for half in (0, 1):
            stage[k % 2, half] = total[half * tokens : (half + 1) * tokens].astype(jnp.bfloat16)
        to_core(k).start()
        if k % 2 == 1:
            own_out(k).start()
        if make is y_copies:
            tick(step)
            step += 1

    kinds = 3
    base = len(plans) * held

    def grads_out(e, kind):
        slot = (kinds * e + kind) % 2
        return pltpu.make_async_copy(stage_w.at[slot], grads.at[e, :, kind], grads_done.at[slot])

    def expert(e, carry):
        for kind in range(kinds):
            for part in range(4):
                bank = (base + 4 * kind + part) % 2
                await_all(load_w(e + first, kind, part, bank))
                if part < 3:
                    begin_all(load_w(e + first, kind, part + 1, 1 - bank))
                elif kind < kinds - 1:
                    begin_all(load_w(e + first, kind + 1, 0, 1 - bank))
                else:

                    @pl.when(e + first + 1 < held)
                    def _():
                        begin_all(load_w(e + first + 1, 0, 0, 1 - bank))

                term = contract(right_c[bank], left_a[bank, :tokens], 0, 0)
                if part == 0:
                    total_w[...] = term
                else:
                    total_w[...] += term

            @pl.when(kinds * e + kind >= 2)
            def _():
                grads_out(e, kind).wait()

            slot = (kinds * e + kind) % 2
            rows = stage_w.shape[2]
            for j in range(count):
                stage_w[slot, j] = total_w[j * rows : (j + 1) * rows].astype(jnp.bfloat16)
            grads_out(e, kind).start()
            tick(step + kinds * e + kind)
        return carry

    lax.fori_loop(0, late, expert, 0)
    step += kinds * late

    def drain(later, carry):
        tick(later)
        return carry

    lax.fori_loop(step, max(step, many * hops), drain, 0)
    end(streams)
    for k in (1, 3):
        to_core(k).wait_recv()
        near_out(k).start()
    for k in (0, 2):
        to_chip(k).wait_recv()
        far_out(k).start()
    router_to_chip().wait_recv()
    router_out = pltpu.make_async_copy(router_chip, router_far, rows_ready.at[0])
    router_out.start()
    router_to_core().wait_send()
    router_to_chip().wait_send()
    router_out.wait()
    for kind in (kinds - 2, kinds - 1):
        grads_out(late - 1, kind).wait()
    own_out(3).wait()
    to_chip(2).wait_send()
    for k in (2, 3):
        to_core(k).wait_send()
    for k in (1, 3):
        near_out(k).wait()
    for k in (0, 2):
        far_out(k).wait()


def overlap(unit, near, far, w_gate, w_up, w_down, hs, cots, gates, router_so_far, first):
    many, count, rows3, columns = unit.shape
    tokens, width = hs[0].shape
    held = w_gate.shape[0]
    shape, half = (rows3, columns), (rows3, columns // 2)
    block = jax.ShapeDtypeStruct((tokens, width), jnp.bfloat16)
    dma = pltpu.SemaphoreType.DMA

    def buffers(*shape):
        return pltpu.VMEM(shape, jnp.bfloat16)

    flops = 2 * tokens * width * columns * (4 * 3 * held + 12 * (held - first))
    inputs = [unit, *near, *far, w_gate, w_up, w_down, *hs, *cots, *gates, *router_so_far]
    late = held - first
    small = gates[0].shape
    unit_sum, grads, *blocks, router_far, _, _, _ = pl.pallas_call(
        functools.partial(overlap_kernel, count, first, [shape] * many),
        out_shape=[
            jax.ShapeDtypeStruct(unit.shape, unit.dtype),
            jax.ShapeDtypeStruct((held - first, count, 3, rows3 // 3, columns), jnp.bfloat16),
        ]
        + [block] * 6
        + [jax.ShapeDtypeStruct(small, jnp.float32)]
        + [jax.ShapeDtypeStruct((late, 2 * tokens, columns), jnp.bfloat16)] * 3,
        in_specs=[pl.BlockSpec(memory_space=pl.ANY)] * len(inputs),
        out_specs=[pl.BlockSpec(memory_space=pl.ANY)] * 12,
        scratch_shapes=[
            *[buffers(2, SLOTS, *half)] * many,
            *[buffers(2, 2, *half)] * many,
            buffers(2, 2 * tokens, columns),
            buffers(2, 2 * tokens, columns),
            buffers(2, width, columns),
            buffers(2, width, columns),
            buffers(2, columns, width),
            pltpu.VMEM((2 * tokens, width), jnp.float32),
            pltpu.VMEM((width, columns), jnp.float32),
            buffers(2, 2, tokens, width),
            buffers(2, count, rows3 // 3, columns),
            buffers(4, tokens, width),
            buffers(2, tokens, width),
            pltpu.VMEM((2,) + small, jnp.float32),
            pltpu.VMEM((2,) + small, jnp.float32),
            pltpu.VMEM(small, jnp.float32),
            pltpu.VMEM(small, jnp.float32),
            dma((2, 5)),
            dma((4,)),
            dma((4,)),
            dma((2,)),
            dma((2,)),
            dma((6,)),
            dma((2,)),
            dma((8,)),
            dma((2, 3)),
            dma((2,)),
            dma((2,)),
            dma((2 * many, SLOTS)),
            dma((2 * many, SLOTS)),
            dma((2 * many, 2)),
            dma((2 * many, SLOTS)),
            pltpu.SemaphoreType.REGULAR((2 * many,)),
        ],
        compiler_params=pltpu.CompilerParams(
            collective_id=1, has_side_effects=True, vmem_limit_bytes=60 * 2**20
        ),
        cost_estimate=pl.CostEstimate(flops=flops, bytes_accessed=8 * unit.size, transcendentals=0),
        name="overlap",
    )(*inputs)
    grads = grads.reshape(held - first, count, rows3, columns)
    return unit_sum, grads, blocks[:3], blocks[3:], router_far


def finish_kernel(firsts, *refs):
    units, (dense_o, dense_qkv) = refs[: len(firsts) - 1], refs[len(firsts) - 1 : len(firsts) + 1]
    gate, up, down, out, query, key, value, extra_o, extra_qkv = refs[len(firsts) + 1 :]

    @pl.when((pl.program_id(0) == 0) & (pl.program_id(1) == 0))
    def _():
        for dense, parts in ((dense_o, (out, extra_o)), (dense_qkv, (query, key, value, extra_qkv))):
            start = 0
            for part in parts:
                columns = part.shape[1]
                rows = dense.shape[1]
                for j in range(part.shape[0] // rows):
                    part[j * rows : (j + 1) * rows] = dense[j, :, start : start + columns].astype(jnp.float32)
                start += columns

    for index, unit in enumerate(units):
        e = pl.program_id(0)

        @pl.when((e >= firsts[index]) & (e < firsts[index + 1]))
        def _():
            rows = unit.shape[2] // 3
            for k in range(unit.shape[1]):
                gate[0, k * rows : (k + 1) * rows] = unit[0, k, :rows].astype(jnp.float32)
                up[0, k * rows : (k + 1) * rows] = unit[0, k, rows : 2 * rows].astype(jnp.float32)
            turned = jnp.concatenate([unit[0, k, 2 * rows :] for k in range(unit.shape[1])], 0)
            down[0] = turned.astype(jnp.float32).T


def finish(units, dense, width, key_width):
    count, rows3, columns = units[0].shape[1:]
    rows = rows3 // 3
    pair = count // 4
    small = [
        jax.ShapeDtypeStruct((width // 4, part), jnp.float32)
        for part in (width, width, key_width, key_width, 2 * LANES, 2 * LANES)
    ]
    firsts = [0]
    for unit in units:
        firsts.append(firsts[-1] + unit.shape[0])
    experts = firsts[-1]

    def place(index):
        first, end = firsts[index], firsts[index + 1]

        def chunk(e, c):
            inside = jnp.clip(e, first, end - 1)
            return (inside - first, jnp.where(e < first, 0, jnp.where(e >= end, 3, c)), 0, 0)

        return chunk

    return pl.pallas_call(
        functools.partial(finish_kernel, firsts),
        grid=(experts, 4),
        in_specs=[pl.BlockSpec((1, pair, rows3, columns), place(index)) for index in range(len(units))]
        + [whole(part) for part in dense],
        out_specs=[
            pl.BlockSpec((1, pair * rows, columns), lambda e, c: (e, c, 0)),
            pl.BlockSpec((1, pair * rows, columns), lambda e, c: (e, c, 0)),
            pl.BlockSpec((1, columns, pair * rows), lambda e, c: (e, 0, c)),
        ]
        + [whole(part) for part in small],
        out_shape=[
            jax.ShapeDtypeStruct((experts, width, columns), jnp.float32),
            jax.ShapeDtypeStruct((experts, width, columns), jnp.float32),
            jax.ShapeDtypeStruct((experts, columns, width), jnp.float32),
        ]
        + small,
        name="finish",
        compiler_params=pltpu.CompilerParams(vmem_limit_bytes=VMEM_BYTES),
    )(*units, *dense)


def swap_core(value):
    return lax.ppermute(value, "ep", [(0, 1), (1, 0), (2, 3), (3, 2)])


def swap_chip(value):
    return lax.ppermute(value, "ep", [(0, 2), (2, 0), (1, 3), (3, 1)])


def add_bf(a, b):
    return (a.astype(jnp.float32) + b.astype(jnp.float32)).astype(jnp.bfloat16)


def per_device(
    tokens,
    norm_attn,
    w_query,
    key_projection,
    value_projection,
    w_out,
    norm_ffn,
    w_router,
    w_gate,
    w_up,
    w_down,
    routes,
    cotangent,
):
    token_count, width = tokens.shape
    experts_all = w_router.shape[1]
    held = w_gate.shape[0]
    replicas = lax.axis_size("rep")
    cot_near = (cotangent, swap_core(cotangent))
    cot_far = swap_chip(cotangent)
    cosine, sine = rope_tables(token_count)
    normed, queries, keys, values, log_totals, attn, resid, h_two, probs, combine = attention_forward(
        tokens, norm_attn, w_query, key_projection, value_projection, cosine, sine, w_out, norm_ffn, w_router, routes
    )
    h_two, combine, cot_far = lax.optimization_barrier((h_two, combine, cot_far))
    h_near = (h_two, swap_core(h_two))
    gates_near = (combine, swap_core(combine))
    h_far, gates_far = swap_chip(h_two), swap_chip(combine)
    near = expert_pass(held, h_near, cot_near, gates_near, w_gate, w_up, w_down)
    near, h_far, gates_far = lax.optimization_barrier((near, h_far, gates_far))
    h_far = (h_far, swap_core(h_far))
    cot_far = (cot_far, swap_core(cot_far))
    gates_far = (gates_far, swap_core(gates_far))
    far = expert_pass(EARLY, h_far, cot_far, gates_far, w_gate, w_up, w_down)
    ghs, dgs, dus = zip(near[:3], far[:3])
    hs, cots = h_near + h_far, cot_near + cot_far

    router_own, router_near = near[3], swap_core(near[4])
    early = weight_grads(replicas, 0, EARLY, hs, cots, ghs, dgs, dus)
    early, late, (dh_own, dh_near, dh_far), (y_own, y_near, y_far), router_far = overlap(
        early, near[:3], far[:3], w_gate, w_up, w_down, hs, cots, gates_far, far[3:], EARLY
    )
    sent = ring_chunks(late, 1)
    arrived = ring_hop(sent, replicas)
    dh_own, sent = lax.optimization_barrier((dh_own, sent))
    d_resid, grad_out, d_attn = branch_back(
        dh_own, dh_near, dh_far, router_own, router_near, router_far, routes, probs, resid, norm_ffn, cotangent,
        w_router, w_out, h_two, attn,
    )
    arrived, d_attn = lax.optimization_barrier((arrived, d_attn))
    sent = ring_chunks(late, 2, arrived)
    arrived = ring_hop(sent, replicas)
    sent, d_attn = lax.optimization_barrier((sent, d_attn))
    d_pre = attention_back(d_attn, queries, keys, values, log_totals, cosine, sine)
    arrived, d_pre = lax.optimization_barrier((arrived, d_pre))
    sent = ring_chunks(late, 3, arrived)
    arrived = ring_hop(sent, replicas)
    sent, d_pre = lax.optimization_barrier((sent, d_pre))
    d_input, grad_qkv = input_back(
        d_pre, normed, tokens, norm_attn, d_resid, w_query, key_projection, value_projection
    )
    arrived, grad_qkv = lax.optimization_barrier((arrived, grad_qkv))
    initial = ring_chunks(late, 4, arrived)
    mixed = (
        resid + y_own.astype(jnp.float32) + y_near.astype(jnp.float32) + y_far.astype(jnp.float32)
    ).astype(jnp.bfloat16)
    late, sum_o, sum_qkv = ring_sum(late, [grad_out, grad_qkv], 3, initial)
    full_gate, full_up, full_down, sum_o, sum_q, sum_k, sum_v, extra_o, extra_qkv = finish(
        [early, late], [sum_o, sum_qkv], width, key_projection.shape[1]
    )
    sum_r, sum_nf, sum_na = extra_o[:, :experts_all], extra_o[:, LANES], extra_qkv[:, 0]
    return (
        mixed,
        d_input,
        sum_na,
        sum_q,
        sum_k,
        sum_v,
        sum_o,
        sum_nf,
        sum_r,
        full_gate,
        full_up,
        full_down,
    )


def solution(mesh):
    placed = (
        P(("rep", "ep"), None),
        P(),
        P(),
        P(),
        P(),
        P(),
        P(),
        P(),
        P("ep", None, None),
        P("ep", None, None),
        P("ep", None, None),
        P(("rep", "ep"), None),
        P(("rep", "ep"), None),
    )
    return jax.shard_map(
        per_device,
        mesh=mesh,
        in_specs=placed,
        out_specs=(
            P(("rep", "ep"), None),
            P(("rep", "ep"), None),
            P("ep"),
            P("ep", None),
            P("ep", None),
            P("ep", None),
            P("ep", None),
            P("ep"),
            P("ep", None),
            P("ep", None, None),
            P("ep", None, None),
            P("ep", None, None),
        ),
        check_vma=False,
    )
```

```python
import functools
import math

import jax
import jax.numpy as jnp
from jax import lax
from jax.experimental import pallas as pl
from jax.experimental.pallas import tpu as pltpu
from jax.sharding import PartitionSpec as P

QUERY_HEADS = 24
KEY_VALUE_HEADS = 8
HEAD_SIZE = 64
TOPK = 8
SEQUENCE_TOKENS = 512
BLOCK = 256
EARLY = 2


epsilon = 1e-06
masked_value = -1e30


def rope_tables(token_count):
    half = HEAD_SIZE // 2
    places = (jnp.arange(token_count) % SEQUENCE_TOKENS).astype(jnp.float32)
    rates = jnp.exp(jnp.arange(half, dtype=jnp.float32) * (-2.0 * math.log(10000.0) / HEAD_SIZE))
    angles = places[:, None] * rates[None, :]
    cosine, sine = jnp.cos(angles), jnp.sin(angles)
    return (
        jnp.concatenate([cosine] * 4, 1),
        jnp.concatenate([-sine, sine] * 2, 1),
    )


def contract(left, right, left_dim, right_dim):
    return lax.dot_general(
        left, right, (((left_dim,), (right_dim,)), ((), ())), preferred_element_type=jnp.float32
    )


def whole(array):
    return pl.BlockSpec(
        array.shape, lambda *_: (0,) * array.ndim, pipeline_mode=pl.Buffered(1)
    )


def each(array):
    return pl.BlockSpec((1,) + array.shape[1:], lambda e, *_: (e,) + (0,) * (array.ndim - 1))


VMEM_BYTES = 56 * 2**20


def expert_tile(entries, cotangents, gates, mine, w_gate, w_up, w_down):
    gate_pre = contract(entries, w_gate, 1, 0)
    up_pre = contract(entries, w_up, 1, 0)
    back = contract(cotangents, w_down, 1, 1)
    column = jnp.sum(jnp.where(mine, gates, 0.0), 1, keepdims=True)
    sigma = jax.nn.sigmoid(gate_pre)
    swish = gate_pre * sigma
    hidden = (swish * up_pre).astype(jnp.bfloat16).astype(jnp.float32)
    d_hidden = column * back
    return (
        (column * hidden).astype(jnp.bfloat16),
        (d_hidden * up_pre * (sigma * (1.0 + gate_pre * (1.0 - sigma)))).astype(jnp.bfloat16),
        (d_hidden * swish).astype(jnp.bfloat16),
        jnp.sum(hidden * back, 1, keepdims=True),
    )


def expert_kernel(tile, held, h0, h1, c0, c1, gates0, gates1, w_gate, w_up, w_down, gh, dg, du, d_router0, d_router1):
    e = pl.program_id(0)
    lanes, tokens = gates0.shape
    expert = lax.axis_index("ep") * held + e
    lane = lax.broadcasted_iota(jnp.int32, (tile, lanes), 1)

    @pl.when(e == 0)
    def _():
        d_router0[...] = jnp.zeros_like(d_router0)
        d_router1[...] = jnp.zeros_like(d_router1)

    for base, rows_h, rows_c, gates, d_router in (
        (0, h0, c0, gates0, d_router0),
        (tokens, h1, c1, gates1, d_router1),
    ):
        for start in range(0, tokens, tile):
            rows = slice(start, start + tile)
            out = slice(base + start, base + start + tile)
            results = expert_tile(
                rows_h[rows, :], rows_c[rows, :], gates[:, rows].T, lane == expert, w_gate[0], w_up[0], w_down[0]
            )
            gh[0, out, :], dg[0, out, :], du[0, out, :] = results[:3]
            d_router[rows, :] = jnp.where(lane == expert, results[3], d_router[rows, :])


def expert_pass(many, hs, cots, gates, w_gate, w_up, w_down):
    count, width = hs[0].shape
    tokens = 2 * count
    held, _, hidden_units = w_gate.shape
    part = jax.ShapeDtypeStruct((many, tokens, hidden_units), jnp.bfloat16)
    gate_shape = gates[0].shape[::-1]
    return pl.pallas_call(
        functools.partial(expert_kernel, 256, held),
        grid=(many,),
        in_specs=[whole(a) for a in (*hs, *cots, *gates)] + [each(a) for a in (w_gate, w_up, w_down)],
        out_specs=[each(part)] * 3 + [pl.BlockSpec(gate_shape, lambda e: (0, 0))] * 2,
        out_shape=[part] * 3 + [jax.ShapeDtypeStruct(gate_shape, jnp.float32)] * 2,
        compiler_params=pltpu.CompilerParams(vmem_limit_bytes=VMEM_BYTES),
        cost_estimate=pl.CostEstimate(
            flops=6 * many * tokens * width * hidden_units,
            bytes_accessed=6 * many * width * hidden_units,
            transcendentals=many * tokens * hidden_units,
        ),
        name="expert_pass",
    )(*hs, *cots, *gates, w_gate, w_up, w_down)


def weight_kernel(*refs):
    hs, cots, passes, unit = refs[:4], refs[4:8], refs[8:14], refs[14]
    kind = pl.program_id(1)

    def put(lefts, rights):
        count = lefts[0].shape[0]
        result = sum(
            contract(lefts[k][...], rights[k // 2][0, (k % 2) * count : (k % 2 + 1) * count], 0, 0)
            for k in range(4)
        ).astype(jnp.bfloat16)
        rows = unit.shape[3]
        for j in range(unit.shape[1]):
            unit[0, j, 0] = result[j * rows : (j + 1) * rows]

    pl.when(kind == 0)(lambda: put(hs, passes[2:4]))
    pl.when(kind == 1)(lambda: put(hs, passes[4:6]))
    pl.when(kind == 2)(lambda: put(cots, passes[:2]))


def weight_grads(count, first, many, hs, cots, ghs, dgs, dus):
    width = hs[0].shape[1]
    _, tokens, hidden_units = dgs[0].shape
    entry = pl.BlockSpec((1, tokens, hidden_units), lambda e, k: (e + first, 0, 0))
    unit = pl.pallas_call(
        weight_kernel,
        grid=(many, 3),
        in_specs=[whole(hs[0])] * 8 + [entry] * 6,
        out_specs=pl.BlockSpec((1, count, 1, width // count, hidden_units), lambda e, k: (e, 0, k, 0, 0)),
        out_shape=jax.ShapeDtypeStruct((many, count, 3, width // count, hidden_units), jnp.bfloat16),
        compiler_params=pltpu.CompilerParams(vmem_limit_bytes=VMEM_BYTES),
        cost_estimate=pl.CostEstimate(
            flops=12 * many * tokens * width * hidden_units,
            bytes_accessed=6 * many * (width + 2 * tokens) * hidden_units,
            transcendentals=0,
        ),
        name="weight_grads",
    )(*hs, *cots, *ghs, *dgs, *dus)
    return unit.reshape(many, count, 3 * (width // count), hidden_units)


def sum_kernel(right_dim, pairs, *refs):
    lefts, rights, outs, total = refs[:pairs], refs[pairs : 2 * pairs], refs[-3:-1], refs[-1]
    e = pl.program_id(0)
    term = sum(contract(left[0], right[0], 1, right_dim) for left, right in zip(lefts, rights))

    @pl.when(e == 0)
    def _():
        total[...] = term

    @pl.when(e > 0)
    def _():
        total[...] += term

    @pl.when(e == pl.num_programs(0) - 1)
    def _():
        for k, out in enumerate(outs):
            count = out.shape[0]
            out[...] = total[k * count : (k + 1) * count].astype(out.dtype)


def sum_over_experts(lefts, rights, right_dim):
    held, tokens, inner = lefts[0].shape
    width = rights[0].shape[2 - right_dim]
    return pl.pallas_call(
        functools.partial(sum_kernel, right_dim, len(lefts)),
        grid=(held,),
        in_specs=[each(a) for a in lefts] + [each(a) for a in rights],
        out_specs=[pl.BlockSpec((tokens // 2, width), lambda e: (0, 0))] * 2,
        out_shape=[jax.ShapeDtypeStruct((tokens // 2, width), jnp.bfloat16)] * 2,
        scratch_shapes=[pltpu.VMEM((tokens, width), jnp.float32)],
        compiler_params=pltpu.CompilerParams(vmem_limit_bytes=VMEM_BYTES),
        cost_estimate=pl.CostEstimate(
            flops=2 * len(lefts) * held * tokens * width * inner,
            bytes_accessed=2 * len(lefts) * held * (tokens + width) * inner,
            transcendentals=0,
        ),
        name="sum_over_experts",
    )(*lefts, *rights)


def rotate(values, cosine, sine, way):
    lane = lax.broadcasted_iota(jnp.int32, cosine.shape, 1)
    first = lane % HEAD_SIZE < HEAD_SIZE // 2
    lanes = cosine.shape[1]
    half = HEAD_SIZE // 2
    pieces = []
    for start in range(0, values.shape[1], lanes):
        piece = values[:, start : start + lanes]
        other = jnp.where(first, pltpu.roll(piece, lanes - half, 1), pltpu.roll(piece, half, 1))
        pieces.append(piece * cosine + way * (other * sine))
    return jnp.concatenate(pieces, 1)


def heads_of(array, group, rows, queries):
    return jnp.concatenate(
        [
            array[rows, (group * queries + j) * HEAD_SIZE : (group * queries + j + 1) * HEAD_SIZE]
            for j in range(queries)
        ],
        0,
    )


IN_VMEM = pl.BlockSpec(memory_space=pltpu.VMEM)
IN_PLACE = pl.BlockSpec(memory_space=pl.ANY)


def moves(semaphores, *pairs):
    return [pltpu.make_async_copy(source, target, semaphores.at[k]) for k, (source, target) in enumerate(pairs)]


def chosen_of(routes, shape):
    expert = lax.broadcasted_iota(jnp.int32, shape, 1)
    picks = routes[...].T
    chosen = picks[:, :1] == expert
    for k in range(1, picks.shape[1]):
        chosen = chosen | (picks[:, k : k + 1] == expert)
    return chosen


def attention_kernel(
    tokens, norm_attn, w_query_in, w_key_in, w_value_in, cosine, sine, w_out_in, norm_ffn, w_router, routes,
    normed_out, queries_out, keys_out, values_out, log_totals, attn_out, resid_out, h_two, probs, combine,
    w_query, w_key, w_value, w_out, normed, queries, keys, values, attn, resid, arrived, left,
):
    count, width = tokens.shape
    weights = moves(
        arrived, (w_query_in, w_query), (w_key_in, w_key), (w_value_in, w_value), (w_out_in, w_out)
    )
    results = moves(
        left, (normed, normed_out), (queries, queries_out), (keys, keys_out), (values, values_out), (attn, attn_out),
        (resid, resid_out),
    )
    for weight in weights:
        weight.start()
    field = tokens[...].astype(jnp.float32)
    inverse = lax.rsqrt(jnp.mean(field * field, -1, keepdims=True) + epsilon)
    first = (field * inverse * norm_attn[...].astype(jnp.float32)).astype(jnp.bfloat16)
    normed[...] = first
    results[0].start()
    for weight in weights[:3]:
        weight.wait()
    queries[...] = rotate(contract(first, w_query[...], 1, 0), cosine[...], sine[...], 1).astype(jnp.bfloat16)
    keys[...] = rotate(contract(first, w_key[...], 1, 0), cosine[...], sine[...], 1).astype(jnp.bfloat16)
    values[...] = contract(first, w_value[...], 1, 0).astype(jnp.bfloat16)
    for result in results[1:4]:
        result.start()
    groups = keys.shape[1] // HEAD_SIZE
    per_group = queries.shape[1] // keys.shape[1]
    lane = lax.broadcasted_iota(jnp.int32, (BLOCK, log_totals.shape[1]), 1)
    for block in range(count // BLOCK):
        rows = slice(block * BLOCK, (block + 1) * BLOCK)
        seen = slice(0, (block + 1) * BLOCK)
        logs = jnp.zeros((BLOCK, log_totals.shape[1]), jnp.float32)
        for group in range(groups):
            cut = slice(group * HEAD_SIZE, (group + 1) * HEAD_SIZE)
            scores = contract(heads_of(queries, group, rows, per_group), keys[seen, cut], 1, 1)
            scores = scores * HEAD_SIZE ** (-0.5)
            highest = jnp.max(scores, -1, keepdims=True)
            shifted = jnp.exp(scores - highest)
            sums = jnp.sum(shifted, -1, keepdims=True)
            probs_bf = (shifted * (1.0 / sums)).astype(jnp.bfloat16)
            mix = contract(probs_bf, values[seen, cut], 1, 0).astype(jnp.bfloat16)
            log_sum = highest + jnp.log(sums)
            for j in range(per_group):
                head = group * per_group + j
                part = slice(j * BLOCK, (j + 1) * BLOCK)
                attn[rows, head * HEAD_SIZE : (head + 1) * HEAD_SIZE] = mix[part]
                logs = jnp.where(lane == head, log_sum[part], logs)
        log_totals[rows, :] = logs
    results[4].start()
    weights[3].wait()
    total = field + contract(attn[...], w_out[...], 1, 0)
    resid[...] = total
    results[5].start()
    inverse = lax.rsqrt(jnp.mean(total * total, -1, keepdims=True) + epsilon)
    second = (total * inverse * norm_ffn[...].astype(jnp.float32)).astype(jnp.bfloat16)
    h_two[...] = second
    logits = contract(second, w_router[...], 1, 1)
    shifted = jnp.exp(logits - jnp.max(logits, -1, keepdims=True))
    soft = shifted / jnp.sum(shifted, -1, keepdims=True)
    probs[...] = soft
    combine[...] = jnp.where(chosen_of(routes, logits.shape), soft, 0.0).T
    for result in results:
        result.wait()


LANES = 128


def attention_forward(tokens, norm_attn, w_query, w_key, w_value, cosine, sine, w_out, norm_ffn, w_router, routes):
    count, width = tokens.shape
    experts = w_router.shape[1]
    key_width = w_key.shape[1]
    shape = jax.ShapeDtypeStruct
    return pl.pallas_call(
        attention_kernel,
        out_shape=[
            shape((count, width), jnp.bfloat16),
            shape((count, width), jnp.bfloat16),
            shape((count, key_width), jnp.bfloat16),
            shape((count, key_width), jnp.bfloat16),
            shape((count, LANES), jnp.float32),
            shape((count, width), jnp.bfloat16),
            shape((count, width), jnp.float32),
            shape((count, width), jnp.bfloat16),
            shape((count, experts), jnp.float32),
            shape((experts, count), jnp.float32),
        ],
        in_specs=[IN_VMEM] * 2 + [IN_PLACE] * 3 + [IN_VMEM] * 2 + [IN_PLACE] + [IN_VMEM] * 3,
        out_specs=[IN_PLACE] * 4 + [IN_VMEM] + [IN_PLACE] * 2 + [IN_VMEM] * 3,
        scratch_shapes=[
            pltpu.VMEM(weight.shape, weight.dtype) for weight in (w_query, w_key, w_value, w_out)
        ]
        + [
            pltpu.VMEM((count, width), jnp.bfloat16),
            pltpu.VMEM((count, width), jnp.bfloat16),
            pltpu.VMEM((count, key_width), jnp.bfloat16),
            pltpu.VMEM((count, key_width), jnp.bfloat16),
            pltpu.VMEM((count, width), jnp.bfloat16),
            pltpu.VMEM((count, width), jnp.float32),
            pltpu.SemaphoreType.DMA((4,)),
            pltpu.SemaphoreType.DMA((6,)),
        ],
        compiler_params=pltpu.CompilerParams(vmem_limit_bytes=VMEM_BYTES),
        cost_estimate=pl.CostEstimate(
            flops=6 * count * width * width, bytes_accessed=8 * width * width, transcendentals=24 * count * count
        ),
        name="attention_forward",
    )(
        tokens, norm_attn[None], w_query, w_key, w_value, cosine, sine, w_out, norm_ffn[None], w_router.T, routes.T
    )


def as_lane(row):
    first = lax.broadcasted_iota(jnp.int32, (LANES, row.shape[1]), 0) == 0
    return jnp.where(first, row, 0.0).T.astype(jnp.bfloat16)


def branch_back_kernel(
    dh_own, dh_near, dh_far, router_own, router_near, router_far, routes, probs, resid, norm_ffn, cotangent, w_router, w_out_in, h_two_in, attn_in,
    d_resid_out, grad_out_out, d_attn, w_out, h_two, attn, d_resid, grad_out, d_branch, arrived, left,
):
    count, width = resid.shape
    experts = probs.shape[1]
    inputs = moves(arrived, (w_out_in, w_out), (h_two_in, h_two), (attn_in, attn))
    results = moves(left, (d_resid, d_resid_out), (grad_out, grad_out_out))
    for copy in inputs:
        copy.start()
    soft = probs[...]
    to_router = jnp.where(
        chosen_of(routes, soft.shape), router_own[...] + router_near[...] + router_far[...], 0.0
    )
    d_logits = (soft * (to_router - jnp.sum(soft * to_router, -1, keepdims=True))).astype(jnp.bfloat16)
    d_normed = (
        dh_own[...].astype(jnp.float32)
        + dh_near[...].astype(jnp.float32)
        + dh_far[...].astype(jnp.float32)
        + contract(d_logits, w_router[...], 1, 0)
    )
    total = resid[...]
    inverse = lax.rsqrt(jnp.mean(total * total, -1, keepdims=True) + epsilon)
    normal = total * inverse
    scaled = d_normed * norm_ffn[...].astype(jnp.float32)
    back = cotangent[...].astype(jnp.float32) + inverse * (
        scaled - normal * jnp.mean(scaled * normal, -1, keepdims=True)
    )
    d_resid[...] = back
    results[0].start()
    d_branch[...] = back.astype(jnp.bfloat16)
    for copy in inputs:
        copy.wait()
    grad_out[:, :width] = contract(attn[...], d_branch[...], 0, 0).astype(jnp.bfloat16)
    d_logits = jnp.concatenate([d_logits, jnp.zeros((count, LANES - experts), jnp.bfloat16)], 1)
    grad_out[:, width : width + LANES] = contract(h_two[...], d_logits, 0, 0).astype(jnp.bfloat16)
    grad_out[:, width + LANES :] = as_lane(jnp.sum(d_normed * normal, 0, keepdims=True))
    results[1].start()
    d_attn[...] = contract(d_branch[...], w_out[...], 1, 1).astype(jnp.bfloat16)
    for copy in results:
        copy.wait()


def attention_back_kernel(
    d_attn, queries, keys, values, log_totals, cosine, sine, d_pre, d_queries, d_keys, d_values
):
    count, width = queries.shape
    groups = keys.shape[1] // HEAD_SIZE
    per_group = queries.shape[1] // keys.shape[1]
    factor = HEAD_SIZE ** (-0.5)
    lane = lax.broadcasted_iota(jnp.int32, (BLOCK, log_totals.shape[1]), 1)
    for block in reversed(range(count // BLOCK)):
        rows = slice(block * BLOCK, (block + 1) * BLOCK)
        seen = slice(0, (block + 1) * BLOCK)
        logs = log_totals[rows, :]
        for group in range(groups):
            cut = slice(group * HEAD_SIZE, (group + 1) * HEAD_SIZE)
            part_q = heads_of(queries, group, rows, per_group)
            part_d = heads_of(d_attn, group, rows, per_group)
            log_sum = jnp.concatenate(
                [
                    jnp.sum(jnp.where(lane == group * per_group + j, logs, 0.0), 1, keepdims=True)
                    for j in range(per_group)
                ],
                0,
            )
            part_k, part_v = keys[seen, cut], values[seen, cut]
            probs_f = jnp.exp(contract(part_q, part_k, 1, 1) * factor - log_sum)
            d_probs = contract(part_d, part_v, 1, 1)
            centre = jnp.sum(probs_f * d_probs, -1, keepdims=True)
            d_scores = (probs_f * (d_probs - centre)).astype(jnp.bfloat16)
            turned = contract(d_scores, part_k, 1, 0) * factor
            for j in range(per_group):
                head = group * per_group + j
                d_queries[rows, head * HEAD_SIZE : (head + 1) * HEAD_SIZE] = turned[j * BLOCK : (j + 1) * BLOCK]
            new_k = contract(d_scores, part_q, 0, 0) * factor
            new_v = contract(probs_f.astype(jnp.bfloat16), part_d, 0, 0)
            if block == count // BLOCK - 1:
                d_keys[seen, cut] = new_k
                d_values[seen, cut] = new_v
            else:
                d_keys[seen, cut] += new_k
                d_values[seen, cut] += new_v
    key_width = keys.shape[1]
    d_pre[:, :width] = rotate(d_queries[...], cosine[...], sine[...], -1).astype(jnp.bfloat16)
    d_pre[:, width : width + key_width] = rotate(d_keys[...], cosine[...], sine[...], -1).astype(jnp.bfloat16)
    d_pre[:, width + key_width :] = d_values[...].astype(jnp.bfloat16)


def branch_back(dh_own, dh_near, dh_far, router_own, router_near, router_far, routes, probs, resid, norm_ffn, cotangent,
                w_router, w_out, h_two, attn):
    count, width = resid.shape
    shape = jax.ShapeDtypeStruct
    return pl.pallas_call(
        branch_back_kernel,
        out_shape=[
            shape((count, width), jnp.float32),
            shape((width, width + 2 * LANES), jnp.bfloat16),
            shape((count, width), jnp.bfloat16),
        ],
        in_specs=[IN_VMEM] * 12 + [IN_PLACE] * 3,
        out_specs=[IN_PLACE] * 2 + [IN_VMEM],
        scratch_shapes=[
            pltpu.VMEM(w_out.shape, jnp.bfloat16),
            pltpu.VMEM((count, width), jnp.bfloat16),
            pltpu.VMEM((count, width), jnp.bfloat16),
            pltpu.VMEM((count, width), jnp.float32),
            pltpu.VMEM((width, width + 2 * LANES), jnp.bfloat16),
            pltpu.VMEM((count, width), jnp.bfloat16),
            pltpu.SemaphoreType.DMA((3,)),
            pltpu.SemaphoreType.DMA((2,)),
        ],
        compiler_params=pltpu.CompilerParams(vmem_limit_bytes=VMEM_BYTES),
        cost_estimate=pl.CostEstimate(
            flops=4 * count * width * width, bytes_accessed=8 * width * width, transcendentals=0
        ),
        name="branch_back",
    )(
        dh_own, dh_near, dh_far, router_own, router_near, router_far, routes.T, probs, resid, norm_ffn[None], cotangent,
        w_router.T, w_out, h_two, attn,
    )


def attention_back(d_attn, queries, keys, values, log_totals, cosine, sine):
    count, width = queries.shape
    key_width = keys.shape[1]
    return pl.pallas_call(
        attention_back_kernel,
        out_shape=jax.ShapeDtypeStruct((count, width + 2 * key_width), jnp.bfloat16),
        scratch_shapes=[
            pltpu.VMEM((count, width), jnp.float32),
            pltpu.VMEM((count, key_width), jnp.float32),
            pltpu.VMEM((count, key_width), jnp.float32),
        ],
        compiler_params=pltpu.CompilerParams(vmem_limit_bytes=VMEM_BYTES),
        cost_estimate=pl.CostEstimate(
            flops=8 * count * width * width, bytes_accessed=4 * width * width, transcendentals=24 * count * count
        ),
        name="attention_back",
    )(d_attn, queries, keys, values, log_totals, cosine, sine)


def input_kernel(
    d_pre, normed, tokens_in, norm_attn, d_resid_in, w_query_in, w_key_in, w_value_in, d_input, grads_out,
    tokens, d_resid, w_query, w_key, w_value, grads, arrived, left,
):
    width, key_width = w_query.shape[1], w_key.shape[1]
    inputs = moves(
        arrived, (w_query_in, w_query), (w_key_in, w_key), (w_value_in, w_value), (tokens_in, tokens), (d_resid_in, d_resid)
    )
    for copy in inputs:
        copy.start()
    wide = d_pre.shape[1]
    results = moves(
        left,
        *[
            (grads.at[:, pl.ds(start, key_width)], grads_out.at[:, pl.ds(start, key_width)])
            for start in range(0, wide, key_width)
        ],
        (grads.at[:, pl.ds(wide, 2 * LANES)], grads_out.at[:, pl.ds(wide, 2 * LANES)]),
    )
    for k, start in enumerate(range(0, wide, key_width)):
        cut = slice(start, start + key_width)
        grads[:, cut] = contract(normed[...], d_pre[:, cut], 0, 0).astype(jnp.bfloat16)
        results[k].start()
    for copy in inputs:
        copy.wait()
    d_normed = (
        contract(d_pre[:, :width], w_query[...], 1, 1)
        + contract(d_pre[:, width : width + key_width], w_key[...], 1, 1)
        + contract(d_pre[:, width + key_width :], w_value[...], 1, 1)
    )
    field = tokens[...].astype(jnp.float32)
    inverse = lax.rsqrt(jnp.mean(field * field, -1, keepdims=True) + epsilon)
    normal = field * inverse
    scaled = d_normed * norm_attn[...].astype(jnp.float32)
    grads[:, wide : wide + LANES] = as_lane(jnp.sum(d_normed * normal, 0, keepdims=True))
    grads[:, wide + LANES :] = jnp.zeros((width, LANES), jnp.bfloat16)
    results[-1].start()
    d_input[...] = d_resid[...] + inverse * (scaled - normal * jnp.mean(scaled * normal, -1, keepdims=True))
    for copy in results:
        copy.wait()


def input_back(d_pre, normed, tokens, norm_attn, d_resid, w_query, w_key, w_value):
    count, width = tokens.shape
    shape = jax.ShapeDtypeStruct
    return pl.pallas_call(
        input_kernel,
        out_shape=[
            shape((count, width), jnp.float32),
            shape((width, d_pre.shape[1] + 2 * LANES), jnp.bfloat16),
        ],
        in_specs=[IN_VMEM] * 2 + [IN_PLACE, IN_VMEM] + [IN_PLACE] * 4,
        out_specs=[IN_VMEM, IN_PLACE],
        scratch_shapes=[
            pltpu.VMEM((count, width), jnp.bfloat16),
            pltpu.VMEM((count, width), jnp.float32),
            *[pltpu.VMEM(weight.shape, jnp.bfloat16) for weight in (w_query, w_key, w_value)],
            pltpu.VMEM((width, d_pre.shape[1] + 2 * LANES), jnp.bfloat16),
            pltpu.SemaphoreType.DMA((5,)),
            pltpu.SemaphoreType.DMA((d_pre.shape[1] // w_key.shape[1] + 1,)),
        ],
        compiler_params=pltpu.CompilerParams(vmem_limit_bytes=VMEM_BYTES),
        cost_estimate=pl.CostEstimate(
            flops=8 * count * width * width, bytes_accessed=12 * width * width, transcendentals=0
        ),
        name="input_back",
    )(d_pre, normed, tokens, norm_attn[None], d_resid, w_query, w_key, w_value)


SLOTS = 3


def ring_device(place, count):
    back = place // (count // 2)
    return (1 - back) * 2 * place + back * (2 * (count - 1 - place) + 1)


def ring_place(count):
    here = lax.axis_index("rep")
    odd = here % 2
    rank = here // 2 + odd * (count - 1 - 2 * (here // 2))
    after = ring_device((rank + 1) % count, count)
    before = ring_device((rank + count - 1) % count, count)
    return rank, after, before


def group_places():
    holder = lax.axis_index("ep")
    core = holder + 1 - 2 * (holder % 2)
    return holder, core, (holder + 2) % 4, (core + 2) % 4


def greet(after, before, core, chip):
    barrier = pltpu.get_barrier_semaphore()
    for neighbour in (before, after):
        pl.semaphore_signal(barrier, inc=1, device_id={"rep": neighbour})
    for neighbour in (core, chip):
        pl.semaphore_signal(barrier, inc=1, device_id={"ep": neighbour})
    pl.semaphore_wait(barrier, 4)


def ring_tools(count, shapes, sources, sums, held, terms, semaphores, start=0, initial=()):
    arrived, sent, loaded, stored, credit = semaphores
    rank, after, before = ring_place(count)
    hops = 2 * (count - 1)

    def columns(index, way):
        half = shapes[index][1] // 2
        return pl.ds(way * half, half)

    def send(index, way, hop):
        stream = 2 * index + way
        source = (hop + SLOTS - 1) % SLOTS
        slot = hop % SLOTS
        return pltpu.make_async_remote_copy(
            src_ref=held[index].at[way, source],
            dst_ref=held[index].at[way, slot],
            send_sem=sent.at[stream, slot],
            recv_sem=arrived.at[stream, slot],
            device_id={"rep": before if way else after},
        )

    def load(index, way, hop):
        step = hop + 2
        chunk = (rank + step) % count if way else (rank + 2 * count - step) % count
        return pltpu.make_async_copy(
            sources[index].at[chunk, :, columns(index, way)],
            terms[index].at[way, hop % 2],
            loaded.at[2 * index + way, hop % 2],
        )

    started = initial[0].shape[0] if initial else 0

    def begins(index):
        return start if index < started else 0

    def first(index, way):
        chunk = (rank + 1) % count if way else (rank + count - 1) % count
        source = initial[way].at[index] if index < started else sources[index].at[chunk, :, columns(index, way)]
        slot = (begins(index) + SLOTS - 1) % SLOTS
        return pltpu.make_async_copy(source, held[index].at[way, slot], stored.at[2 * index + way, slot])

    def store(index, way, hop):
        step = hop - (count - 2)
        chunk = (rank + step) % count if way else (rank + count - step) % count
        return pltpu.make_async_copy(
            held[index].at[way, hop % SLOTS],
            sums[index].at[chunk, :, columns(index, way)],
            stored.at[2 * index + way, hop % SLOTS],
        )

    def release(index, way):
        pl.semaphore_signal(
            credit.at[2 * index + way], inc=1, device_id={"rep": after if way else before}
        )

    def begin(streams):
        for index, way in streams:
            first(index, way).start()
        for index, way in streams:
            load(index, way, begins(index)).start()
            load(index, way, begins(index) + 1).start()
        for index, way in streams:
            first(index, way).wait()
            send(index, way, begins(index)).start()

    def take(index, way, hop):
        send(index, way, hop).wait_recv()
        send(index, way, hop).wait_send()

    def pass_on(index, way, hop):
        @pl.when(hop + 1 >= begins(index) + 2)
        def _():
            pl.semaphore_wait(credit.at[2 * index + way], 1)

        send(index, way, hop + 1).start()

    def add_step(streams, hop):
        for index, way in streams:
            take(index, way, hop)

            @pl.when(hop <= hops - 3)
            def _():
                release(index, way)

            load(index, way, hop).wait()
            slot = hop % SLOTS
            held[index][way, slot] = (
                held[index][way, slot].astype(jnp.float32)
                + terms[index][way, hop % 2].astype(jnp.float32)
            ).astype(jnp.bfloat16)
            pass_on(index, way, hop)

            @pl.when(hop + 2 <= count - 2)
            def _():
                load(index, way, hop + 2).start()

            @pl.when(hop == count - 2)
            def _():
                store(index, way, hop).start()

    def hand_step(streams, hop):
        for index, way in streams:
            take(index, way, hop)
            store(index, way, hop - 1).wait()

            @pl.when(hop <= hops - 3)
            def _():
                release(index, way)

            @pl.when(hop + 1 < hops)
            def _():
                pass_on(index, way, hop)

            store(index, way, hop).start()

    def end(streams):
        for index, way in streams:
            store(index, way, hops - 1).wait()

    return begin, add_step, hand_step, end


def both_ways(indices):
    return [(index, way) for index in indices for way in (0, 1)]


def ring_kernel(count, many, lag, start, shapes, *refs):
    dense = len(shapes) - many
    inputs, initial, refs = refs[: 1 + dense], refs[1 + dense : 3 + dense], refs[3 + dense :]
    outputs, rest = refs[: 1 + dense], refs[1 + dense :]
    total = len(shapes)
    held, terms, rest = rest[:total], rest[total : 2 * total], rest[2 * total :]
    own, near, far, joined, rest = (
        rest[:dense], rest[dense : 2 * dense], rest[2 * dense : 3 * dense], rest[3 * dense : 4 * dense], rest[4 * dense :]
    )
    near_sent, near_arrived, own_loaded, far_sent, far_arrived = rest[:5]
    sources = [inputs[0].at[k] for k in range(many)] + list(joined)
    sums = [outputs[0].at[k] for k in range(many)] + list(outputs[1:])
    _, after, before = ring_place(count)
    holder, core, chip, far_core = group_places()
    hops = 2 * (count - 1)
    greet(after, before, core, chip)
    begin, add_step, hand_step, end = ring_tools(
        count, shapes, sources, sums, held, terms, rest[5:], start, initial
    )

    def block(k, index):
        rows = own[k].shape[1]
        return inputs[1 + k].at[pl.ds(pl.multiple_of(index * rows, 8), rows), :]

    def to_core(k, part):
        return pltpu.make_async_remote_copy(
            src_ref=block(k, far_core if part else core),
            dst_ref=near[k].at[part],
            send_sem=near_sent.at[k, part],
            recv_sem=near_arrived.at[k, part],
            device_id={"ep": core},
        )

    def own_block(k, part):
        return pltpu.make_async_copy(
            block(k, chip if part else holder), own[k].at[part], own_loaded.at[k, part]
        )

    def to_chip(k):
        return pltpu.make_async_remote_copy(
            src_ref=own[k].at[1],
            dst_ref=far[k],
            send_sem=far_sent.at[k],
            recv_sem=far_arrived.at[k],
            device_id={"ep": chip},
        )

    pieces = 8

    def send_far():
        for k in range(dense):
            to_core(k, 1).wait_recv()
            own_block(k, 1).wait()
            rows = own[k].shape[1] // pieces
            for j in range(pieces):
                cut = slice(j * rows, (j + 1) * rows)
                own[k][1, cut] = (
                    own[k][1, cut].astype(jnp.float32) + near[k][1, cut].astype(jnp.float32)
                ).astype(jnp.bfloat16)
            to_chip(k).start()

    def join():
        for k in range(dense):
            to_core(k, 0).wait_recv()
            own_block(k, 0).wait()
            to_chip(k).wait_recv()
            to_chip(k).wait_send()
            for part in (0, 1):
                to_core(k, part).wait_send()
            rows = joined[k].shape[1]
            for j in range(count):
                if j * rows < own[k].shape[1]:
                    cut = slice(j * rows, (j + 1) * rows)
                    joined[k][j] = (
                        own[k][0, cut].astype(jnp.float32)
                        + near[k][0, cut].astype(jnp.float32)
                        + far[k][cut].astype(jnp.float32)
                    ).astype(jnp.bfloat16)
                else:
                    joined[k][j] = jnp.zeros(joined[k].shape[1:], jnp.bfloat16)

    early_streams, late_streams = both_ways(range(many)), both_ways(range(many, total))
    for k in range(dense):
        for part in (1, 0):
            to_core(k, part).start()
            own_block(k, part).start()
    begin(early_streams)
    ends = sorted({0, 1, lag, count - 1 - start, hops - start, lag + count - 1, lag + hops})
    for low, high in zip(ends[:-1], ends[1:]):
        if low == 1:
            send_far()
        if low == lag:
            join()
            begin(late_streams)

        def ticks(tick, carry, low=low):
            for streams, zero in ((early_streams, -start), (late_streams, lag)):
                if max(zero, 0) <= low < zero + count - 1:
                    add_step(streams, tick - zero)
                elif zero + count - 1 <= low < zero + hops:
                    hand_step(streams, tick - zero)
            return carry

        lax.fori_loop(low, high, ticks, 0)
    end(early_streams + late_streams)


def ring_sum(late, partials, start, initial):
    many, count = late.shape[:2]
    quarters = [(partial.shape[0] // 4, partial.shape[1]) for partial in partials]
    cuts = [(-(-rows // (8 * count)) * 8, columns) for rows, columns in quarters]
    shapes = [late.shape[2:]] * many + cuts
    total, dense = len(shapes), len(partials)
    halves = [(rows, columns // 2) for rows, columns in shapes]
    size = late.size + sum(partial.size for partial in partials)
    dma = pltpu.SemaphoreType.DMA
    return pl.pallas_call(
        functools.partial(ring_kernel, count, many, 5, start, shapes),
        out_shape=[jax.ShapeDtypeStruct(late.shape, late.dtype)]
        + [jax.ShapeDtypeStruct((count,) + cut, late.dtype) for cut in cuts],
        in_specs=[pl.BlockSpec(memory_space=pl.ANY)] * (3 + dense),
        out_specs=[pl.BlockSpec(memory_space=pl.ANY)] * (1 + dense),
        scratch_shapes=[pltpu.VMEM((2, SLOTS) + half, jnp.bfloat16) for half in halves]
        + [pltpu.VMEM((2, 2) + half, jnp.bfloat16) for half in halves]
        + [pltpu.VMEM((2,) + quarter, jnp.bfloat16) for quarter in quarters]
        + [pltpu.VMEM((2,) + quarter, jnp.bfloat16) for quarter in quarters]
        + [pltpu.VMEM(quarter, jnp.bfloat16) for quarter in quarters]
        + [pltpu.VMEM((count,) + cut, jnp.bfloat16) for cut in cuts]
        + [
            dma((dense, 2)),
            dma((dense, 2)),
            dma((dense, 2)),
            dma((dense,)),
            dma((dense,)),
            dma((2 * total, SLOTS)),
            dma((2 * total, SLOTS)),
            dma((2 * total, 2)),
            dma((2 * total, SLOTS)),
            pltpu.SemaphoreType.REGULAR((2 * total,)),
        ],
        compiler_params=pltpu.CompilerParams(
            collective_id=0, has_side_effects=True, vmem_limit_bytes=VMEM_BYTES
        ),
        cost_estimate=pl.CostEstimate(flops=2 * size, bytes_accessed=8 * size, transcendentals=0),
        name="ring_sum",
    )(late, *partials, *initial)


def chunk_kernel(chunks, forth, back, *refs):
    for term, held, out in zip((forth, back), refs[:-2] or (None, None), refs[-2:]):
        if held is None:
            out[...] = term[:, 0]
        else:
            out[...] = (term[:, 0].astype(jnp.float32) + held[...].astype(jnp.float32)).astype(out.dtype)


def ring_chunks(units, step, held=()):
    many, count, rows, columns = units.shape
    rank, _, _ = ring_place(count)
    chunks = jnp.stack([(rank + count - step) % count, (rank + step) % count])
    half = columns // 2
    block = pl.BlockSpec((many, rows, half), lambda e, chunks: (0, 0, 0))
    return pl.pallas_call(
        chunk_kernel,
        grid_spec=pltpu.PrefetchScalarGridSpec(
            num_scalar_prefetch=1,
            grid=(1,),
            in_specs=[
                pl.BlockSpec((many, 1, rows, half), lambda e, chunks: (0, chunks[0], 0, 0)),
                pl.BlockSpec((many, 1, rows, half), lambda e, chunks: (0, chunks[1], 0, 1)),
            ]
            + [block] * len(held),
            out_specs=[block] * 2,
        ),
        out_shape=[jax.ShapeDtypeStruct((many, rows, half), units.dtype)] * 2,
        compiler_params=pltpu.CompilerParams(vmem_limit_bytes=VMEM_BYTES),
        name="ring_chunks",
    )(chunks, units, units, *held)


def ring_hop(parts, count):
    places = [ring_device(place, count) for place in range(count)]
    pairs = [(places[k], places[(k + 1) % count]) for k in range(count)]
    turned = [(b, a) for a, b in pairs]
    return lax.ppermute(parts[0], "rep", pairs), lax.ppermute(parts[1], "rep", turned)


def overlap_kernel(count, first, shapes, *refs):
    unit, near, far, (w_gate, w_up, w_down), hs, cots = (
        refs[0], refs[1:4], refs[4:7], refs[7:10], refs[10:14], refs[14:18]
    )
    gates, router_so_far, refs = refs[18:20], refs[20:22], refs[22:]
    unit_sum, grads, outs, router_far, rest_far, refs = refs[0], refs[1], refs[2:8], refs[8], refs[9:12], refs[12:]
    many = len(shapes)
    held_slots, terms, refs = refs[:many], refs[many : 2 * many], refs[2 * many :]
    (
        left_a, left_b, right_a, right_b, right_c, total, total_w, stage, stage_w, from_core, from_chip,
        gate_rows, router, router_core, router_chip,
        ready, core_sent, core_arrived, chip_sent, chip_arrived, out_done, grads_done, rows_ready, rest_done,
        router_sent, router_arrived,
    ) = refs[:26]
    held = w_gate.shape[0]
    tokens = hs[0].shape[0]
    _, after, before = ring_place(count)
    holder, core, chip, _ = group_places()
    hops = 2 * (count - 1)
    greet(after, before, core, chip)
    streams = both_ways(range(many))
    begin, add_step, hand_step, end = ring_tools(
        count,
        shapes,
        [unit.at[k] for k in range(many)],
        [unit_sum.at[k] for k in range(many)],
        held_slots,
        terms,
        refs[26:],
    )

    def tick(step):
        hop = step // many
        for k in range(many):
            turn = step % many == k
            pl.when(turn & (hop < count - 1))(lambda: add_step(both_ways([k]), hop))
            pl.when(turn & (hop >= count - 1) & (hop < hops))(lambda: hand_step(both_ways([k]), hop))

    def copies(bank, *pairs):
        return [pltpu.make_async_copy(source, target, ready.at[bank, k]) for source, target, k in pairs]

    def dh_copies(side, e, place, bank):
        return copies(
            bank,
            (side[1].at[place], left_a.at[bank], 0),
            (side[2].at[place], left_b.at[bank], 1),
            (w_gate.at[e], right_a.at[bank], 2),
            (w_up.at[e], right_b.at[bank], 3),
        )

    def y_copies(side, e, place, bank):
        return copies(bank, (side[0].at[place], left_a.at[bank], 0), (w_down.at[e], right_c.at[bank], 4))

    def load_sum(make, is_far, e, bank):
        if is_far:
            pl.when(e < first)(lambda: begin_all(make(far, e, e, bank)))
            pl.when(e >= first)(lambda: begin_all(make(rest_far, e, e - first, bank)))
        else:
            begin_all(make(near, e, e, bank))

    def load_w(e, kind, part, bank):
        rows = pl.ds((part % 2) * tokens, tokens)
        source = (1, 2, 0)[kind]
        right = rest_far[source].at[e - first, rows, :] if part // 2 else near[source].at[e, rows, :]
        left = (hs, hs, cots)[kind][part]
        return copies(bank, (right, left_a.at[bank, pl.ds(0, tokens), :], 0), (left, right_c.at[bank], 4))

    def load_expert(e, bank):
        return copies(
            bank,
            (w_gate.at[e], right_a.at[bank], 2),
            (w_up.at[e], right_b.at[bank], 3),
            (w_down.at[e], right_c.at[bank], 4),
        )

    def begin_all(made):
        for copy in made:
            copy.start()

    def await_all(made):
        for copy in made:
            copy.wait()

    def to_core(k):
        return pltpu.make_async_remote_copy(
            src_ref=stage.at[k % 2, 1],
            dst_ref=from_core.at[k],
            send_sem=core_sent.at[k],
            recv_sem=core_arrived.at[k],
            device_id={"ep": core},
        )

    def to_chip(k):
        return pltpu.make_async_remote_copy(
            src_ref=stage.at[0, 0],
            dst_ref=from_chip.at[k // 2],
            send_sem=chip_sent.at[k // 2],
            recv_sem=chip_arrived.at[k // 2],
            device_id={"ep": chip},
        )

    def send_chip(k):
        to_core(k).wait_recv()
        stage[0, 0] = (stage[0, 0].astype(jnp.float32) + from_core[k].astype(jnp.float32)).astype(jnp.bfloat16)
        to_chip(k).start()

    def own_out(k):
        return pltpu.make_async_copy(stage.at[1, 0], outs[3 * (k // 2)], out_done.at[3 * (k // 2)])

    def near_out(k):
        return pltpu.make_async_copy(from_core.at[k], outs[3 * (k // 2) + 1], out_done.at[3 * (k // 2) + 1])

    def far_out(k):
        return pltpu.make_async_copy(from_chip.at[k // 2], outs[3 * (k // 2) + 2], out_done.at[3 * (k // 2) + 2])

    far_rows = [
        pltpu.make_async_copy(source, target, rows_ready.at[k])
        for k, (source, target) in enumerate(
            [(hs[2], stage.at[0, 0]), (hs[3], stage.at[0, 1]), (cots[2], stage.at[1, 0]), (cots[3], stage.at[1, 1])]
            + [(gates[part], gate_rows.at[part]) for part in (0, 1)]
            + [(router_so_far[part], router.at[part]) for part in (0, 1)]
        )
    ]
    late = held - first
    tile = tokens // 2
    lane = lax.broadcasted_iota(jnp.int32, (tile, gates[0].shape[0]), 1)

    def rest_out(e, part, kind):
        slot = part % 2
        return pltpu.make_async_copy(
            left_b.at[slot, pl.ds(kind * tile, tile), :],
            rest_far[kind].at[e, pl.ds(part * tile, tile), :],
            rest_done.at[slot, kind],
        )

    begin_all(far_rows)
    begin_all(load_expert(first, 0))
    begin(streams)
    await_all(far_rows)
    step = 0

    def one_expert(e, carry):
        bank = e % 2
        await_all(load_expert(e + first, bank))

        @pl.when(e + 1 < late)
        def _():
            begin_all(load_expert(e + 1 + first, 1 - bank))

        mine = lane == holder * held + first + e
        for part in range(4):
            block, rows = part // 2, slice((part % 2) * tile, (part % 2 + 1) * tile)
            results = expert_tile(
                stage[0, block, rows], stage[1, block, rows], gate_rows[block, :, rows].T, mine,
                right_a[bank], right_b[bank], right_c[bank],
            )
            router[block, rows] = jnp.where(mine, results[3], router[block, rows])
            for kind in range(3):
                if part >= 2:
                    rest_out(e, part, kind).wait()
                else:
                    pl.when(e > 0)(lambda: rest_out(e, part, kind).wait())
                left_b[part % 2, kind * tile : (kind + 1) * tile] = results[kind]
                rest_out(e, part, kind).start()
            if part % 2 == 1:

                @pl.when(e >= 1)
                def _():
                    tick(step + 2 * (e - 1) + part // 2)

        return carry

    lax.fori_loop(0, late, one_expert, 0)
    step += 2 * (late - 1)
    for part in (2, 3):
        for kind in range(3):
            rest_out(late - 1, part, kind).wait()

    def router_to_core():
        return pltpu.make_async_remote_copy(
            src_ref=router.at[1],
            dst_ref=router_core,
            send_sem=router_sent.at[0],
            recv_sem=router_arrived.at[0],
            device_id={"ep": core},
        )

    def router_to_chip():
        return pltpu.make_async_remote_copy(
            src_ref=router.at[0],
            dst_ref=router_chip,
            send_sem=router_sent.at[1],
            recv_sem=router_arrived.at[1],
            device_id={"ep": chip},
        )

    router_to_core().start()
    plans = [(dh_copies, True), (dh_copies, False), (y_copies, True), (y_copies, False)]
    load_sum(dh_copies, True, 0, 0)
    for k, (make, is_far) in enumerate(plans):
        base = k * held

        def next_first(bank, k=k):
            if k + 1 < len(plans):
                load_sum(*plans[k + 1], 0, bank)
            else:
                begin_all(load_w(first, 0, 0, bank))

        every = 1 if make is dh_copies else 2

        def piece(e, carry, k=k, make=make, is_far=is_far, base=base, step=step, every=every, next_first=next_first):
            bank = (base + e) % 2
            await_all(make(near, e, e, bank))

            @pl.when(e + 1 < held)
            def _():
                load_sum(make, is_far, e + 1, 1 - bank)

            @pl.when(e + 1 == held)
            def _():
                next_first(1 - bank)

            if make is dh_copies:
                term = contract(left_a[bank], right_a[bank], 1, 1) + contract(left_b[bank], right_b[bank], 1, 1)
            else:
                term = contract(left_a[bank], right_c[bank], 1, 0)

            @pl.when(e == 0)
            def _():
                total[...] = term

            @pl.when(e > 0)
            def _():
                total[...] += term

            @pl.when((e + 1) % every == 0)
            def _():
                tick(step + e // every)

            if k % 2 == 1:

                @pl.when(e == 1)
                def _():
                    send_chip(k - 1)
                    if k == 1:
                        router_to_core().wait_recv()
                        router[0] += router_core[...]
                        router_to_chip().start()

            return carry

        lax.fori_loop(0, held, piece, 0)
        step += held // every
        if k >= 2:
            to_core(k - 2).wait_send()
            if k == 2:
                to_chip(0).wait_send()
            else:
                own_out(1).wait()
        for half in (0, 1):
            stage[k % 2, half] = total[half * tokens : (half + 1) * tokens].astype(jnp.bfloat16)
        to_core(k).start()
        if k % 2 == 1:
            own_out(k).start()
        if make is y_copies:
            tick(step)
            step += 1

    kinds = 3
    base = len(plans) * held

    def grads_out(e, kind):
        slot = (kinds * e + kind) % 2
        return pltpu.make_async_copy(stage_w.at[slot], grads.at[e, :, kind], grads_done.at[slot])

    def expert(e, carry):
        for kind in range(kinds):
            for part in range(4):
                bank = (base + 4 * kind + part) % 2
                await_all(load_w(e + first, kind, part, bank))
                if part < 3:
                    begin_all(load_w(e + first, kind, part + 1, 1 - bank))
                elif kind < kinds - 1:
                    begin_all(load_w(e + first, kind + 1, 0, 1 - bank))
                else:

                    @pl.when(e + first + 1 < held)
                    def _():
                        begin_all(load_w(e + first + 1, 0, 0, 1 - bank))

                term = contract(right_c[bank], left_a[bank, :tokens], 0, 0)
                if part == 0:
                    total_w[...] = term
                else:
                    total_w[...] += term

            @pl.when(kinds * e + kind >= 2)
            def _():
                grads_out(e, kind).wait()

            slot = (kinds * e + kind) % 2
            rows = stage_w.shape[2]
            for j in range(count):
                stage_w[slot, j] = total_w[j * rows : (j + 1) * rows].astype(jnp.bfloat16)
            grads_out(e, kind).start()
            tick(step + kinds * e + kind)
        return carry

    lax.fori_loop(0, late, expert, 0)
    step += kinds * late

    def drain(later, carry):
        tick(later)
        return carry

    lax.fori_loop(step, max(step, many * hops), drain, 0)
    end(streams)
    for k in (1, 3):
        to_core(k).wait_recv()
        near_out(k).start()
    for k in (0, 2):
        to_chip(k).wait_recv()
        far_out(k).start()
    router_to_chip().wait_recv()
    router_out = pltpu.make_async_copy(router_chip, router_far, rows_ready.at[0])
    router_out.start()
    router_to_core().wait_send()
    router_to_chip().wait_send()
    router_out.wait()
    for kind in (kinds - 2, kinds - 1):
        grads_out(late - 1, kind).wait()
    own_out(3).wait()
    to_chip(2).wait_send()
    for k in (2, 3):
        to_core(k).wait_send()
    for k in (1, 3):
        near_out(k).wait()
    for k in (0, 2):
        far_out(k).wait()


def overlap(unit, near, far, w_gate, w_up, w_down, hs, cots, gates, router_so_far, first):
    many, count, rows3, columns = unit.shape
    tokens, width = hs[0].shape
    held = w_gate.shape[0]
    shape, half = (rows3, columns), (rows3, columns // 2)
    block = jax.ShapeDtypeStruct((tokens, width), jnp.bfloat16)
    dma = pltpu.SemaphoreType.DMA

    def buffers(*shape):
        return pltpu.VMEM(shape, jnp.bfloat16)

    flops = 2 * tokens * width * columns * (4 * 3 * held + 12 * (held - first))
    inputs = [unit, *near, *far, w_gate, w_up, w_down, *hs, *cots, *gates, *router_so_far]
    late = held - first
    small = router_so_far[0].shape
    unit_sum, grads, *blocks, router_far, _, _, _ = pl.pallas_call(
        functools.partial(overlap_kernel, count, first, [shape] * many),
        out_shape=[
            jax.ShapeDtypeStruct(unit.shape, unit.dtype),
            jax.ShapeDtypeStruct((held - first, count, 3, rows3 // 3, columns), jnp.bfloat16),
        ]
        + [block] * 6
        + [jax.ShapeDtypeStruct(small, jnp.float32)]
        + [jax.ShapeDtypeStruct((late, 2 * tokens, columns), jnp.bfloat16)] * 3,
        in_specs=[pl.BlockSpec(memory_space=pl.ANY)] * len(inputs),
        out_specs=[pl.BlockSpec(memory_space=pl.ANY)] * 12,
        scratch_shapes=[
            *[buffers(2, SLOTS, *half)] * many,
            *[buffers(2, 2, *half)] * many,
            buffers(2, 2 * tokens, columns),
            buffers(2, 2 * tokens, columns),
            buffers(2, width, columns),
            buffers(2, width, columns),
            buffers(2, columns, width),
            pltpu.VMEM((2 * tokens, width), jnp.float32),
            pltpu.VMEM((width, columns), jnp.float32),
            buffers(2, 2, tokens, width),
            buffers(2, count, rows3 // 3, columns),
            buffers(4, tokens, width),
            buffers(2, tokens, width),
            pltpu.VMEM((2,) + gates[0].shape, jnp.float32),
            pltpu.VMEM((2,) + small, jnp.float32),
            pltpu.VMEM(small, jnp.float32),
            pltpu.VMEM(small, jnp.float32),
            dma((2, 5)),
            dma((4,)),
            dma((4,)),
            dma((2,)),
            dma((2,)),
            dma((6,)),
            dma((2,)),
            dma((8,)),
            dma((2, 3)),
            dma((2,)),
            dma((2,)),
            dma((2 * many, SLOTS)),
            dma((2 * many, SLOTS)),
            dma((2 * many, 2)),
            dma((2 * many, SLOTS)),
            pltpu.SemaphoreType.REGULAR((2 * many,)),
        ],
        compiler_params=pltpu.CompilerParams(
            collective_id=1, has_side_effects=True, vmem_limit_bytes=60 * 2**20
        ),
        cost_estimate=pl.CostEstimate(flops=flops, bytes_accessed=8 * unit.size, transcendentals=0),
        name="overlap",
    )(*inputs)
    grads = grads.reshape(held - first, count, rows3, columns)
    return unit_sum, grads, blocks[:3], blocks[3:], router_far


def finish_kernel(firsts, *refs):
    units, (dense_o, dense_qkv) = refs[: len(firsts) - 1], refs[len(firsts) - 1 : len(firsts) + 1]
    gate, up, down, out, query, key, value, extra_o, extra_qkv = refs[len(firsts) + 1 :]

    @pl.when((pl.program_id(0) == 0) & (pl.program_id(1) == 0))
    def _():
        for dense, parts in ((dense_o, (out, extra_o)), (dense_qkv, (query, key, value, extra_qkv))):
            start = 0
            for part in parts:
                columns = part.shape[1]
                rows = dense.shape[1]
                for j in range(part.shape[0] // rows):
                    part[j * rows : (j + 1) * rows] = dense[j, :, start : start + columns].astype(jnp.float32)
                start += columns

    for index, unit in enumerate(units):
        e = pl.program_id(0)

        @pl.when((e >= firsts[index]) & (e < firsts[index + 1]))
        def _():
            rows = unit.shape[2] // 3
            for k in range(unit.shape[1]):
                gate[0, k * rows : (k + 1) * rows] = unit[0, k, :rows].astype(jnp.float32)
                up[0, k * rows : (k + 1) * rows] = unit[0, k, rows : 2 * rows].astype(jnp.float32)
            turned = jnp.concatenate([unit[0, k, 2 * rows :] for k in range(unit.shape[1])], 0)
            down[0] = turned.astype(jnp.float32).T


def finish(units, dense, width, key_width):
    count, rows3, columns = units[0].shape[1:]
    rows = rows3 // 3
    pair = count // 4
    small = [
        jax.ShapeDtypeStruct((width // 4, part), jnp.float32)
        for part in (width, width, key_width, key_width, 2 * LANES, 2 * LANES)
    ]
    firsts = [0]
    for unit in units:
        firsts.append(firsts[-1] + unit.shape[0])
    experts = firsts[-1]

    def place(index):
        first, end = firsts[index], firsts[index + 1]

        def chunk(e, c):
            inside = jnp.clip(e, first, end - 1)
            return (inside - first, jnp.where(e < first, 0, jnp.where(e >= end, 3, c)), 0, 0)

        return chunk

    return pl.pallas_call(
        functools.partial(finish_kernel, firsts),
        grid=(experts, 4),
        in_specs=[pl.BlockSpec((1, pair, rows3, columns), place(index)) for index in range(len(units))]
        + [whole(part) for part in dense],
        out_specs=[
            pl.BlockSpec((1, pair * rows, columns), lambda e, c: (e, c, 0)),
            pl.BlockSpec((1, pair * rows, columns), lambda e, c: (e, c, 0)),
            pl.BlockSpec((1, columns, pair * rows), lambda e, c: (e, 0, c)),
        ]
        + [whole(part) for part in small],
        out_shape=[
            jax.ShapeDtypeStruct((experts, width, columns), jnp.float32),
            jax.ShapeDtypeStruct((experts, width, columns), jnp.float32),
            jax.ShapeDtypeStruct((experts, columns, width), jnp.float32),
        ]
        + small,
        name="finish",
        compiler_params=pltpu.CompilerParams(vmem_limit_bytes=VMEM_BYTES),
    )(*units, *dense)


def swap_core(value):
    return lax.ppermute(value, "ep", [(0, 1), (1, 0), (2, 3), (3, 2)])


def swap_chip(value):
    return lax.ppermute(value, "ep", [(0, 2), (2, 0), (1, 3), (3, 1)])


def add_bf(a, b):
    return (a.astype(jnp.float32) + b.astype(jnp.float32)).astype(jnp.bfloat16)


def per_device(
    tokens,
    norm_attn,
    w_query,
    key_projection,
    value_projection,
    w_out,
    norm_ffn,
    w_router,
    w_gate,
    w_up,
    w_down,
    routes,
    cotangent,
):
    token_count, width = tokens.shape
    experts_all = w_router.shape[1]
    held = w_gate.shape[0]
    replicas = lax.axis_size("rep")
    cot_near = (cotangent, swap_core(cotangent))
    cot_far = swap_chip(cotangent)
    cosine, sine = rope_tables(token_count)
    normed, queries, keys, values, log_totals, attn, resid, h_two, probs, combine = attention_forward(
        tokens, norm_attn, w_query, key_projection, value_projection, cosine, sine, w_out, norm_ffn, w_router, routes
    )
    h_two, combine, cot_far = lax.optimization_barrier((h_two, combine, cot_far))
    h_near = (h_two, swap_core(h_two))
    gates_near = (combine, swap_core(combine))
    h_far, gates_far = swap_chip(h_two), swap_chip(combine)
    near = expert_pass(held, h_near, cot_near, gates_near, w_gate, w_up, w_down)
    near, h_far, gates_far = lax.optimization_barrier((near, h_far, gates_far))
    h_far = (h_far, swap_core(h_far))
    cot_far = (cot_far, swap_core(cot_far))
    gates_far = (gates_far, swap_core(gates_far))
    far = expert_pass(EARLY, h_far, cot_far, gates_far, w_gate, w_up, w_down)
    ghs, dgs, dus = zip(near[:3], far[:3])
    hs, cots = h_near + h_far, cot_near + cot_far

    router_own, router_near = near[3], swap_core(near[4])
    early = weight_grads(replicas, 0, EARLY, hs, cots, ghs, dgs, dus)
    early, late, (dh_own, dh_near, dh_far), (y_own, y_near, y_far), router_far = overlap(
        early, near[:3], far[:3], w_gate, w_up, w_down, hs, cots, gates_far, far[3:], EARLY
    )
    sent = ring_chunks(late, 1)
    arrived = ring_hop(sent, replicas)
    dh_own, sent = lax.optimization_barrier((dh_own, sent))
    d_resid, grad_out, d_attn = branch_back(
        dh_own, dh_near, dh_far, router_own, router_near, router_far, routes, probs, resid, norm_ffn, cotangent,
        w_router, w_out, h_two, attn,
    )
    arrived, d_attn = lax.optimization_barrier((arrived, d_attn))
    sent = ring_chunks(late, 2, arrived)
    arrived = ring_hop(sent, replicas)
    sent, d_attn = lax.optimization_barrier((sent, d_attn))
    d_pre = attention_back(d_attn, queries, keys, values, log_totals, cosine, sine)
    arrived, d_pre = lax.optimization_barrier((arrived, d_pre))
    sent = ring_chunks(late, 3, arrived)
    arrived = ring_hop(sent, replicas)
    sent, d_pre = lax.optimization_barrier((sent, d_pre))
    d_input, grad_qkv = input_back(
        d_pre, normed, tokens, norm_attn, d_resid, w_query, key_projection, value_projection
    )
    arrived, grad_qkv = lax.optimization_barrier((arrived, grad_qkv))
    initial = ring_chunks(late, 4, arrived)
    mixed = (
        resid + y_own.astype(jnp.float32) + y_near.astype(jnp.float32) + y_far.astype(jnp.float32)
    ).astype(jnp.bfloat16)
    late, sum_o, sum_qkv = ring_sum(late, [grad_out, grad_qkv], 3, initial)
    full_gate, full_up, full_down, sum_o, sum_q, sum_k, sum_v, extra_o, extra_qkv = finish(
        [early, late], [sum_o, sum_qkv], width, key_projection.shape[1]
    )
    sum_r, sum_nf, sum_na = extra_o[:, :experts_all], extra_o[:, LANES], extra_qkv[:, 0]
    return (
        mixed,
        d_input,
        sum_na,
        sum_q,
        sum_k,
        sum_v,
        sum_o,
        sum_nf,
        sum_r,
        full_gate,
        full_up,
        full_down,
    )


def solution(mesh):
    placed = (
        P(("rep", "ep"), None),
        P(),
        P(),
        P(),
        P(),
        P(),
        P(),
        P(),
        P("ep", None, None),
        P("ep", None, None),
        P("ep", None, None),
        P(("rep", "ep"), None),
        P(("rep", "ep"), None),
    )
    return jax.shard_map(
        per_device,
        mesh=mesh,
        in_specs=placed,
        out_specs=(
            P(("rep", "ep"), None),
            P(("rep", "ep"), None),
            P("ep"),
            P("ep", None),
            P("ep", None),
            P("ep", None),
            P("ep", None),
            P("ep"),
            P("ep", None),
            P("ep", None, None),
            P("ep", None, None),
            P("ep", None, None),
        ),
        check_vma=False,
    )
```
